32 devices in a mesh: grp: 4 (over y, core), rep: 8 (over z, x).
Axes of the slice: x: 2, y: 2, z: 4, core: 2. Of those that a mesh axis runs over, the one named last changes fastest.
Arguments:
- tokens: bfloat16 [16, 1024, 960], P('rep', 'grp'), may hold values from -6 to 6
- w_query: bfloat16 [960, 960], P('grp'), may hold values from -0.1875 to 0.1875
- w_key: bfloat16 [960, 320], P('grp'), may hold values from -0.1875 to 0.1875
- w_value: bfloat16 [960, 320], P('grp'), may hold values from -0.1875 to 0.1875
- w_out: bfloat16 [960, 960], P('grp'), may hold values from -2.5 to 2.5
- w_gate: bfloat16 [960, 2560], P(None, 'grp'), may hold values from -0.1875 to 0.1875
- w_up: bfloat16 [960, 2560], P(None, 'grp'), may hold values from -0.1875 to 0.1875
- w_down: bfloat16 [2560, 960], P('grp'), may hold values from -0.125 to 0.125
- gain_attn: bfloat16 [960], P('grp'), may hold values from 0.25 to 1.75
- gain_mlp: bfloat16 [960], P('grp'), may hold values from 0.25 to 1.75
- span_order: int32 [16, 4], P('rep'), may hold values from 0 to 3, each once within a row
- piece_starts: int32 [16, 2], P('rep'), may hold values from 0 to 768, as said below
- cotangent: bfloat16 [16, 1024, 960], P('rep', 'grp'), may hold values from -6 to 6
Outputs:
- block_out: float32 [16, 1024, 960], P('rep', 'grp')
- grad_tokens: float32 [16, 1024, 960], P('rep', 'grp')
- grad_w_query: float32 [960, 960], P('grp')
- grad_w_key: float32 [960, 320], P('grp')
- grad_w_value: float32 [960, 320], P('grp')
- grad_w_out: float32 [960, 960], P('grp')
- grad_w_gate: float32 [960, 2560], P(None, 'grp')
- grad_w_up: float32 [960, 2560], P(None, 'grp')
- grad_w_down: float32 [2560, 960], P('grp')
- grad_gain_attn: float32 [960], P('grp')
- grad_gain_mlp: float32 [960], P('grp')
The draws below stay inside these ranges and needn't reach their ends.
Inputs may be any that keep to these rules, and one draw needn't show every extreme that they name: `span_order`: each row names every one of the sequence's 4 spans once. `piece_starts`: each sequence holds 2 pieces of 256 places at these starts, inside the sequence, in increasing order, not intersecting; some sequence has a piece at its start and some sequence has a piece at its end.
All inputs are finite; a program needn't handle non-finite values.
Results may differ from the reference program's by a relative error of at most 0.019.
Values may be sent and summed in bfloat16 or wider, within the bound.
No kernel may reach another device: no remote copies, remote signals or barrier semaphores. Data moves between devices by JAX's collectives and lax.ppermute only.
A program may use at most 256 MiB of HBM per device.

```python
import jax
import jax.numpy as jnp
from jax import lax

D = 960
HD = 64
FF = 2560
SPAN = 256
PIECE = 256
LEN = 1024
SEQS = 16
QW = 960
KW = 320
N_GRP = 4


def draw_piece_starts(key, part):
    first_key = jax.random.fold_in(key, 11)
    second_key = jax.random.fold_in(key, 12)
    low_row_key = jax.random.fold_in(key, 13)
    high_row_key = jax.random.fold_in(key, 14)
    leading = jax.random.randint(first_key, (SEQS,), 0, LEN - 2 * PIECE + 1)
    row_ids = jnp.arange(SEQS, dtype=jnp.int32)
    low_row = jax.random.randint(low_row_key, (), 0, SEQS)
    high_row = jax.random.randint(high_row_key, (), 0, SEQS)
    leading = jnp.where(row_ids == low_row, 0, leading)
    spare_room = LEN - 2 * PIECE - leading + 1
    second = leading + PIECE + jax.random.randint(second_key, (SEQS,), 0, spare_room)
    second = jnp.where(row_ids == high_row, LEN - PIECE, second)
    return jnp.stack([leading, second], axis=-1).astype(jnp.int32)


def levels(stream_key, shape, split, smallest, top_value):
    loudness = 1.0
    for position, blocks in split:
        draws = jax.random.uniform(jax.random.fold_in(jax.random.fold_in(stream_key, 6), position), (blocks,), jnp.float32, smallest / len(split), top_value / len(split))
        loudness = loudness * jnp.repeat(jnp.exp(draws), shape[position] // blocks).reshape((-1,) + (1,) * (len(shape) - 1 - position))
    return loudness


def normal_values(own_key, extent, scale, limit, pieces=(), kind=jnp.bfloat16):
    level = levels(own_key, extent, pieces, -0.22, 0.18) if pieces else 1.0
    drawn = jax.random.normal(own_key, extent, jnp.float32) * scale * level
    return jnp.minimum(jnp.maximum(drawn, -limit), limit).astype(kind)


def setup_inputs(seed: int = 0) -> dict:
    streams_of = jax.random.split(jax.random.key(seed), 14)
    return {
        "tokens": normal_values(streams_of[0], (SEQS, LEN, D), 1.0, 6.0, ((0, 8), (1, 4))),
        "w_query": normal_values(streams_of[1], (D, QW), D ** -0.5, 0.1875, ((0, 4),)),
        "w_key": normal_values(streams_of[2], (D, KW), D ** -0.5, 0.1875, ((0, 4),)),
        "w_value": normal_values(streams_of[3], (D, KW), D ** -0.5, 0.1875, ((0, 4),)),
        "w_out": normal_values(streams_of[4], (QW, D), 5 ** -0.5, 2.5, ((0, 4),)),
        "w_gate": normal_values(streams_of[5], (D, FF), D ** -0.5, 0.1875, ((1, 4),)),
        "w_up": normal_values(streams_of[6], (D, FF), D ** -0.5, 0.1875, ((1, 4),)),
        "w_down": normal_values(streams_of[7], (FF, D), FF ** -0.5, 0.125, ((0, 4),)),
        "gain_attn": jnp.clip(1.0 + 0.15 * jax.random.normal(streams_of[8], (D,), jnp.float32), 0.25, 1.75).astype(jnp.bfloat16),
        "gain_mlp": jnp.clip(1.0 + 0.15 * jax.random.normal(streams_of[9], (D,), jnp.float32), 0.25, 1.75).astype(jnp.bfloat16),
        "span_order": jax.vmap(lambda own: jax.random.permutation(own, N_GRP))(jax.random.split(streams_of[10], SEQS)).reshape((SEQS, N_GRP)).astype(jnp.int32),
        "piece_starts": draw_piece_starts(jax.random.fold_in(streams_of[13], 71), 0),
        "cotangent": normal_values(streams_of[12], (SEQS, LEN, D), 1.0, 6.0, ((0, 8), (1, 4))),
    }


NORM_EPS = 1e-05
ROPE_BASE = 10000.0
MASKED_SCORE = -1e+30

@jax.custom_vjp
def low(v):
    return lax.optimization_barrier(v.astype(jnp.bfloat16)).astype(jnp.float32)

@jax.custom_vjp
def low_back(v):
    return v

def low_keep(v):
    return (low(v), None)

def low_pass(kept, grad):
    return (grad,)

def back_keep(v):
    return (v, None)

def back_low(kept, grad):
    return (low(grad),)
low.defvjp(low_keep, low_pass)
low_back.defvjp(back_keep, back_low)

def precise(left_mat, right_mat):
    return jnp.dot(left_mat, right_mat, precision=lax.Precision.HIGHEST)

def rms_scale(hidden_in, gain_vec):
    inverse = lax.rsqrt(lax.optimization_barrier(jnp.mean(hidden_in * hidden_in, axis=-1, keepdims=True)) + NORM_EPS)
    return hidden_in * inverse * gain_vec

def rotate(values, places, direction):
    half_dim = HD // 2
    shaped = values.reshape(values.shape[:-1] + (values.shape[-1] // HD, HD))
    frequency = ROPE_BASE ** (-2.0 * jnp.arange(half_dim, dtype=jnp.float32) / HD)
    angles = places.astype(jnp.float32)[..., None, None] * frequency
    cosine = jnp.cos(angles)
    sine_val = jnp.sin(angles)
    leading = shaped[..., :half_dim]
    second = shaped[..., half_dim:]
    turned = jnp.concatenate([leading * cosine - direction * second * sine_val, second * cosine + direction * leading * sine_val], axis=-1)
    return turned.reshape(values.shape)

def allowed_mask(query_pos, key_pos, starts):
    causal = key_pos[None, :] <= query_pos[:, None]
    query_in = (query_pos[:, None] >= starts[None, :]) & (query_pos[:, None] < starts[None, :] + PIECE)
    key_in = (key_pos[:, None] >= starts[None, :]) & (key_pos[:, None] < starts[None, :] + PIECE)
    inside = jnp.any(query_in[:, None, :] & key_in[None, :, :], axis=-1)
    return causal | inside

def attend_one(bundle):
    queries, key_rows, value_rows, places, starts = bundle
    length = queries.shape[0]
    heads_kv = key_rows.shape[-1] // HD
    grouped = queries.reshape(length, heads_kv, -1, HD)
    key_heads = key_rows.reshape(length, heads_kv, HD)
    value_heads = value_rows.reshape(length, heads_kv, HD)
    scores = jnp.einsum('qkgd,pkd->kgqp', grouped, key_heads, precision=lax.Precision.HIGHEST) * HD ** (-0.5)
    scores = low_back(scores)
    allowed = allowed_mask(places, places, starts)
    masked = jnp.where(allowed[None, None], scores, MASKED_SCORE)
    row_peak = lax.optimization_barrier(jnp.max(masked, axis=-1, keepdims=True))
    exponent = jnp.exp(masked - row_peak)
    probability = low(exponent / lax.optimization_barrier(jnp.sum(exponent, axis=-1, keepdims=True)))
    mixed_out = jnp.einsum('kgqp,pkd->qkgd', probability, value_heads, precision=lax.Precision.HIGHEST)
    return mixed_out.reshape(length, -1)

def forward(tokens, w_query, w_key, w_value, w_out, w_gate, w_up, w_down, gain_attn, gain_mlp, places, starts):
    seq_count, length, width = tokens.shape
    norm_one = low(rms_scale(tokens, gain_attn)).reshape(-1, width)
    query_lin = low_back(precise(norm_one, w_query))
    key_lin = low_back(precise(norm_one, w_key))
    value_lin = low(low_back(precise(norm_one, w_value)))
    queries = low(rotate(query_lin.reshape(seq_count, length, -1), places, 1.0))
    key_rows = low(rotate(key_lin.reshape(seq_count, length, -1), places, 1.0))
    attended = lax.map(jax.checkpoint(attend_one), (queries, key_rows, value_lin.reshape(seq_count, length, -1), places, starts))
    attended = low(low_back(attended)).reshape(-1, w_out.shape[0])
    branch_attn = low_back(precise(attended, w_out)).reshape(tokens.shape)
    middle = tokens + branch_attn
    norm_two = low(rms_scale(middle, gain_mlp)).reshape(-1, width)
    gate_lin = low_back(precise(norm_two, w_gate))
    up_lin = low_back(precise(norm_two, w_up))
    hidden = low(jax.nn.silu(gate_lin) * up_lin)
    branch_mlp = low_back(precise(hidden, w_down)).reshape(tokens.shape)
    return middle + branch_mlp

def reference(tokens, w_query, w_key, w_value, w_out, w_gate, w_up, w_down, gain_attn, gain_mlp, span_order, piece_starts, cotangent):
    places = (span_order[:, :, None] * SPAN + jnp.arange(SPAN, dtype=jnp.int32)[None, None, :]).reshape(span_order.shape[0], -1).astype(jnp.int32)
    floats = [argument.astype(jnp.float32) for argument in (tokens, w_query, w_key, w_value, w_out, w_gate, w_up, w_down, gain_attn, gain_mlp)]

    def closed(*inputs):
        return forward(*inputs, places, piece_starts)
    block_out, pullback = jax.vjp(closed, *floats)
    grads = pullback(cotangent.astype(jnp.float32))
    return (block_out, grads[0], grads[1], grads[2], grads[3], grads[4], grads[5], grads[6], grads[7], grads[8], grads[9])
```

```python
import jax
import jax.numpy as jnp
from jax import lax
from jax.sharding import PartitionSpec as P

HD = 64
PIECE = 256


NORM_EPS = 1e-05
ROPE_BASE = 10000.0
MASKED_SCORE = -1e30


def rotate(values, places, direction):
    half_dim = HD // 2
    shaped = values.reshape(values.shape[:-1] + (values.shape[-1] // HD, HD))
    frequency = ROPE_BASE ** (-2.0 * jnp.arange(half_dim, dtype=jnp.float32) / HD)
    angles = places.astype(jnp.float32)[..., None, None] * frequency
    cosine = jnp.cos(angles)
    sine_val = jnp.sin(angles)
    leading = shaped[..., :half_dim]
    second = shaped[..., half_dim:]
    turned = jnp.concatenate(
        [
            leading * cosine - direction * second * sine_val,
            second * cosine + direction * leading * sine_val,
        ],
        axis=-1,
    )
    return turned.reshape(values.shape)


def allowed_mask(query_pos, key_pos, starts):
    causal = key_pos[None, :] <= query_pos[:, None]
    query_in = (query_pos[:, None] >= starts[None, :]) & (
        query_pos[:, None] < starts[None, :] + PIECE
    )
    key_in = (key_pos[:, None] >= starts[None, :]) & (key_pos[:, None] < starts[None, :] + PIECE)
    inside = jnp.any(query_in[:, None, :] & key_in[None, :, :], axis=-1)
    return causal | inside


def norm_scale(hidden_in, gain_vec):
    inverse = lax.rsqrt(jnp.mean(hidden_in * hidden_in, axis=-1, keepdims=True) + NORM_EPS)
    return (hidden_in * inverse * gain_vec, inverse)


def norm_back(hidden_in, inverse, gain_vec, grad_norm):
    scaled = grad_norm * gain_vec
    grad_in = inverse * scaled - hidden_in * inverse * inverse * inverse * jnp.mean(
        scaled * hidden_in, axis=-1, keepdims=True
    )
    grad_gain = jnp.sum(grad_norm * hidden_in * inverse, axis=0)
    return (grad_in, grad_gain)


def score_block(queries, key_rows, query_pos, key_pos, starts):
    q_count = queries.shape[0]
    heads_kv = key_rows.shape[-1] // HD
    grouped = queries.reshape(q_count, heads_kv, -1, HD)
    key_heads = key_rows.reshape(-1, heads_kv, HD)
    scores = jnp.einsum(
        "qkgd,pkd->kgqp", grouped, key_heads, preferred_element_type=jnp.float32
    ) * HD ** (-0.5)
    masked = jnp.where(allowed_mask(query_pos, key_pos, starts)[None, None], scores, MASKED_SCORE)
    return (masked, grouped, key_heads)


def attend_forward(bundle):
    queries, key_rows, value_rows, query_pos, key_pos, starts = bundle
    q_count = queries.shape[0]
    masked, grouped, key_heads = score_block(queries, key_rows, query_pos, key_pos, starts)
    value_heads = value_rows.reshape(-1, key_heads.shape[1], HD)
    row_peak = jnp.max(masked, axis=-1, keepdims=True)
    exponent = jnp.exp(masked - row_peak)
    total_sum = jnp.sum(exponent, axis=-1, keepdims=True)
    probability = (exponent / total_sum).astype(jnp.bfloat16)
    mixed_out = jnp.einsum(
        "kgqp,pkd->qkgd", probability, value_heads, preferred_element_type=jnp.float32
    )
    log_total = row_peak + jnp.log(total_sum)
    return (mixed_out.reshape(q_count, -1).astype(jnp.bfloat16), log_total)


def attend_backward(bundle):
    queries, key_rows, value_rows, query_pos, key_pos, starts, log_total, grad_mixed = bundle
    q_count = queries.shape[0]
    masked, grouped, key_heads = score_block(queries, key_rows, query_pos, key_pos, starts)
    heads_kv = key_heads.shape[1]
    value_heads = value_rows.reshape(-1, heads_kv, HD)
    probability = jnp.exp(masked - log_total)
    prob_low = probability.astype(jnp.bfloat16)
    grad_heads = grad_mixed.reshape(q_count, heads_kv, -1, HD)
    grad_prob = jnp.einsum(
        "qkgd,pkd->kgqp", grad_heads, value_heads, preferred_element_type=jnp.float32
    )
    inner_sum = jnp.sum(probability * grad_prob, axis=-1, keepdims=True)
    grad_scores = (probability * (grad_prob - inner_sum)).astype(jnp.bfloat16)
    scale_val = HD ** (-0.5)
    grad_query = (
        jnp.einsum("kgqp,pkd->qkgd", grad_scores, key_heads, preferred_element_type=jnp.float32)
        * scale_val
    )
    grad_key = (
        jnp.einsum("kgqp,qkgd->pkd", grad_scores, grouped, preferred_element_type=jnp.float32)
        * scale_val
    )
    grad_value = jnp.einsum(
        "kgqp,qkgd->pkd", prob_low, grad_heads, preferred_element_type=jnp.float32
    )
    return (
        grad_query.reshape(q_count, -1),
        grad_key.reshape(grad_key.shape[0], -1),
        grad_value.reshape(grad_value.shape[0], -1),
    )


def left_dot(left_mat, right_mat):
    return lax.dot_general(
        left_mat, right_mat, (((0,), (0,)), ((), ())), preferred_element_type=jnp.float32
    )


def right_dot(left_mat, right_mat):
    return lax.dot_general(
        left_mat, right_mat, (((1,), (1,)), ((), ())), preferred_element_type=jnp.float32
    )


def swap(values, axis, count, mask):
    return lax.ppermute(values, axis, [(i, i ^ mask) for i in range(count)])


def group_blocks(own):
    across = swap(own, "grp", 4, 2)
    beside = swap(own, "grp", 4, 1)
    corner = swap(across, "grp", 4, 1)
    return own, beside, across, corner


def group_sum(parts):
    low = jnp.bfloat16
    beside = swap(jnp.stack([parts[1], parts[3]]).astype(low), "grp", 4, 1).astype(jnp.float32)
    across = swap((parts[2] + beside[1]).astype(low), "grp", 4, 2).astype(jnp.float32)
    return parts[0] + beside[0] + across


def absolute(blocks, rank):
    stacked = jnp.stack(blocks)
    return jnp.take(stacked, jnp.arange(len(blocks)) ^ rank, axis=0)


def rep_sum(chunks, ranks):
    low = jnp.bfloat16
    rank = lax.axis_index("rep")
    low_rank = rank & 7
    slots = jnp.take(chunks, jnp.arange(8) ^ low_rank, axis=0)
    one = swap(slots[jnp.array([1, 3, 5, 7])].astype(low), "rep", ranks, 1)
    slots = slots[jnp.array([0, 2, 4, 6])] + one.astype(jnp.float32)
    two = swap(slots[jnp.array([1, 3])].astype(low), "rep", ranks, 2)
    slots = slots[jnp.array([0, 2])] + two.astype(jnp.float32)
    three = swap(slots[1:2].astype(low), "rep", ranks, 4)
    mine = slots[0:1] + three.astype(jnp.float32)
    mine = mine.astype(low)
    if ranks > 8:
        others = [[j * 8 + i for j in range(ranks // 8)] for i in range(8)]
        mine = lax.psum(mine, "rep", axis_index_groups=others)
    held = jnp.stack([mine[0], swap(mine, "rep", ranks, 4)[0]])
    other = swap(held, "rep", ranks, 2)
    held = jnp.stack([held[0], other[0], held[1], other[1]])
    other = swap(held, "rep", ranks, 1)
    held = jnp.stack([held[0], other[0], held[1], other[1], held[2], other[2], held[3], other[3]])
    return jnp.take(held, jnp.arange(8) ^ low_rank, axis=0)


def body(
    tokens,
    w_query,
    w_key,
    w_value,
    w_out,
    w_gate,
    w_up,
    w_down,
    gain_attn,
    gain_mlp,
    span_order,
    piece_starts,
    cotangent,
):
    groups = lax.axis_size("grp")
    ranks = lax.axis_size("rep")
    rank_grp = lax.axis_index("grp")
    seq_count, span_len, width = tokens.shape
    low = jnp.bfloat16
    shard_rows = w_query.shape[0]
    gains = jnp.zeros((16, w_key.shape[1] + w_value.shape[1]), low)
    gains = gains.at[0, :shard_rows].set(gain_attn).at[1, :shard_rows].set(gain_mlp)
    kv_shard = jnp.concatenate([jnp.concatenate([w_key, w_value], axis=1), gains], axis=0)
    kv_full = absolute(group_blocks(kv_shard), rank_grp)
    full_kv = kv_full[:, :shard_rows].reshape(width, -1)
    gain_one = kv_full[:, shard_rows, :shard_rows].reshape(width).astype(jnp.float32)
    gain_two = kv_full[:, shard_rows + 1, :shard_rows].reshape(width).astype(jnp.float32)
    full_query = absolute(group_blocks(w_query), rank_grp).reshape(width, -1)
    full_out = absolute(group_blocks(w_out), rank_grp).reshape(-1, width)
    kw = w_key.shape[1]

    rel = jnp.arange(groups, dtype=jnp.int32) ^ rank_grp
    order = jnp.take(span_order, rel, axis=1)
    offsets = jnp.arange(span_len, dtype=jnp.int32)
    query_pos = order[:, 0, None] * span_len + offsets[None, :]
    key_pos = (order[:, :, None] * span_len + offsets[None, None, :]).reshape(seq_count, -1)
    token_rows = tokens.reshape(-1, width).astype(jnp.float32)
    norm_one, inverse_one = norm_scale(token_rows, gain_one)
    norm_low = norm_one.astype(low)
    kv_lin = jnp.dot(norm_low, full_kv, preferred_element_type=jnp.float32)
    query_lin = jnp.dot(norm_low, full_query, preferred_element_type=jnp.float32)
    queries = rotate(query_lin.reshape(seq_count, span_len, -1), query_pos, 1.0).astype(low)
    key_local = rotate(kv_lin[:, :kw].reshape(seq_count, span_len, -1), query_pos, 1.0).astype(low)
    value_local = kv_lin[:, kw:].reshape(seq_count, span_len, -1).astype(low)
    kv_local = jnp.concatenate([key_local, value_local], axis=-1)
    kv_all = [jnp.concatenate(group_blocks(kv_local[s]), axis=0) for s in range(seq_count)]
    cot_blocks = group_blocks(cotangent)

    middles, x_blocks, logs, attendeds, inverse_twos = [], [], [], [], []
    for s in range(seq_count):
        attended, log_total = attend_forward(
            (queries[s], kv_all[s][:, :kw], kv_all[s][:, kw:], query_pos[s], key_pos[s], piece_starts[s])
        )
        middle = tokens[s].astype(jnp.float32) + jnp.dot(
            attended, full_out, preferred_element_type=jnp.float32
        )
        norm_two, inverse_two = norm_scale(middle, gain_two)
        x_blocks.append(group_blocks(norm_two.astype(low)))
        middles.append(middle)
        logs.append(log_total)
        attendeds.append(attended)
        inverse_twos.append(inverse_two)

    outs, grad_norms, hid, gg, gu, xs, cs = [], [], [], [], [], [], []
    for s in range(seq_count):
        x = jnp.concatenate(x_blocks[s], axis=0)
        cot = jnp.concatenate([c[s] for c in cot_blocks], axis=0)
        gate_lin = jnp.dot(x, w_gate, preferred_element_type=jnp.float32)
        up_lin = jnp.dot(x, w_up, preferred_element_type=jnp.float32)
        gate_sig = jax.nn.sigmoid(gate_lin)
        swish = gate_lin * gate_sig
        hidden = (swish * up_lin).astype(low)
        out_part = jnp.dot(hidden, w_down, preferred_element_type=jnp.float32)
        grad_hidden = right_dot(cot, w_down)
        grad_gate = (grad_hidden * up_lin * gate_sig * (1.0 + gate_lin * (1.0 - gate_sig))).astype(low)
        grad_up = (grad_hidden * swish).astype(low)
        grad_x = right_dot(grad_gate, w_gate) + right_dot(grad_up, w_up)
        outs.append(middles[s] + group_sum(out_part.reshape(groups, span_len, -1)))
        grad_norms.append(group_sum(grad_x.reshape(groups, span_len, -1)))
        hid.append(hidden)
        gg.append(grad_gate)
        gu.append(grad_up)
        xs.append(x)
        cs.append(cot)
    x_all, cot_all = jnp.concatenate(xs), jnp.concatenate(cs)
    grad_gate_w = left_dot(x_all, jnp.concatenate(gg))
    grad_up_w = left_dot(x_all, jnp.concatenate(gu))
    grad_down_w = left_dot(jnp.concatenate(hid), cot_all)
    ff = grad_gate_w.shape[1]
    gate_up = rep_sum(jnp.concatenate([grad_gate_w, grad_up_w], axis=1).reshape(8, -1, 2 * ff), ranks)
    gate_up = gate_up.reshape(width, 2 * ff).astype(jnp.float32)
    down = rep_sum(grad_down_w.reshape(8, -1, width), ranks).reshape(ff, width).astype(jnp.float32)

    gq, gkv, grad_mids, gain_twos, branches = [], [], [], [], []
    for s in range(seq_count):
        grad_mid_norm, grad_gain_two = norm_back(middles[s], inverse_twos[s], gain_two, grad_norms[s])
        grad_middle = cotangent[s].astype(jnp.float32) + grad_mid_norm
        grad_branch = grad_middle.astype(low)
        grad_attended = right_dot(grad_branch, full_out).astype(low)
        grad_query_rot, grad_key_all, grad_value_all = attend_backward(
            (
                queries[s],
                kv_all[s][:, :kw],
                kv_all[s][:, kw:],
                query_pos[s],
                key_pos[s],
                piece_starts[s],
                logs[s],
                grad_attended,
            )
        )
        both = jnp.concatenate([grad_key_all, grad_value_all], axis=-1)
        own = group_sum(both.reshape(groups, span_len, -1))
        gq.append(rotate(grad_query_rot, query_pos[s], -1.0).astype(low))
        gkv.append(
            jnp.concatenate([rotate(own[:, :kw], query_pos[s], -1.0), own[:, kw:]], axis=1).astype(low)
        )
        grad_mids.append(grad_middle)
        gain_twos.append(grad_gain_two)
        branches.append(grad_branch)
    grad_q_low, grad_kv_low = jnp.concatenate(gq), jnp.concatenate(gkv)
    grad_out_w = left_dot(jnp.concatenate(attendeds), jnp.concatenate(branches))
    grad_query_w = left_dot(norm_low, grad_q_low)
    grad_kv_w = left_dot(norm_low, grad_kv_low)
    grad_norm_one = right_dot(grad_q_low, full_query) + right_dot(grad_kv_low, full_kv)
    grad_middle = jnp.concatenate(grad_mids)
    grad_tok_norm, grad_gain_one = norm_back(token_rows, inverse_one, gain_one, grad_norm_one)
    grad_tokens = grad_middle + grad_tok_norm
    grad_gain_two = gain_twos[0] + gain_twos[1]

    gain_rows = jnp.zeros((groups, 8, 2 * width + 2 * kw), jnp.float32)
    gain_rows = gain_rows.at[:, 0, :shard_rows].set(grad_gain_one.reshape(groups, -1))
    gain_rows = gain_rows.at[:, 1, :shard_rows].set(grad_gain_two.reshape(groups, -1))
    attn_w = jnp.concatenate([grad_query_w, grad_out_w, grad_kv_w], axis=1).reshape(groups, shard_rows, -1)
    attn_w = jnp.concatenate([attn_w, gain_rows], axis=1)
    attn_w = jnp.take(attn_w, rel, axis=0)
    own_w = group_sum([attn_w[k] for k in range(groups)])
    own_w = rep_sum(own_w.reshape(8, -1, own_w.shape[1]), ranks).reshape(own_w.shape)
    own_w = own_w.astype(jnp.float32)
    return (
        jnp.stack(outs),
        grad_tokens.reshape(tokens.shape),
        own_w[:shard_rows, :width],
        own_w[:shard_rows, 2 * width : 2 * width + kw],
        own_w[:shard_rows, 2 * width + kw :],
        own_w[:shard_rows, width : 2 * width],
        gate_up[:, :ff],
        gate_up[:, ff:],
        down,
        own_w[shard_rows, :shard_rows],
        own_w[shard_rows + 1, :shard_rows],
    )


def solution(mesh):
    placed = (
        P("rep", "grp", None),
        P("grp", None),
        P("grp", None),
        P("grp", None),
        P("grp", None),
        P(None, "grp"),
        P(None, "grp"),
        P("grp", None),
        P("grp"),
        P("grp"),
        P("rep", None),
        P("rep", None),
        P("rep", "grp", None),
    )
    return jax.shard_map(
        body,
        mesh=mesh,
        in_specs=placed,
        out_specs=(
            P("rep", "grp", None),
            P("rep", "grp", None),
            P("grp", None),
            P("grp", None),
            P("grp", None),
            P("grp", None),
            P(None, "grp"),
            P(None, "grp"),
            P("grp", None),
            P("grp"),
            P("grp"),
        ),
        check_vma=False,
    )
```

```python
import functools

import jax
import jax.numpy as jnp
from jax import lax
from jax.experimental import pallas as pl
from jax.experimental.pallas import tpu as pltpu
from jax.sharding import PartitionSpec as P

HD = 64
PIECE = 256
LANES = 128
GROUP = 4
PARTS = 8
GAIN_ROWS = 16
SLOTS = (7, 3, 5, 1, 6, 2, 4, 0)


NORM_EPS = 1e-05
ROPE_BASE = 10000.0
MASKED_SCORE = -1e30
SCALE = HD ** (-0.5)

LOW = jnp.bfloat16
FULL = jnp.float32
NN = (((1,), (0,)), ((), ()))
NT = (((1,), (1,)), ((), ()))
TN = (((0,), (0,)), ((), ()))
TT = (((0,), (1,)), ((), ()))


def dot(left_mat, right_mat, form=NN):
    return lax.dot_general(left_mat, right_mat, form, preferred_element_type=FULL)


def swap(values, axis, count, mask):
    return lax.ppermute(values, axis, [(i, i ^ mask) for i in range(count)])


def group_blocks(own):
    across = swap(own, "grp", GROUP, 2)
    beside = swap(own, "grp", GROUP, 1)
    corner = swap(across, "grp", GROUP, 1)
    return own, beside, across, corner


def group_terms(keep, send):
    beside = swap(send, "grp", GROUP, 1)
    across = (keep[1].astype(FULL) + beside[1].astype(FULL)).astype(LOW)
    return keep[0], beside[0], swap(across, "grp", GROUP, 2)


def three(terms):
    return terms[0].astype(FULL) + terms[1].astype(FULL) + terms[2].astype(FULL)


def rep_sum(first, second, third, last, ranks):
    one = swap(first, "rep", ranks, 1)
    two = (second.astype(FULL) + one[0:2].astype(FULL)).astype(LOW)
    two = swap(two, "rep", ranks, 2)
    four = (third.astype(FULL) + one[2:3].astype(FULL) + two[0:1].astype(FULL)).astype(LOW)
    four = swap(four, "rep", ranks, 4)
    mine = last.astype(FULL) + one[3:4].astype(FULL) + two[1:2].astype(FULL) + four.astype(FULL)
    mine = mine.astype(LOW)
    if ranks > PARTS:
        others = [[j * PARTS + i for j in range(ranks // PARTS)] for i in range(PARTS)]
        mine = lax.psum(mine, "rep", axis_index_groups=others)
    held = jnp.concatenate([mine, swap(mine, "rep", ranks, 4)])
    held = jnp.concatenate([held, swap(held, "rep", ranks, 2)])
    return held, swap(held, "rep", ranks, 1)


def call(kernel, name, out_shape, *, grid=(), prefetch=0, in_specs, out_specs, scratch=(), flops=0, moved=0, vmem=56):
    return pl.pallas_call(
        kernel,
        name=name,
        out_shape=out_shape,
        grid_spec=pltpu.PrefetchScalarGridSpec(
            num_scalar_prefetch=prefetch,
            grid=grid,
            in_specs=in_specs,
            out_specs=out_specs,
            scratch_shapes=list(scratch),
        ),
        compiler_params=pltpu.CompilerParams(vmem_limit_bytes=vmem << 20),
        cost_estimate=pl.CostEstimate(flops=int(flops), bytes_accessed=int(moved), transcendentals=0),
    )


def whole(shape):
    return pl.BlockSpec(shape, lambda *_: (0,) * len(shape))


def shape_of(shape, kind=LOW):
    return jax.ShapeDtypeStruct(shape, kind)


def lane_index(rows):
    return lax.broadcasted_iota(jnp.int32, (rows, LANES), 1)


def turn(slab, cosine, sine_val, lane):
    swapped = jnp.where(
        lane % HD < HD // 2, pltpu.roll(slab, LANES - HD // 2, 1), pltpu.roll(slab, HD // 2, 1)
    )
    return slab * cosine + swapped * sine_val


def assemble(rank, blocks, scratch, rows, columns):
    for k in range(GROUP):
        start = pl.multiple_of((rank ^ k) * rows, 16)
        scratch[pl.ds(start, rows), 0:columns] = blocks[k][0:rows, :]


def keys_values_kernel(ranks, tok_ref, b0, b1, b2, b3, cos_ref, sin_ref, norm_ref, kv_refs_a, kv_refs_b, gain_ref, w_ref):
    width = tok_ref.shape[1]
    kw2 = b0.shape[1]
    shard = b0.shape[0] - GAIN_ROWS
    span = kv_refs_a.shape[0]
    blocks = (b0, b1, b2, b3)
    rows = sum(b[shard : shard + GAIN_ROWS, :].astype(FULL) for b in blocks)
    gain_one = jnp.concatenate([rows[0:1, :], rows[1:2, : width - kw2]], axis=1)
    gain_two = jnp.concatenate([rows[2:3, :], rows[3:4, : width - kw2]], axis=1)
    gain_ref[0:1, :] = gain_one
    gain_ref[1:2, :] = gain_two
    gain_ref[2:8, :] = jnp.zeros((6, width), FULL)
    assemble(ranks[0], blocks, w_ref, shard, kw2)
    lane = lane_index(span)
    heads = kw2 // LANES
    for s, out in enumerate((kv_refs_a, kv_refs_b)):
        part = slice(s * span, (s + 1) * span)
        x = tok_ref[part, :].astype(FULL)
        inverse = lax.rsqrt(jnp.mean(x * x, axis=-1, keepdims=True) + NORM_EPS)
        norm = (x * inverse * gain_one).astype(LOW)
        norm_ref[part, :] = norm
        kv = dot(norm, w_ref[...])
        cosine, sine_val = cos_ref[part, :], sin_ref[part, :]
        for h in range(heads):
            key = kv[:, (h // 2) * LANES : (h // 2 + 1) * LANES]
            key = turn(key, cosine, sine_val, lane)
            if h % 2:
                key = pltpu.roll(key, HD, 1)
            v = heads + h
            value = kv[:, (v // 2) * LANES : (v // 2 + 1) * LANES]
            if v % 2 == 0:
                value = pltpu.roll(value, HD, 1)
            out[:, h * LANES : (h + 1) * LANES] = jnp.where(lane < HD, key, value).astype(LOW)


def queries_kernel(ranks, norm_ref, b0, b1, b2, b3, cos_ref, sin_ref, q_ref, w_ref):
    width = b0.shape[1]
    shard = b0.shape[0]
    span = norm_ref.shape[0] // 2
    padded = w_ref.shape[1]
    assemble(ranks[0], (b0, b1, b2, b3), w_ref, shard, width)
    if padded > width:
        w_ref[:, width:padded] = jnp.zeros((w_ref.shape[0], padded - width), LOW)
    lane = lane_index(span)
    heads = width // HD
    for s in range(2):
        part = slice(s * span, (s + 1) * span)
        query = dot(norm_ref[part, :], w_ref[...])
        cosine, sine_val = cos_ref[part, :], sin_ref[part, :]
        for j in range(padded // LANES):
            slab = turn(query[:, j * LANES : (j + 1) * LANES], cosine, sine_val, lane) * SCALE
            even = jnp.where(lane < HD, slab, 0.0)
            q_ref[part, 2 * j * LANES : (2 * j + 1) * LANES] = even.astype(LOW)
            if 2 * j + 1 < heads:
                odd = jnp.where(lane < HD, pltpu.roll(slab, HD, 1), 0.0)
                q_ref[part, (2 * j + 1) * LANES : (2 * j + 2) * LANES] = odd.astype(LOW)


def attend_kernel(seq, ranks, order, starts, q_ref, b0, b1, b2, b3, p_ref, o_ref, bias_ref):
    span = q_ref.shape[0]
    per = q_ref.shape[1] // LANES
    rank = ranks[0]

    @pl.when(pl.program_id(0) == 0)
    def _():
        query_pos = order[seq, rank] * span + lax.broadcasted_iota(jnp.int32, (span, span), 1)
        query_in = []
        for m in range(2):
            start = starts[seq, m]
            query_in.append((query_pos >= start) & (query_pos < start + PIECE))
        for k in range(GROUP):
            key_pos = order[seq, rank ^ k] * span + lax.broadcasted_iota(jnp.int32, (span, span), 0)
            allowed = key_pos <= query_pos
            for m in range(2):
                start = starts[seq, m]
                key_in = (key_pos >= start) & (key_pos < start + PIECE)
                allowed = allowed | (query_in[m] & key_in)
            bias_ref[k * span : (k + 1) * span, :] = jnp.where(allowed, 0.0, MASKED_SCORE)

    kv = jnp.concatenate([b0[...], b1[...], b2[...], b3[...]], axis=0)
    kv_t = kv.T
    for i in range(per):
        scores = dot(kv, q_ref[:, i * LANES : (i + 1) * LANES], NT) + bias_ref[...]
        peak = jnp.max(scores, axis=0, keepdims=True)
        exponent = jnp.exp(scores - peak)
        total = jnp.sum(exponent, axis=0, keepdims=True)
        probs = (exponent * (1.0 / total)).astype(LOW)
        p_ref[0, :, i * span : (i + 1) * span] = probs
        mixed = dot(kv_t, probs)
        o_ref[i * HD : (i + 1) * HD, :] = mixed[HD : 2 * HD, :].astype(LOW)


def middle_kernel(ranks, att_ref, b0, b1, b2, b3, tok_ref, gain_ref, mid_ref, x_ref, w_ref):
    width = b0.shape[1]
    shard = b0.shape[0]
    assemble(ranks[0], (b0, b1, b2, b3), w_ref, shard, width)
    middle = tok_ref[0].astype(FULL) + dot(att_ref[...], w_ref[...], TN)
    mid_ref[...] = middle
    inverse = lax.rsqrt(jnp.mean(middle * middle, axis=-1, keepdims=True) + NORM_EPS)
    x_ref[...] = (middle * inverse * gain_ref[1:2, :]).astype(LOW)


def forward_back_kernel(x0, x1, x2, x3, c0, c1, c2, c3, wg_ref, wu_ref, wd_ref, ko_ref, so_ref, kg_ref, sg_ref, hid_ref, gg_ref, gu_ref, xs, cs):
    k = pl.program_id(0)
    for i, (x, c) in enumerate(((x0, c0), (x1, c1), (x2, c2), (x3, c3))):

        @pl.when(k == i)
        def _(x=x, c=c):
            xs[...] = x[...]
            cs[...] = c[0]

    x = xs[...]
    gate = dot(x, wg_ref[...])
    up = dot(x, wu_ref[...])
    grad_hidden = dot(cs[...], wd_ref[...], NT)
    sig = 1.0 / (1.0 + jnp.exp(-gate))
    swish = gate * sig
    hidden = (swish * up).astype(LOW)
    grad_gate = (grad_hidden * up * sig * (1.0 + gate * (1.0 - sig))).astype(LOW)
    grad_up = (grad_hidden * swish).astype(LOW)
    hid_ref[...] = hidden
    gg_ref[...] = grad_gate
    gu_ref[...] = grad_up
    grad_x = (dot(grad_gate, wg_ref[...], NT) + dot(grad_up, wu_ref[...], NT)).astype(LOW)
    out = dot(hidden, wd_ref[...]).astype(LOW)
    half = k // 2

    @pl.when(k % 2 == 0)
    def _():
        kg_ref[half] = grad_x
        ko_ref[half] = out

    @pl.when(k % 2 == 1)
    def _():
        sg_ref[half] = grad_x
        so_ref[half] = out


def weight_kernel(ranks, *refs):
    xs = refs[0:8]
    cs = refs[8:12]
    rows = refs[12:18]
    first, second, third, last = refs[18:22]
    left, left_t, right, acc, sem = refs[22:27]
    m = pl.program_id(0)
    span = left.shape[2]
    copies = []
    for s in range(2):
        for k in range(GROUP):
            b = s * GROUP + k
            copies.append(pltpu.make_async_copy(xs[b], left.at[0, b], sem.at[b]))
            copies.append(pltpu.make_async_copy(cs[k].at[s], left.at[1, b], sem.at[8 + b]))
        for n in range(3):
            copies.append(
                pltpu.make_async_copy(
                    rows[s * 3 + n], right.at[n, pl.ds(s * GROUP * span, GROUP * span)], sem.at[16 + s * 3 + n]
                )
            )

    @pl.when(m == 0)
    def _():
        for copy in copies:
            copy.start()
        for copy in copies:
            copy.wait()

    @pl.when(m != 1)
    def _():
        side = m // 2

        def flip(b, carry):
            start = pl.multiple_of(b * span, LANES)
            left_t[:, pl.ds(start, span)] = left[side, b].T
            return carry

        lax.fori_loop(0, 2 * GROUP, flip, 0)

    acc[...] = dot(left_t[...], right[m])
    part = acc.shape[0] // PARTS
    outs = [(first, i) for i in range(4)] + [(second, 0), (second, 1), (third, 0), (last, 0)]
    for (out, i), slot in zip(outs, SLOTS):
        start = pl.multiple_of((slot ^ ranks[1]) * part, 8)
        out[i] = acc[pl.ds(start, part), :].astype(LOW)


def branch_kernel(ranks, mid_ref, cot_ref, e0, e1, e2, gain_ref, b0, b1, b2, b3, att_ref, gm_ref, gb_ref, do_ref, delta_ref, gain_out, w_ref):
    width = b0.shape[1]
    shard = b0.shape[0]
    span = mid_ref.shape[0]
    padded = w_ref.shape[0]
    assemble(ranks[0], (b0, b1, b2, b3), w_ref, shard, width)
    if padded > width:
        w_ref[width:padded, :] = jnp.zeros((padded - width, width), LOW)
    middle = mid_ref[...]
    grad = e0[0].astype(FULL) + e1[0].astype(FULL) + e2[...].astype(FULL)
    inverse = lax.rsqrt(jnp.mean(middle * middle, axis=-1, keepdims=True) + NORM_EPS)
    scaled = grad * gain_ref[1:2, :]
    turned = jnp.mean(scaled * middle, axis=-1, keepdims=True)
    grad_middle = cot_ref[0].astype(FULL) + inverse * scaled - middle * (inverse * inverse * inverse * turned)
    gain_out[0:1, :] = jnp.sum(grad * middle * inverse, axis=0, keepdims=True)
    gain_out[1:8, :] = jnp.zeros((7, width), FULL)
    gm_ref[...] = grad_middle
    branch = grad_middle.astype(LOW)
    gb_ref[...] = branch
    lane = lane_index(span)
    grad_att = dot(branch, w_ref[...], NT)
    heads = width // HD
    for j in range(padded // LANES):
        slab = grad_att[:, j * LANES : (j + 1) * LANES]
        even = jnp.where(lane >= HD, pltpu.roll(slab, HD, 1), 0.0)
        do_ref[:, 2 * j * LANES : (2 * j + 1) * LANES] = even.astype(LOW)
        if 2 * j + 1 < heads:
            odd = jnp.where(lane >= HD, slab, 0.0)
            do_ref[:, (2 * j + 1) * LANES : (2 * j + 2) * LANES] = odd.astype(LOW)
    grad_att_t = dot(w_ref[0:width, :], branch, NT).astype(LOW).astype(FULL)
    both = grad_att_t * att_ref[...].astype(FULL)
    for h in range(heads):
        delta_ref[h : h + 1, :] = jnp.sum(both[h * HD : (h + 1) * HD, :], axis=0, keepdims=True)
    delta_ref[heads:, :] = jnp.zeros((delta_ref.shape[0] - heads, span), FULL)


def attend_back_kernel(q_ref, b0, b1, b2, b3, p_ref, do_ref, delta_ref, cos_ref, sin_ref, gq_ref, keep_ref, send_ref):
    span = q_ref.shape[0]
    per = q_ref.shape[1] // LANES
    h = pl.program_id(0)
    kv = jnp.concatenate([b0[...], b1[...], b2[...], b3[...]], axis=0)
    kv_t = kv.T
    cosine, sine_val = cos_ref[0], sin_ref[0]
    total = None
    for i in range(per):
        out_grad = do_ref[:, i * LANES : (i + 1) * LANES]
        probs = p_ref[0, :, i * span : (i + 1) * span]
        grad_probs = dot(kv, out_grad, NT)
        delta = delta_ref[pl.ds(per * h + i, 1), :]
        grad_scores = (probs.astype(FULL) * (grad_probs - delta)).astype(LOW)
        grad_q = dot(kv_t, grad_scores)
        one = grad_q[0 : HD // 2, :] * SCALE
        two = grad_q[HD // 2 : HD, :] * SCALE
        gq_ref[i * HD : i * HD + HD // 2, :] = (one * cosine + two * sine_val).astype(LOW)
        gq_ref[i * HD + HD // 2 : (i + 1) * HD, :] = (two * cosine - one * sine_val).astype(LOW)
        both = dot(grad_scores, q_ref[:, i * LANES : (i + 1) * LANES]) + dot(probs, out_grad)
        total = both if total is None else total + both
    total = total.astype(LOW)
    keep_ref[0] = total[0:span, :]
    send_ref[0] = total[span : 2 * span, :]
    keep_ref[1] = total[2 * span : 3 * span, :]
    send_ref[1] = total[3 * span : 4 * span, :]


def spread(ranks, acc, keep_ref, send_ref):
    part = acc.shape[1] // PARTS
    for k in range(GROUP):
        out = send_ref if k % 2 else keep_ref
        for i, slot in enumerate(SLOTS):
            start = pl.multiple_of((slot ^ ranks[1]) * part, 8)
            out[k // 2, i] = acc[ranks[0] ^ k, pl.ds(start, part), :].astype(LOW)


def out_weight_kernel(ranks, att_a, att_b, gb_a, gb_b, keep_ref, send_ref, acc):
    width = gb_a.shape[1]
    shard = width // GROUP
    for b in range(GROUP):
        rows = slice(b * shard, (b + 1) * shard)
        acc[b, 0:shard, :] = dot(att_a[rows, :], gb_a[...]) + dot(att_b[rows, :], gb_b[...])
        acc[b, shard:, :] = jnp.zeros((acc.shape[1] - shard, width), FULL)
    spread(ranks, acc, keep_ref, send_ref)


def last_kernel(ranks, *refs):
    (norm_ref, gq_a, gq_b) = refs[0:3]
    kv_terms = (refs[3:6], refs[6:9])
    cos_ref, sin_ref = refs[9:11]
    q_blocks, kv_blocks = refs[11:15], refs[15:19]
    tok_ref, gm_a, gm_b, gain_ref, gain_a, gain_b = refs[19:25]
    out_ref, keep_ref, send_ref = refs[25:28]
    wq_ref, wkv_ref, gkv_ref, acc = refs[28:32]
    width = norm_ref.shape[1]
    span = gq_a.shape[1]
    shard = width // GROUP
    kw2 = wkv_ref.shape[1]
    heads = kw2 // LANES
    assemble(ranks[0], q_blocks, wq_ref, shard, width)
    assemble(ranks[0], kv_blocks, wkv_ref, shard, kw2)
    lane = lane_index(span)
    grad_gain = jnp.zeros((1, width), FULL)
    for s in range(2):
        part = slice(s * span, (s + 1) * span)
        e0, e1, e2 = kv_terms[s]
        keys, values = [], []
        for h in range(heads):
            cut = slice(h * LANES, (h + 1) * LANES)
            slab = e0[0, :, cut].astype(FULL) + e1[0, :, cut].astype(FULL) + e2[:, cut].astype(FULL)
            keys.append(turn(slab, cos_ref[part, :], -sin_ref[part, :], lane))
            values.append(slab)
        plain = []
        for t in range(2 * heads):
            if t < heads:
                plain.append(keys[t] if t % 2 == 0 else pltpu.roll(keys[t], HD, 1))
            else:
                plain.append(values[t - heads] if t % 2 else pltpu.roll(values[t - heads], HD, 1))
        for j in range(heads):
            pair = jnp.where(lane < HD, plain[2 * j], plain[2 * j + 1])
            gkv_ref[part, j * LANES : (j + 1) * LANES] = pair.astype(LOW)
        gq = (gq_a, gq_b)[s]
        grad_norm = dot(gq[...], wq_ref[...], TT) + dot(gkv_ref[part, :], wkv_ref[...], NT)
        x = tok_ref[part, :].astype(FULL)
        inverse = lax.rsqrt(jnp.mean(x * x, axis=-1, keepdims=True) + NORM_EPS)
        scaled = grad_norm * gain_ref[0:1, :]
        turned = jnp.mean(scaled * x, axis=-1, keepdims=True)
        out_ref[part, :] = (gm_a, gm_b)[s][...] + inverse * scaled - x * (inverse * inverse * inverse * turned)
        grad_gain = grad_gain + jnp.sum(grad_norm * x * inverse, axis=0, keepdims=True)
    norm_t = norm_ref[...].T
    gain_two = gain_a[0:1, :] + gain_b[0:1, :]
    for b in range(GROUP):
        rows = norm_t[b * shard : (b + 1) * shard, :]
        acc[b, 0:shard, 0:width] = dot(rows[:, 0:span], gq_a[...], NT) + dot(rows[:, span:], gq_b[...], NT)
        acc[b, 0:shard, width:] = dot(rows, gkv_ref[...])
        acc[b, shard:, :] = jnp.zeros((acc.shape[1] - shard, acc.shape[2]), FULL)
        acc[b, shard : shard + 1, 0:width] = grad_gain
        acc[b, shard + 1 : shard + 2, 0:width] = gain_two
    spread(ranks, acc, keep_ref, send_ref)


def place(slot):
    return ((slot >> 2) & 1) + ((slot >> 1) & 1) * 2


def forward_weights_kernel(ranks, even, odd, gate_ref, up_ref, down_ref, scratch):
    part = even.shape[1]
    columns = gate_ref.shape[1]
    for a in range(PARTS):
        slot = ranks[1] ^ a
        index = place(slot)
        rows = slice(a * part, (a + 1) * part)

        @pl.when(slot % 2 == 0)
        def _(rows=rows, index=index):
            gate_ref[rows, :] = even[index, :, 0:columns].astype(FULL)
            up_ref[rows, :] = even[index, :, columns : 2 * columns].astype(FULL)
            scratch[rows, :] = even[index, :, 2 * columns :].astype(FULL)

        @pl.when(slot % 2 == 1)
        def _(rows=rows, index=index):
            gate_ref[rows, :] = odd[index, :, 0:columns].astype(FULL)
            up_ref[rows, :] = odd[index, :, columns : 2 * columns].astype(FULL)
            scratch[rows, :] = odd[index, :, 2 * columns :].astype(FULL)

    down_ref[...] = scratch[...].T


def attention_weights_kernel(ranks, even, odd, even_o, odd_o, q_ref, k_ref, v_ref, o_ref, gain_ref, scratch, scratch_o):
    part = even.shape[1]
    shard, width = q_ref.shape
    kw = k_ref.shape[1]
    for a in range(PARTS):
        slot = ranks[1] ^ a
        index = place(slot)
        rows = slice(a * part, (a + 1) * part)

        @pl.when(slot % 2 == 0)
        def _(rows=rows, index=index):
            scratch[rows, :] = even[index].astype(FULL)
            scratch_o[rows, :] = even_o[index].astype(FULL)

        @pl.when(slot % 2 == 1)
        def _(rows=rows, index=index):
            scratch[rows, :] = odd[index].astype(FULL)
            scratch_o[rows, :] = odd_o[index].astype(FULL)

    q_ref[...] = scratch[0:shard, 0:width]
    k_ref[...] = scratch[0:shard, width : width + kw]
    v_ref[...] = scratch[0:shard, width + kw : width + 2 * kw]
    o_ref[...] = scratch_o[0:shard, :]
    gain_ref[...] = scratch[shard : shard + 8, 0:width]


def tables(places):
    half = HD // 2
    frequency = ROPE_BASE ** (-2.0 * jnp.arange(half, dtype=FULL) / HD)
    spots = places.astype(FULL)
    angles = spots.reshape(-1, 1) * frequency
    cosine, sine_val = jnp.cos(angles), jnp.sin(angles)
    cos_rows = jnp.concatenate([cosine] * 4, axis=1)
    sin_rows = jnp.concatenate([-sine_val, sine_val, -sine_val, sine_val], axis=1)
    cols = spots[:, None, :] * frequency[None, :, None]
    return cos_rows, sin_rows, jnp.cos(cols), jnp.sin(cols)


def body(
    tokens,
    w_query,
    w_key,
    w_value,
    w_out,
    w_gate,
    w_up,
    w_down,
    gain_attn,
    gain_mlp,
    span_order,
    piece_starts,
    cotangent,
):
    ranks = lax.axis_size("rep")
    rank_grp = lax.axis_index("grp")
    seq_count, span, width = tokens.shape
    shard = w_query.shape[0]
    kw = w_key.shape[1]
    kw2 = 2 * kw
    kv_heads = kw // HD
    per = width // kw
    ff = w_gate.shape[1]
    rows = seq_count * span
    length = GROUP * span
    padded = -(-width // LANES) * LANES
    place_of = jnp.stack([rank_grp, lax.axis_index("rep") % PARTS]).astype(jnp.int32)
    any_spec = pl.BlockSpec(memory_space=pl.ANY)

    gains = jnp.zeros((2, 2 * kw2), LOW)
    gains = lax.dynamic_update_slice(gains, jnp.stack([gain_attn, gain_mlp]), (0, rank_grp * shard))
    gains = jnp.pad(gains.reshape(4, kw2), ((0, GAIN_ROWS - 4), (0, 0)))
    kv_shard = jnp.concatenate([jnp.concatenate([w_key, w_value], axis=1), gains], axis=0)
    kv_blocks = group_blocks(kv_shard)
    q_blocks = group_blocks(w_query)
    o_blocks = group_blocks(w_out)
    own_span = lax.dynamic_slice(span_order, (0, rank_grp), (seq_count, 1))
    places = own_span * span + jnp.arange(span, dtype=jnp.int32)[None, :]
    cos_rows, sin_rows, cos_cols, sin_cols = tables(places)
    token_rows = tokens.reshape(rows, width)

    table = whole((rows, LANES))
    norm_low, kv_a, kv_b, gain_rows = call(
        keys_values_kernel,
        "keys_values",
        (shape_of((rows, width)), shape_of((span, kw2)), shape_of((span, kw2)), shape_of((8, width), FULL)),
        prefetch=1,
        grid=(1,),
        in_specs=[whole((rows, width))] + [whole(kv_shard.shape)] * 4 + [table, table],
        out_specs=(whole((rows, width)), whole((span, kw2)), whole((span, kw2)), whole((8, width))),
        scratch=[pltpu.VMEM((width, kw2), LOW)],
        flops=2 * rows * width * kw2,
        moved=4 * rows * width + 2 * width * kw2 + 2 * rows * kw2,
    )(place_of, token_rows, *kv_blocks, cos_rows, sin_rows)
    queries = call(
        queries_kernel,
        "queries",
        shape_of((rows, per * kv_heads * LANES)),
        prefetch=1,
        grid=(1,),
        in_specs=[whole((rows, width))] + [whole((shard, width))] * 4 + [table, table],
        out_specs=whole((rows, per * kv_heads * LANES)),
        scratch=[pltpu.VMEM((width, padded), LOW)],
        flops=2 * rows * width * padded,
        moved=2 * rows * width + 2 * width * width + 4 * rows * width,
    )(place_of, norm_low, *q_blocks, cos_rows, sin_rows)

    kv_all = [group_blocks(kv_a), group_blocks(kv_b)]
    cot_blocks = group_blocks(cotangent)
    head = pl.BlockSpec((span, LANES), lambda h, *_: (0, h))
    stats, attended, middles, x_blocks = [], [], [], []
    for s in range(seq_count):
        probs, att = call(
            functools.partial(attend_kernel, s),
            "attend",
            (shape_of((kv_heads, length, per * span)), shape_of((width, span))),
            prefetch=3,
            grid=(kv_heads,),
            in_specs=[pl.BlockSpec((span, per * LANES), lambda h, *_, s=s: (s, h))] + [head] * 4,
            out_specs=(
                pl.BlockSpec((1, length, per * span), lambda h, *_: (h, 0, 0)),
                pl.BlockSpec((per * HD, span), lambda h, *_: (h, 0)),
            ),
            scratch=[pltpu.VMEM((length, span), FULL)],
            flops=8 * span * length * width * 2,
            moved=2 * kv_heads * length * per * span + 2 * length * kw2 + 6 * span * width,
        )(place_of, span_order, piece_starts, queries, *kv_all[s])
        middle, x = call(
            middle_kernel,
            "middle",
            (shape_of((span, width), FULL), shape_of((span, width))),
            prefetch=1,
            grid=(1,),
            in_specs=[whole((width, span))]
            + [whole((shard, width))] * 4
            + [pl.BlockSpec((1, span, width), lambda *_, s=s: (s, 0, 0)), whole((8, width))],
            out_specs=(whole((span, width)), whole((span, width))),
            scratch=[pltpu.VMEM((width, width), LOW)],
            flops=2 * span * width * width,
            moved=10 * span * width + 2 * width * width,
        )(place_of, att, *o_blocks, tokens, gain_rows)
        stats.append(probs)
        attended.append(att)
        middles.append(middle)
        x_blocks.append(group_blocks(x))

    outs, grads, saved = [], [], []
    for s in range(seq_count):
        block = whole((span, width))
        both = whole((2, span, width))
        per_block = pl.BlockSpec((span, ff), lambda k, *_: (k, 0))
        ko, so, kg, sg, hid, gg, gu = call(
            forward_back_kernel,
            "forward_back",
            (shape_of((2, span, width)),) * 4 + (shape_of((length, ff)),) * 3,
            grid=(GROUP,),
            in_specs=[block] * 4
            + [pl.BlockSpec((1, span, width), lambda *_, s=s: (s, 0, 0))] * 4
            + [whole((width, ff)), whole((width, ff)), whole((ff, width))],
            out_specs=(both,) * 4 + (per_block,) * 3,
            scratch=[pltpu.VMEM((span, width), LOW), pltpu.VMEM((span, width), LOW)],
            flops=12 * length * width * ff,
            moved=6 * width * ff + 8 * length * width + 6 * length * ff,
        )(*x_blocks[s], *cot_blocks, w_gate, w_up, w_down)
        grads.append(group_terms(kg, sg) + (kg, sg))
        outs.append((ko, so))
        saved.append((hid, gg, gu))

    part = width // PARTS
    pieces = call(
        weight_kernel,
        "weights",
        tuple(shape_of((n, part, 3 * ff)) for n in (4, 2, 1, 1)),
        prefetch=1,
        grid=(3,),
        in_specs=[any_spec] * 18,
        out_specs=tuple(pl.BlockSpec((n, part, ff), lambda m, *_: (0, 0, m)) for n in (4, 2, 1, 1)),
        scratch=[
            pltpu.VMEM((2, 2 * GROUP, span, width), LOW),
            pltpu.VMEM((width, 2 * length), LOW),
            pltpu.VMEM((3, 2 * length, ff), LOW),
            pltpu.VMEM((width, ff), FULL),
            pltpu.SemaphoreType.DMA((22,)),
        ],
        flops=12 * length * width * ff,
        moved=8 * length * width + 12 * length * ff + 6 * width * ff,
    )(
        place_of,
        *x_blocks[0],
        *x_blocks[1],
        *cot_blocks,
        saved[0][1],
        saved[0][2],
        saved[0][0],
        saved[1][1],
        saved[1][2],
        saved[1][0],
    )
    ff_even, ff_odd = rep_sum(*pieces, ranks)

    block_out = jnp.stack([middles[s] + three(group_terms(*outs[s])) for s in range(seq_count)])

    branches, mids, gain_twos, kv_grads, q_grads = [], [], [], [], []
    for s in range(seq_count):
        keep_term, beside_term, across_term = grads[s][0:3]
        block = whole((span, width))
        grad_middle, branch, out_grad, delta, gain_two = call(
            branch_kernel,
            "branch",
            (
                shape_of((span, width), FULL),
                shape_of((span, width)),
                shape_of((span, per * kv_heads * LANES)),
                shape_of((16, span), FULL),
                shape_of((8, width), FULL),
            ),
            prefetch=1,
            grid=(1,),
            in_specs=[
                block,
                pl.BlockSpec((1, span, width), lambda *_, s=s: (s, 0, 0)),
                pl.BlockSpec((1, span, width), lambda *_: (0, 0, 0)),
                pl.BlockSpec((1, span, width), lambda *_: (0, 0, 0)),
                block,
                whole((8, width)),
            ]
            + [whole((shard, width))] * 4
            + [whole((width, span))],
            out_specs=(block, block, whole((span, per * kv_heads * LANES)), whole((16, span)), whole((8, width))),
            scratch=[pltpu.VMEM((padded, width), LOW)],
            flops=4 * span * width * width,
            moved=20 * span * width + 2 * width * width,
        )(place_of, middles[s], cotangent, keep_term[None], beside_term[None], across_term, gain_rows, *o_blocks, attended[s])
        column = pl.BlockSpec((1, HD // 2, span), lambda *_, s=s: (s, 0, 0))
        halves = pl.BlockSpec((2, span, LANES), lambda h, *_: (0, 0, h))
        grad_q, kv_keep, kv_send = call(
            attend_back_kernel,
            "attend_back",
            (shape_of((width, span)), shape_of((2, span, kw2)), shape_of((2, span, kw2))),
            grid=(kv_heads,),
            in_specs=[pl.BlockSpec((span, per * LANES), lambda h, *_, s=s: (s, h))]
            + [head] * 4
            + [
                pl.BlockSpec((1, length, per * span), lambda h, *_: (h, 0, 0)),
                pl.BlockSpec((span, per * LANES), lambda h, *_: (0, h)),
                whole((16, span)),
                column,
                column,
            ],
            out_specs=(pl.BlockSpec((per * HD, span), lambda h, *_: (h, 0)), halves, halves),
            flops=16 * span * length * width * 2,
            moved=2 * kv_heads * length * per * span + 4 * length * kw2 + 8 * span * width,
        )(queries, *kv_all[s], stats[s], out_grad, delta, cos_cols, sin_cols)
        q_grads.append(grad_q)
        kv_grads.append(group_terms(kv_keep, kv_send))
        branches.append(branch)
        mids.append(grad_middle)
        gain_twos.append(gain_two)

    grown = shard + GAIN_ROWS
    cut = grown // PARTS
    spread_out = lambda columns: (shape_of((2, PARTS, cut, columns)),) * 2
    spread_spec = lambda columns: (whole((2, PARTS, cut, columns)),) * 2
    out_keep, out_send = call(
        out_weight_kernel,
        "out_weights",
        spread_out(width),
        prefetch=1,
        grid=(1,),
        in_specs=[whole((width, span))] * 2 + [whole((span, width))] * 2,
        out_specs=spread_spec(width),
        scratch=[pltpu.VMEM((GROUP, grown, width), FULL)],
        flops=2 * rows * width * width,
        moved=4 * rows * width + 2 * width * width,
    )(place_of, *attended, *branches)

    def owned(keep, send):
        terms = group_terms(keep, send)
        cuts = (slice(0, 4), slice(4, 6), slice(6, 7), slice(7, 8))
        return [three([t[c] for t in terms]).astype(LOW) for c in cuts]

    o_even, o_odd = rep_sum(*owned(out_keep, out_send), ranks)

    block = whole((span, width))
    one = pl.BlockSpec((1, span, kw2), lambda *_: (0, 0, 0))
    kv_term = [one, one, whole((span, kw2))]
    terms = []
    for keep_term, beside_term, across_term in kv_grads:
        terms += [keep_term[None], beside_term[None], across_term]
    total = width + kw2
    grad_tokens, w_keep, w_send = call(
        last_kernel,
        "last",
        (shape_of((rows, width), FULL),) + spread_out(total),
        prefetch=1,
        grid=(1,),
        in_specs=[whole((rows, width)), whole((width, span)), whole((width, span))]
        + kv_term * 2
        + [table, table]
        + [whole((shard, width))] * 4
        + [whole(kv_shard.shape)] * 4
        + [whole((rows, width)), block, block]
        + [whole((8, width))] * 3,
        out_specs=(whole((rows, width)),) + spread_spec(total),
        scratch=[
            pltpu.VMEM((width, width), LOW),
            pltpu.VMEM((width, kw2), LOW),
            pltpu.VMEM((rows, kw2), LOW),
            pltpu.VMEM((GROUP, grown, total), FULL),
        ],
        flops=4 * rows * width * total,
        moved=14 * rows * width + 4 * width * total,
    )(
        place_of,
        norm_low,
        *q_grads,
        *terms,
        cos_rows,
        sin_rows,
        *q_blocks,
        *kv_blocks,
        token_rows,
        *mids,
        gain_rows,
        *gain_twos,
    )
    w_even, w_odd = rep_sum(*owned(w_keep, w_send), ranks)

    grad_gate, grad_up, grad_down = call(
        forward_weights_kernel,
        "forward_weights",
        (shape_of((width, ff), FULL), shape_of((width, ff), FULL), shape_of((ff, width), FULL)),
        prefetch=1,
        grid=(1,),
        in_specs=[whole((4, part, 3 * ff))] * 2,
        out_specs=(whole((width, ff)), whole((width, ff)), whole((ff, width))),
        scratch=[pltpu.VMEM((width, ff), FULL)],
        moved=18 * width * ff,
    )(place_of, ff_even, ff_odd)
    grad_query, grad_key, grad_value, grad_out, grad_gains = call(
        attention_weights_kernel,
        "attention_weights",
        (
            shape_of((shard, width), FULL),
            shape_of((shard, kw), FULL),
            shape_of((shard, kw), FULL),
            shape_of((shard, width), FULL),
            shape_of((8, width), FULL),
        ),
        prefetch=1,
        grid=(1,),
        in_specs=[whole((4, cut, total))] * 2 + [whole((4, cut, width))] * 2,
        out_specs=(
            whole((shard, width)),
            whole((shard, kw)),
            whole((shard, kw)),
            whole((shard, width)),
            whole((8, width)),
        ),
        scratch=[pltpu.VMEM((grown, total), FULL), pltpu.VMEM((grown, width), FULL)],
        moved=6 * shard * (total + width),
    )(place_of, w_even, w_odd, o_even, o_odd)
    own_gains = lax.dynamic_slice(grad_gains, (0, rank_grp * shard), (2, shard))
    return (
        block_out,
        grad_tokens.reshape(tokens.shape),
        grad_query,
        grad_key,
        grad_value,
        grad_out,
        grad_gate,
        grad_up,
        grad_down,
        own_gains[0],
        own_gains[1],
    )


def solution(mesh):
    placed = (
        P("rep", "grp", None),
        P("grp", None),
        P("grp", None),
        P("grp", None),
        P("grp", None),
        P(None, "grp"),
        P(None, "grp"),
        P("grp", None),
        P("grp"),
        P("grp"),
        P("rep", None),
        P("rep", None),
        P("rep", "grp", None),
    )
    return jax.shard_map(
        body,
        mesh=mesh,
        in_specs=placed,
        out_specs=(
            P("rep", "grp", None),
            P("rep", "grp", None),
            P("grp", None),
            P("grp", None),
            P("grp", None),
            P("grp", None),
            P(None, "grp"),
            P(None, "grp"),
            P("grp", None),
            P("grp"),
            P("grp"),
        ),
        check_vma=False,
    )
```

```python
import functools

import jax
import jax.numpy as jnp
from jax import lax
from jax.experimental import pallas as pl
from jax.experimental.pallas import tpu as pltpu
from jax.sharding import PartitionSpec as P

HD = 64
PIECE = 256
LANES = 128
GROUP = 4
PARTS = 8
GAIN_ROWS = 16
RATE = 1.0e9
SLOTS = (7, 3, 5, 1, 6, 2, 4, 0)


NORM_EPS = 1e-05
ROPE_BASE = 10000.0
MASKED_SCORE = -1e30
SCALE = HD ** (-0.5)

LOW = jnp.bfloat16
FULL = jnp.float32
NN = (((1,), (0,)), ((), ()))
NT = (((1,), (1,)), ((), ()))
TN = (((0,), (0,)), ((), ()))


def dot(left_mat, right_mat, form=NN):
    return lax.dot_general(left_mat, right_mat, form, preferred_element_type=FULL)


def swap(values, axis, count, mask):
    return lax.ppermute(values, axis, [(i, i ^ mask) for i in range(count)])


def after(values, *others):
    return lax.optimization_barrier((values,) + others)[0] if others else values


class Blocks:
    def __init__(self, own, *others):
        self.own = own
        sent = after(own, *others)
        self.across = swap(sent, "grp", GROUP, 2)
        self.sent = sent

    def finish(self, *others):
        pair = after((self.sent, self.across), *others)
        return self.own, swap(pair[0], "grp", GROUP, 1), self.across, swap(pair[1], "grp", GROUP, 1)


class Terms:
    def __init__(self, keep, send):
        self.keep = keep
        self.beside = swap(send, "grp", GROUP, 1)

    def cross(self, *others):
        keep, beside = after((self.keep, self.beside), *others)
        across = (keep[1].astype(FULL) + beside[1].astype(FULL)).astype(LOW)
        self.across = swap(across, "grp", GROUP, 2)
        return across

    def all(self):
        return self.keep, self.beside, self.across


def three(terms):
    return terms[0][0].astype(FULL) + terms[1][0].astype(FULL) + terms[2].astype(FULL)


class RepSum:
    def __init__(self, pieces, ranks):
        self.pieces, self.ranks = pieces, ranks
        self.one = swap(pieces[0], "rep", ranks, 1)

    def second(self, *others):
        self.one = after(self.one, *others)
        two = (self.pieces[1].astype(FULL) + self.one[0:2].astype(FULL)).astype(LOW)
        self.two = swap(two, "rep", self.ranks, 2)
        return two

    def third(self, *others):
        self.two = after(self.two, *others)
        four = self.pieces[2].astype(FULL) + self.one[2:3].astype(FULL) + self.two[0:1].astype(FULL)
        four = four.astype(LOW)
        self.four = swap(four, "rep", self.ranks, 4)
        return four

    def own(self, *others):
        ranks = self.ranks
        self.four = after(self.four, *others)
        mine = self.pieces[3].astype(FULL) + self.one[3:4].astype(FULL) + self.two[1:2].astype(FULL)
        mine = (mine + self.four.astype(FULL)).astype(LOW)
        if ranks > PARTS:
            others = [[j * PARTS + i for j in range(ranks // PARTS)] for i in range(PARTS)]
            mine = lax.psum(mine, "rep", axis_index_groups=others)
        self.mine = mine
        self.back = swap(mine, "rep", ranks, 4)
        return mine

    def spread(self, *others):
        self.back = after(self.back, *others)
        held = jnp.concatenate([self.mine, self.back])
        self.held = held
        self.wide = swap(held, "rep", self.ranks, 2)
        return held

    def done(self, *others):
        self.wide = after(self.wide, *others)
        held = jnp.concatenate([self.held, self.wide])
        return held, swap(held, "rep", self.ranks, 1)


def all_sum(values, ranks):
    for mask in (1, 2):
        values = values + swap(values, "grp", GROUP, mask)
    mask = 1
    while mask < ranks:
        values = values + swap(values, "rep", ranks, mask)
        mask *= 2
    return values


def call(kernel, name, out_shape, *, grid=(1,), prefetch=0, in_specs, out_specs, scratch=(), micros=1, vmem=56):
    return pl.pallas_call(
        kernel,
        name=name,
        out_shape=out_shape,
        grid_spec=pltpu.PrefetchScalarGridSpec(
            num_scalar_prefetch=prefetch,
            grid=grid,
            in_specs=in_specs,
            out_specs=out_specs,
            scratch_shapes=list(scratch),
        ),
        compiler_params=pltpu.CompilerParams(vmem_limit_bytes=vmem << 20),
        cost_estimate=pl.CostEstimate(flops=int(micros * RATE), bytes_accessed=1 << 20, transcendentals=0),
    )


def whole(shape):
    return pl.BlockSpec(shape, lambda *_: (0,) * len(shape))


def shape_of(shape, kind=LOW):
    return jax.ShapeDtypeStruct(shape, kind)


def turn(rows, cosine, sine_val, sign):
    one, two = rows[0 : HD // 2, :], rows[HD // 2 : HD, :]
    sine_val = sine_val * sign
    return one * cosine - two * sine_val, two * cosine + one * sine_val


def assemble(rank, blocks, scratch):
    rows = blocks[0].shape[0]
    for k in range(GROUP):
        start = pl.multiple_of((rank ^ k) * rows, 16)
        scratch[pl.ds(start, rows), :] = blocks[k][...]


def flip_kernel(wg_ref, wu_ref, wdt_ref, wgut_ref, wgu_ref, wd_ref):
    ff = wg_ref.shape[1]
    wgut_ref[0:ff, :] = wg_ref[...].T
    wgut_ref[ff:, :] = wu_ref[...].T
    wgu_ref[:, 0:ff] = wg_ref[...]
    wgu_ref[:, ff:] = wu_ref[...]
    wd_ref[...] = wdt_ref[...].T


def keys_values_kernel(ranks, tok_ref, b0, b1, b2, b3, cos_ref, sin_ref, norm_ref, kv_a, kv_b, gain_ref, w_ref):
    span = tok_ref.shape[2]
    kw2 = kv_a.shape[0]
    kw = kw2 // 2
    assemble(ranks[0], (b0, b1, b2, b3), w_ref)
    gains = w_ref[:, kw2:]
    gain_ref[...] = gains
    gain_one = gains[:, 0:1].astype(FULL)
    for s, out in enumerate((kv_a, kv_b)):
        x = tok_ref[s].astype(FULL)
        inverse = lax.rsqrt(jnp.mean(x * x, axis=0, keepdims=True) + NORM_EPS)
        norm = (x * inverse * gain_one).astype(LOW)
        norm_ref[:, s * span : (s + 1) * span] = norm
        kv = dot(w_ref[:, 0:kw2], norm, TN)
        for h in range(kw // HD):
            one, two = turn(kv[h * HD : (h + 1) * HD, :], cos_ref[s], sin_ref[s], 1.0)
            top = h * 2 * HD
            out[top : top + HD // 2, :] = one.astype(LOW)
            out[top + HD // 2 : top + HD, :] = two.astype(LOW)
            out[top + HD : top + 2 * HD, :] = kv[kw + h * HD : kw + (h + 1) * HD, :].astype(LOW)


def queries_kernel(ranks, norm_ref, b0, b1, b2, b3, cos_ref, sin_ref, q_ref, w_ref):
    width = b0.shape[1]
    span = cos_ref.shape[2]
    assemble(ranks[0], (b0, b1, b2, b3), w_ref)
    for s in range(2):
        part = slice(s * span, (s + 1) * span)
        query = dot(w_ref[...], norm_ref[:, part], TN)
        for h in range(width // HD):
            one, two = turn(query[h * HD : (h + 1) * HD, :], cos_ref[s], sin_ref[s], 1.0)
            q_ref[h * HD : h * HD + HD // 2, part] = (one * SCALE).astype(LOW)
            q_ref[h * HD + HD // 2 : (h + 1) * HD, part] = (two * SCALE).astype(LOW)


def attend_kernel(seq, ranks, order, starts, q_ref, b0, b1, b2, b3, p_ref, o_ref, bias_ref):
    span = q_ref.shape[1]
    per = q_ref.shape[0] // HD
    rank = ranks[0]

    @pl.when(pl.program_id(0) == 0)
    def _():
        query_pos = order[seq, rank] * span + lax.broadcasted_iota(jnp.int32, (span, span), 1)
        query_in = []
        for m in range(2):
            start = starts[seq, m]
            query_in.append((query_pos >= start) & (query_pos < start + PIECE))
        for k in range(GROUP):
            key_pos = order[seq, rank ^ k] * span + lax.broadcasted_iota(jnp.int32, (span, span), 0)
            allowed = key_pos <= query_pos
            for m in range(2):
                start = starts[seq, m]
                key_in = (key_pos >= start) & (key_pos < start + PIECE)
                allowed = allowed | (query_in[m] & key_in)
            bias_ref[k * span : (k + 1) * span, :] = jnp.where(allowed, 0.0, MASKED_SCORE)

    kv_t = jnp.concatenate([b0[...], b1[...], b2[...], b3[...]], axis=1)
    keys = kv_t.T[:, 0:HD]
    values_t = kv_t[HD : 2 * HD, :]
    for i in range(per):
        scores = dot(keys, q_ref[i * HD : (i + 1) * HD, :]) + bias_ref[...]
        peak = jnp.max(scores, axis=0, keepdims=True)
        exponent = jnp.exp(scores - peak)
        total = jnp.sum(exponent, axis=0, keepdims=True)
        probs = (exponent * (1.0 / total)).astype(LOW)
        p_ref[0, :, i * span : (i + 1) * span] = probs
        o_ref[i * HD : (i + 1) * HD, :] = dot(values_t, probs).astype(LOW)


def middle_kernel(ranks, att_ref, b0, b1, b2, b3, tok_ref, gain_ref, mid_ref, x_ref, w_ref):
    assemble(ranks[0], (b0, b1, b2, b3), w_ref)
    middle = tok_ref[0].astype(FULL) + dot(w_ref[...], att_ref[...], TN)
    mid_ref[...] = middle
    inverse = lax.rsqrt(jnp.mean(middle * middle, axis=0, keepdims=True) + NORM_EPS)
    x_ref[...] = (middle * inverse * gain_ref[:, 1:2].astype(FULL)).astype(LOW)


def forward_back_kernel(x0, x1, x2, x3, c0, c1, c2, c3, wgut_ref, wgu_ref, wdt_ref, wd_ref, ko_ref, so_ref, kg_ref, sg_ref, hid_ref, gg_ref, gu_ref, xs, cs, both):
    k = pl.program_id(0)
    ff = wd_ref.shape[0]
    for i, (x, c) in enumerate(((x0, c0), (x1, c1), (x2, c2), (x3, c3))):

        @pl.when(k == i)
        def _(x=x, c=c):
            xs[...] = x[...]
            cs[...] = c[...]

    gate_up = dot(wgut_ref[...], xs[...])
    grad_hidden = dot(wd_ref[...], cs[...])
    gate, up = gate_up[0:ff, :], gate_up[ff:, :]
    sig = 1.0 / (1.0 + jnp.exp(-gate))
    swish = gate * sig
    hidden = (swish * up).astype(LOW)
    grad_gate = (grad_hidden * up * sig * (1.0 + gate * (1.0 - sig))).astype(LOW)
    grad_up = (grad_hidden * swish).astype(LOW)
    hid_ref[...] = hidden
    gg_ref[...] = grad_gate
    gu_ref[...] = grad_up
    both[0:ff, :] = grad_gate
    both[ff:, :] = grad_up
    grad_x = dot(wgu_ref[...], both[...]).astype(LOW)
    out = dot(wdt_ref[...], hid_ref[...]).astype(LOW)
    half = k // 2

    @pl.when(k % 2 == 0)
    def _():
        kg_ref[half] = grad_x
        ko_ref[half] = out

    @pl.when(k % 2 == 1)
    def _():
        sg_ref[half] = grad_x
        so_ref[half] = out


def weight_kernel(stacked, ranks, *refs):
    count = GROUP if stacked else 2 * GROUP
    blocks = refs[0:count]
    rights = refs[count : count + 2]
    outs = refs[count + 2 : count + 6]
    left, right, acc, sem = refs[count + 6 : count + 10]
    span = left.shape[2] // GROUP
    copies = []
    for s in range(2):
        own = []
        for k in range(GROUP):
            source = blocks[k].at[s] if stacked else blocks[s * GROUP + k]
            own.append(pltpu.make_async_copy(source, left.at[s, :, pl.ds(k * span, span)], sem.at[s * 5 + k]))
        own.append(pltpu.make_async_copy(rights[s], right.at[s], sem.at[s * 5 + 4]))
        copies.append(own)
    for own in copies:
        for copy in own:
            copy.start()
    for copy in copies[0]:
        copy.wait()
    acc[...] = dot(left[0], right[0], NT)
    for copy in copies[1]:
        copy.wait()
    acc[...] += dot(left[1], right[1], NT)
    part = acc.shape[0] // PARTS
    places = [(outs[0], i) for i in range(4)] + [(outs[1], 0), (outs[1], 1), (outs[2], 0), (outs[3], 0)]
    for (out, i), slot in zip(places, SLOTS):
        start = pl.multiple_of((slot ^ ranks[1]) * part, 8)
        out[i] = acc[pl.ds(start, part), :].astype(LOW)


def branch_kernel(ranks, mid_ref, cot_ref, e0, e1, e2, gain_ref, b0, b1, b2, b3, att_ref, gm_ref, gb_ref, do_ref, delta_ref, gain_out, w_ref):
    width, span = mid_ref.shape
    assemble(ranks[0], (b0, b1, b2, b3), w_ref)
    middle = mid_ref[...]
    grad = e0[0].astype(FULL) + e1[0].astype(FULL) + e2[...].astype(FULL)
    inverse = lax.rsqrt(jnp.mean(middle * middle, axis=0, keepdims=True) + NORM_EPS)
    scaled = grad * gain_ref[:, 1:2].astype(FULL)
    turned = jnp.mean(scaled * middle, axis=0, keepdims=True)
    grad_middle = cot_ref[0].astype(FULL) + inverse * scaled - middle * (inverse * inverse * inverse * turned)
    gain_out[...] = dot(jnp.ones((8, span), LOW), (grad * middle * inverse).astype(LOW), NT)
    gm_ref[...] = grad_middle
    branch = grad_middle.astype(LOW)
    gb_ref[...] = branch
    grad_att = dot(w_ref[...], branch).astype(LOW)
    do_ref[...] = grad_att
    both = grad_att.astype(FULL) * att_ref[...].astype(FULL)
    heads = width // HD
    for h in range(heads):
        delta_ref[h : h + 1, :] = jnp.sum(both[h * HD : (h + 1) * HD, :], axis=0, keepdims=True)
    delta_ref[heads:, :] = jnp.zeros((delta_ref.shape[0] - heads, span), FULL)


def attend_back_kernel(q_ref, b0, b1, b2, b3, p_ref, do_ref, delta_ref, cos_ref, sin_ref, gq_ref, keep_ref, send_ref, ds_ref):
    span = q_ref.shape[1]
    per = q_ref.shape[0] // HD
    h = pl.program_id(0)
    kv_t = jnp.concatenate([b0[...], b1[...], b2[...], b3[...]], axis=1)
    kv = kv_t.T
    keys_t = kv_t[0:HD, :]
    cosine, sine_val = cos_ref[0], sin_ref[0]
    none = jnp.zeros((HD, span), LOW)
    qs, dos = [], []
    for i in range(per):
        rows = slice(i * HD, (i + 1) * HD)
        out_grad = jnp.concatenate([none, do_ref[rows, :]], axis=0)
        probs = p_ref[0, :, i * span : (i + 1) * span]
        delta = delta_ref[pl.ds(per * h + i, 1), :]
        grad_scores = (probs.astype(FULL) * (dot(kv, out_grad) - delta)).astype(LOW)
        ds_ref[:, i * span : (i + 1) * span] = grad_scores
        one, two = turn(dot(keys_t, grad_scores) * SCALE, cosine, sine_val, -1.0)
        gq_ref[i * HD : i * HD + HD // 2, :] = one.astype(LOW)
        gq_ref[i * HD + HD // 2 : (i + 1) * HD, :] = two.astype(LOW)
        qs.append(jnp.concatenate([q_ref[rows, :], none], axis=0))
        dos.append(out_grad)
    total = dot(ds_ref[...], jnp.concatenate(qs, axis=1), NT)
    total = total + dot(p_ref[0], jnp.concatenate(dos, axis=1), NT)
    total = total.T.astype(LOW)
    keep_ref[0] = total[:, 0:span]
    send_ref[0] = total[:, span : 2 * span]
    keep_ref[1] = total[:, 2 * span : 3 * span]
    send_ref[1] = total[:, 3 * span : 4 * span]


def spread(ranks, acc, keep_ref, send_ref):
    part = acc.shape[1] // PARTS
    for k in range(GROUP):
        out = send_ref if k % 2 else keep_ref
        for i, slot in enumerate(SLOTS):
            start = pl.multiple_of((slot ^ ranks[1]) * part, 8)
            out[k // 2, i] = acc[ranks[0] ^ k, pl.ds(start, part), :].astype(LOW)


def out_weight_kernel(ranks, att_a, att_b, gb_a, gb_b, keep_ref, send_ref, acc):
    width = gb_a.shape[0]
    shard = width // GROUP
    for b in range(GROUP):
        rows = slice(b * shard, (b + 1) * shard)
        acc[b, 0:shard, :] = dot(att_a[rows, :], gb_a[...], NT) + dot(att_b[rows, :], gb_b[...], NT)
        acc[b, shard:, :] = jnp.zeros((acc.shape[1] - shard, width), FULL)
    spread(ranks, acc, keep_ref, send_ref)


def input_weight_kernel(ranks, norm_ref, gq_a, gq_b, a0, a1, a2, b0, b1, b2, cos_ref, sin_ref, keep_ref, send_ref, gkv_ref, acc):
    width = norm_ref.shape[0]
    span = gq_a.shape[1]
    shard = width // GROUP
    kw2 = gkv_ref.shape[0]
    kw = kw2 // 2
    for s, (e0, e1, e2) in enumerate(((a0, a1, a2), (b0, b1, b2))):
        part = slice(s * span, (s + 1) * span)
        grad = e0[0].astype(FULL) + e1[0].astype(FULL) + e2[...].astype(FULL)
        for h in range(kw // HD):
            top = h * 2 * HD
            one, two = turn(grad[top : top + HD, :], cos_ref[s], sin_ref[s], -1.0)
            gkv_ref[h * HD : h * HD + HD // 2, part] = one.astype(LOW)
            gkv_ref[h * HD + HD // 2 : (h + 1) * HD, part] = two.astype(LOW)
            gkv_ref[kw + h * HD : kw + (h + 1) * HD, part] = grad[top + HD : top + 2 * HD, :].astype(LOW)
    for b in range(GROUP):
        rows = slice(b * shard, (b + 1) * shard)
        acc[b, 0:shard, 0:width] = dot(norm_ref[rows, 0:span], gq_a[...], NT) + dot(norm_ref[rows, span:], gq_b[...], NT)
        acc[b, 0:shard, width:] = dot(norm_ref[rows, :], gkv_ref[...], NT)
        acc[b, shard:, :] = jnp.zeros((acc.shape[1] - shard, acc.shape[2]), FULL)
    spread(ranks, acc, keep_ref, send_ref)


def input_grad_kernel(ranks, gq_a, gq_b, gkv_ref, q0, q1, q2, q3, k0, k1, k2, k3, tok_ref, gm_a, gm_b, gain_a, gain_b, out_ref, gain_out, wq_ref, wkv_ref):
    span = gq_a.shape[1]
    kw2 = gkv_ref.shape[0]
    assemble(ranks[0], (q0, q1, q2, q3), wq_ref)
    assemble(ranks[0], (k0, k1, k2, k3), wkv_ref)
    gain_one = wkv_ref[:, kw2 : kw2 + 1].astype(FULL)
    total = None
    for s in range(2):
        part = slice(s * span, (s + 1) * span)
        grad_norm = dot(wq_ref[...], (gq_a, gq_b)[s][...]) + dot(wkv_ref[:, 0:kw2], gkv_ref[:, part])
        x = tok_ref[s].astype(FULL)
        inverse = lax.rsqrt(jnp.mean(x * x, axis=0, keepdims=True) + NORM_EPS)
        scaled = grad_norm * gain_one
        turned = jnp.mean(scaled * x, axis=0, keepdims=True)
        out_ref[s] = (gm_a, gm_b)[s][...] + inverse * scaled - x * (inverse * inverse * inverse * turned)
        row = dot(jnp.ones((8, span), LOW), (grad_norm * x * inverse).astype(LOW), NT)
        total = row if total is None else total + row
    gain_out[0:1, :] = total[0:1, :]
    gain_out[1:2, :] = gain_a[0:1, :] + gain_b[0:1, :]
    gain_out[2:8, :] = total[2:8, :]


def place(slot):
    return ((slot >> 2) & 1) + ((slot >> 1) & 1) * 2


def gathered(ranks, pairs):
    for a in range(PARTS):
        slot = ranks[1] ^ a
        index = place(slot)
        for parity in range(2):

            @pl.when(slot % 2 == parity)
            def _(parity=parity, index=index, a=a):
                for pair in pairs:
                    part = pair[parity].shape[1]
                    pair[2][a * part : (a + 1) * part, :] = pair[parity][index].astype(FULL)


def forward_weights_kernel(ranks, even, odd, out_ref):
    gathered(ranks, [(even, odd, out_ref)])


def attention_weights_kernel(ranks, even, odd, even_o, odd_o, q_ref, k_ref, v_ref, o_ref, scratch, scratch_o):
    shard, width = q_ref.shape
    kw = k_ref.shape[1]
    gathered(ranks, [(even, odd, scratch), (even_o, odd_o, scratch_o)])
    q_ref[...] = scratch[0:shard, 0:width]
    k_ref[...] = scratch[0:shard, width : width + kw]
    v_ref[...] = scratch[0:shard, width + kw : width + 2 * kw]
    o_ref[...] = scratch_o[0:shard, :]


def tables(places):
    half = HD // 2
    frequency = ROPE_BASE ** (-2.0 * jnp.arange(half, dtype=FULL) / HD)
    angles = places.astype(FULL)[:, None, :] * frequency[None, :, None]
    return jnp.cos(angles), jnp.sin(angles)


def body(
    tokens,
    w_query,
    w_key,
    w_value,
    w_out,
    w_gate,
    w_up,
    w_down,
    gain_attn,
    gain_mlp,
    span_order,
    piece_starts,
    cotangent,
):
    ranks = lax.axis_size("rep")
    rank_grp = lax.axis_index("grp")
    seq_count, span, width = tokens.shape
    shard = w_query.shape[0]
    kw = w_key.shape[1]
    kw2 = 2 * kw
    kv_heads = kw // HD
    per = width // kw
    ff = w_gate.shape[1]
    rows = seq_count * span
    length = GROUP * span
    place_of = jnp.stack([rank_grp, lax.axis_index("rep") % PARTS]).astype(jnp.int32)
    any_spec = pl.BlockSpec(memory_space=pl.ANY)
    tok_t = jnp.swapaxes(tokens, 1, 2)
    cot_t = jnp.swapaxes(cotangent, 1, 2)
    wd_t = w_down.T

    gains = jnp.pad(jnp.stack([gain_attn, gain_mlp], axis=1), ((0, 0), (0, LANES - 2)))
    kv_shard = jnp.concatenate([w_key, w_value, gains], axis=1)
    kv_flight = Blocks(kv_shard)
    q_flight = Blocks(w_query)
    own_span = lax.dynamic_slice(span_order, (0, rank_grp), (seq_count, 1))
    places = own_span * span + jnp.arange(span, dtype=jnp.int32)[None, :]
    cos_cols, sin_cols = tables(places)
    table = whole(cos_cols.shape)
    tok_spec = whole(tok_t.shape)
    wgut, wgu, wd = call(
        flip_kernel,
        "flip",
        (shape_of((2 * ff, width)), shape_of((width, 2 * ff)), shape_of((ff, width))),
        in_specs=[whole((width, ff))] * 3,
        out_specs=(whole((2 * ff, width)), whole((width, 2 * ff)), whole((ff, width))),
            micros=5,
    )(after(w_gate, kv_flight.sent), w_up, wd_t)
    kv_blocks = kv_flight.finish()

    one_seq = lambda s: pl.BlockSpec((1, width, span), lambda *_: (s, 0, 0))
    act = whole((width, span))
    norm_low, kv_a, kv_b, gain_cols = call(
        keys_values_kernel,
        "keys_values",
        (shape_of((width, rows)), shape_of((kw2, span)), shape_of((kw2, span)), shape_of((width, LANES))),
        prefetch=1,
        in_specs=[tok_spec] + [whole(kv_shard.shape)] * 4 + [table, table],
        out_specs=(whole((width, rows)), whole((kw2, span)), whole((kw2, span)), whole((width, LANES))),
        scratch=[pltpu.VMEM((width, kw2 + LANES), LOW)],
            micros=4.5,
    )(place_of, after(tok_t, wgut), *kv_blocks, cos_cols, sin_cols)
    kv_flight = [Blocks(kv_a), Blocks(kv_b, kv_a)]
    q_blocks = q_flight.finish(norm_low)
    queries = call(
        queries_kernel,
        "queries",
        shape_of((width, rows)),
        prefetch=1,
        in_specs=[whole((width, rows))] + [whole((shard, width))] * 4 + [table, table],
        out_specs=whole((width, rows)),
        scratch=[pltpu.VMEM((width, width), LOW)],
            micros=5,
    )(place_of, norm_low, *q_blocks, cos_cols, sin_cols)

    o_flight = Blocks(w_out, queries)
    cot_flight = [Blocks(cot_t[0], queries, o_flight.sent), None]
    kv_all = [kv_flight[0].finish(queries), None]
    cot_blocks = [None, None]
    head = pl.BlockSpec((2 * HD, span), lambda h, *_: (h, 0))
    probs_spec = pl.BlockSpec((1, length, per * span), lambda h, *_: (h, 0, 0))
    q_spec = lambda s: pl.BlockSpec((per * HD, span), lambda h, *_: (h, s))
    per_head = pl.BlockSpec((per * HD, span), lambda h, *_: (h, 0))
    def attend_of(s, query):
        return call(
            functools.partial(attend_kernel, s),
            "attend",
            (shape_of((kv_heads, length, per * span)), shape_of((width, span))),
            prefetch=3,
            grid=(kv_heads,),
            in_specs=[q_spec(s)] + [head] * 4,
            out_specs=(probs_spec, per_head),
            scratch=[pltpu.VMEM((length, span), FULL)],
            micros=16,
        )(place_of, span_order, piece_starts, query, *kv_all[s])

    def middle_of(s, att):
        return call(
            middle_kernel,
            "middle",
            (shape_of((width, span), FULL), shape_of((width, span))),
            prefetch=1,
            in_specs=[act] + [whole((shard, width))] * 4 + [one_seq(s), whole((width, LANES))],
            out_specs=(act, act),
            scratch=[pltpu.VMEM((width, width), LOW)],
            micros=4.6,
        )(place_of, att, *o_blocks, tok_t, gain_cols)

    probs_a, att_a = attend_of(0, queries)
    o_blocks = o_flight.finish(att_a)
    kv_all[1] = kv_flight[1].finish(att_a)
    middle_a, x_a = middle_of(0, att_a)
    x_flight = [Blocks(x_a), None]
    cot_flight[1] = Blocks(cot_t[1], x_flight[0].sent, x_a)
    probs_b, att_b = attend_of(1, after(queries, x_a))
    cot_blocks[0] = cot_flight[0].finish(att_b)
    middle_b, x_b = middle_of(1, att_b)
    x_blocks = [x_flight[0].finish(middle_b), None]
    x_flight[1] = Blocks(x_b)
    stats, attended, middles = (probs_a, probs_b), (att_a, att_b), (middle_a, middle_b)

    def forward_back(s, *others):
        both = whole((2, width, span))
        per_block = pl.BlockSpec((ff, span), lambda k, *_: (0, k))
        return call(
            forward_back_kernel,
            "forward_back",
            (shape_of((2, width, span)),) * 4 + (shape_of((ff, length)),) * 3,
            grid=(GROUP,),
            in_specs=[act] * 8
            + [whole((2 * ff, width)), whole((width, 2 * ff)), whole((width, ff)), whole((ff, width))],
            out_specs=(both,) * 4 + (per_block,) * 3,
            scratch=[pltpu.VMEM((width, span), LOW), pltpu.VMEM((width, span), LOW), pltpu.VMEM((2 * ff, span), LOW)],
            micros=19,
        )(*x_blocks[s], *cot_blocks[s], after(wgut, *others), wgu, wd_t, wd)

    ko_a, so_a, kg_a, sg_a, hid_a, gg_a, gu_a = forward_back(0, x_b)
    grad_a = Terms(kg_a, sg_a)
    x_blocks[1] = x_flight[1].finish(hid_a)
    cot_blocks[1] = cot_flight[1].finish(hid_a)
    ko_b, so_b, kg_b, sg_b, hid_b, gg_b, gu_b = forward_back(1, hid_a)
    grad_b = Terms(kg_b, sg_b)
    grad_a.cross(hid_b)
    grads = (grad_a, grad_b)

    part = width // PARTS

    def weights(name, stacked, blocks, rights):
        return call(
            functools.partial(weight_kernel, stacked),
            name,
            tuple(shape_of((n, part, ff)) for n in (4, 2, 1, 1)),
            prefetch=1,
            in_specs=[any_spec] * (len(blocks) + 2),
            out_specs=tuple(whole((n, part, ff)) for n in (4, 2, 1, 1)),
            scratch=[
                pltpu.VMEM((2, width, length), LOW),
                pltpu.VMEM((2, ff, length), LOW),
                pltpu.VMEM((width, ff), FULL),
                pltpu.SemaphoreType.DMA((10,)),
            ],
            micros=8,
        )(place_of, *blocks, *rights)

    def sums(name, stacked, blocks, rights, *others):
        return RepSum(weights(name, stacked, blocks, (after(rights[0], *others), rights[1])), ranks)

    x_all = x_blocks[0] + x_blocks[1]
    cot_all = cot_blocks[0] + cot_blocks[1]
    down_sum = sums("down_weights", False, cot_all, (hid_a, hid_b), grad_b.beside)
    grad_b.cross(down_sum.pieces[0])
    gate_sum = sums("gate_weights", False, x_all, (gg_a, gg_b), down_sum.pieces[0])
    up_sum = sums("up_weights", False, x_all, (gu_a, gu_b), gate_sum.pieces[0])
    out_a = Terms(ko_a, after(so_a, gate_sum.pieces[0]))
    out_b = Terms(ko_b, after(so_b, gate_sum.pieces[0]))

    def branch_of(s, middle):
        keep_term, beside_term, across_term = grads[s].all()
        return call(
            branch_kernel,
            "branch",
            (
                shape_of((width, span), FULL),
                shape_of((width, span)),
                shape_of((width, span)),
                shape_of((16, span), FULL),
                shape_of((8, width), FULL),
            ),
            prefetch=1,
            in_specs=[act, one_seq(s), one_seq(0), one_seq(0), act, whole((width, LANES))]
            + [whole((shard, width))] * 4
            + [act],
            out_specs=(act, act, act, whole((16, span)), whole((8, width))),
            scratch=[pltpu.VMEM((width, width), LOW)],
            micros=5.7,
        )(place_of, middle, cot_t, keep_term, beside_term, across_term, gain_cols, *o_blocks, attended[s])

    def attend_back_of(s, out_grad, delta):
        column = pl.BlockSpec((1, HD // 2, span), lambda *_: (s, 0, 0))
        halves = pl.BlockSpec((2, 2 * HD, span), lambda h, *_: (0, h, 0))
        grad_q, kv_keep, kv_send = call(
            attend_back_kernel,
            "attend_back",
            (shape_of((width, span)), shape_of((2, kw2, span)), shape_of((2, kw2, span))),
            grid=(kv_heads,),
            in_specs=[q_spec(s)] + [head] * 4 + [probs_spec, per_head, whole((16, span)), column, column],
            out_specs=(per_head, halves, halves),
            scratch=[pltpu.VMEM((length, per * span), LOW)],
            micros=15,
        )(queries, *kv_all[s], stats[s], out_grad, delta, cos_cols, sin_cols)
        return grad_q, Terms(kv_keep, kv_send)

    mid_a, branch_a, dout_a, delta_a, gain_a = branch_of(0, after(middles[0], up_sum.pieces[0]))
    out_a.cross(branch_a)
    out_b.cross(branch_a)
    dout_a = after(dout_a, down_sum.second(branch_a))
    gq_a, kv_grad_a = attend_back_of(0, dout_a, delta_a)
    mid_b, branch_b, dout_b, delta_b, gain_b = branch_of(1, after(middles[1], gq_a))
    kv_grad_a.cross(branch_b)
    block_out = jnp.stack(
        [middle + three(after(term.all(), gq_a)) for middle, term in zip(middles, (out_a, out_b))]
    )
    dout_b = after(dout_b, gate_sum.second(gq_a), down_sum.third(gq_a))
    grown = shard + GAIN_ROWS
    cut = grown // PARTS
    spread_out = lambda columns: (shape_of((2, PARTS, cut, columns)),) * 2
    spread_spec = lambda columns: (whole((2, PARTS, cut, columns)),) * 2
    out_parts = call(
        out_weight_kernel,
        "out_weights",
        spread_out(width),
        prefetch=1,
        in_specs=[act] * 4,
        out_specs=spread_spec(width),
        scratch=[pltpu.VMEM((GROUP, grown, width), FULL)],
            micros=5,
    )(place_of, *attended, branch_a, branch_b)

    def owned(terms):
        keep, beside, across = terms.all()
        cuts = (slice(0, 4), slice(4, 6), slice(6, 7), slice(7, 8))
        return [three((keep[:, c], beside[:, c], across[c])).astype(LOW) for c in cuts]

    out_terms = Terms(*out_parts)
    gq_b, kv_grad_b = attend_back_of(1, after(dout_b, out_parts[0]), delta_b)
    kv_grad_b.cross(gq_b)
    out_terms.cross(kv_grad_b.across)
    up_sum.second(gq_b)
    gate_sum.third(gq_b)
    down_sum.own(gq_b)

    one = pl.BlockSpec((1, kw2, span), lambda *_: (0, 0, 0))
    kv_term = [one, one, whole((kw2, span))]
    terms = []
    for term in (kv_grad_a, kv_grad_b):
        terms += term.all()
    total = width + kw2
    w_keep, w_send, gkv = call(
        input_weight_kernel,
        "input_weights",
        spread_out(total) + (shape_of((kw2, rows)),),
        prefetch=1,
        in_specs=[whole((width, rows)), act, act] + kv_term * 2 + [table, table],
        out_specs=spread_spec(total) + (whole((kw2, rows)),),
        scratch=[pltpu.VMEM((GROUP, grown, total), FULL)],
            micros=7,
    )(place_of, norm_low, gq_a, gq_b, *terms, cos_cols, sin_cols)
    w_terms = Terms(w_keep, w_send)
    grad_tokens, gain_part = call(
        input_grad_kernel,
        "input_grad",
        (shape_of((seq_count, width, span), FULL), shape_of((8, width), FULL)),
        prefetch=1,
        in_specs=[act, act, whole((kw2, rows))]
        + [whole((shard, width))] * 4
        + [whole(kv_shard.shape)] * 4
        + [tok_spec, act, act]
        + [whole((8, width))] * 2,
        out_specs=(tok_spec, whole((8, width))),
        scratch=[pltpu.VMEM((width, width), LOW), pltpu.VMEM((width, kw2 + LANES), LOW)],
            micros=8,
    )(place_of, gq_a, gq_b, gkv, *q_blocks, *kv_blocks, tok_t, mid_a, mid_b, gain_a, gain_b)
    w_terms.cross(grad_tokens)
    out_sum = RepSum(owned(out_terms), ranks)
    w_sum = RepSum(owned(w_terms), ranks)
    grad_gains = all_sum(gain_part, ranks)

    up_sum.third(w_keep)
    gate_sum.own(w_keep)
    for chain in (out_sum, w_sum):
        chain.second()
        chain.third()
    every = (down_sum, gate_sum, up_sum, out_sum, w_sum)
    for chain in (up_sum, out_sum, w_sum):
        chain.own()
    for chain in every:
        chain.spread()
    down_pair, gate_pair, up_pair, out_pair, w_pair = [chain.done() for chain in every]

    def finished(name, pair):
        return call(
            forward_weights_kernel,
            name,
            shape_of((width, ff), FULL),
            prefetch=1,
            in_specs=[whole((4, part, ff))] * 2,
            out_specs=whole((width, ff)),
            micros=3.6,
        )(place_of, *pair)

    grad_down = finished("down_done", down_pair).T
    grad_gate = finished("gate_done", gate_pair)
    grad_up = finished("up_done", up_pair)
    grad_query, grad_key, grad_value, grad_out = call(
        attention_weights_kernel,
        "attention_weights",
        (
            shape_of((shard, width), FULL),
            shape_of((shard, kw), FULL),
            shape_of((shard, kw), FULL),
            shape_of((shard, width), FULL),
        ),
        prefetch=1,
        in_specs=[whole((4, cut, total))] * 2 + [whole((4, cut, width))] * 2,
        out_specs=(whole((shard, width)), whole((shard, kw)), whole((shard, kw)), whole((shard, width))),
        scratch=[pltpu.VMEM((grown, total), FULL), pltpu.VMEM((grown, width), FULL)],
            micros=4,
    )(place_of, *w_pair, *out_pair)
    own_gains = lax.dynamic_slice(grad_gains, (0, rank_grp * shard), (2, shard))
    return (
        jnp.swapaxes(block_out, 1, 2),
        jnp.swapaxes(grad_tokens, 1, 2),
        grad_query,
        grad_key,
        grad_value,
        grad_out,
        grad_gate,
        grad_up,
        grad_down,
        own_gains[0],
        own_gains[1],
    )


def solution(mesh):
    placed = (
        P("rep", "grp", None),
        P("grp", None),
        P("grp", None),
        P("grp", None),
        P("grp", None),
        P(None, "grp"),
        P(None, "grp"),
        P("grp", None),
        P("grp"),
        P("grp"),
        P("rep", None),
        P("rep", None),
        P("rep", "grp", None),
    )
    return jax.shard_map(
        body,
        mesh=mesh,
        in_specs=placed,
        out_specs=(
            P("rep", "grp", None),
            P("rep", "grp", None),
            P("grp", None),
            P("grp", None),
            P("grp", None),
            P("grp", None),
            P(None, "grp"),
            P(None, "grp"),
            P("grp", None),
            P("grp"),
            P("grp"),
        ),
        check_vma=False,
    )
```

```python
import functools

import jax
import jax.numpy as jnp
from jax import lax
from jax.experimental import pallas as pl
from jax.experimental.pallas import tpu as pltpu
from jax.sharding import PartitionSpec as P

HD = 64
PIECE = 256
LANES = 128
GROUP = 4
PARTS = 8
GAIN_ROWS = 16
RATE = 2.0e8
SLOTS = (7, 3, 5, 1, 6, 2, 4, 0)


NORM_EPS = 1e-05
ROPE_BASE = 10000.0
MASKED_SCORE = -1e30
SCALE = HD ** (-0.5)

LOW = jnp.bfloat16
FULL = jnp.float32
NN = (((1,), (0,)), ((), ()))
NT = (((1,), (1,)), ((), ()))
TN = (((0,), (0,)), ((), ()))


def dot(left_mat, right_mat, form=NN):
    return lax.dot_general(left_mat, right_mat, form, preferred_element_type=FULL)


def swap(values, axis, count, mask):
    return lax.ppermute(values, axis, [(i, i ^ mask) for i in range(count)])


def after(values, *others):
    return lax.optimization_barrier((values,) + others)[0] if others else values


class Blocks:
    def __init__(self, own, *others):
        self.own = own
        sent = after(own, *others)
        self.across = swap(sent, "grp", GROUP, 2)
        self.sent = sent

    def arrive(self, *others):
        pair = after((self.sent, self.across), *others)
        self.ready = pair
        self.core = swap(pair[0], "grp", GROUP, 1), swap(pair[1], "grp", GROUP, 1)

    def finish(self, *others):
        if not hasattr(self, "core"):
            self.arrive(*others)
        beside, corner = after(self.core, *others)
        return self.own, beside, self.across, corner


class Terms:
    def __init__(self, own, far, send):
        self.own, self.far = own, far
        self.beside = swap(send, "grp", GROUP, 1)

    def cross(self, *others):
        far, beside = after((self.far, self.beside), *others)
        across = (far.astype(FULL) + beside[1].astype(FULL)).astype(LOW)
        self.sent = across
        self.across = swap(across, "grp", GROUP, 2)
        return across

    def all(self):
        return self.own, self.beside, self.across


def three(terms):
    return terms[0].astype(FULL) + terms[1][0].astype(FULL) + terms[2].astype(FULL)


class RepSum:
    def __init__(self, pieces, ranks):
        self.pieces, self.ranks = pieces, ranks
        self.one = swap(pieces[0], "rep", ranks, 1)

    def second(self, *others):
        self.one = after(self.one, *others)
        two = (self.pieces[1].astype(FULL) + self.one[0:2].astype(FULL)).astype(LOW)
        self.held_two = two
        self.two = swap(two, "rep", self.ranks, 2)
        return two

    def third(self, *others):
        self.two = after(self.two, *others)
        four = self.pieces[2].astype(FULL) + self.one[2:3].astype(FULL) + self.two[0:1].astype(FULL)
        four = four.astype(LOW)
        self.four = swap(four, "rep", self.ranks, 4)
        return four

    def own(self, *others):
        ranks = self.ranks
        self.four = after(self.four, *others)
        mine = self.pieces[3].astype(FULL) + self.one[3:4].astype(FULL) + self.two[1:2].astype(FULL)
        mine = (mine + self.four.astype(FULL)).astype(LOW)
        if ranks > PARTS:
            others = [[j * PARTS + i for j in range(ranks // PARTS)] for i in range(PARTS)]
            mine = lax.psum(mine, "rep", axis_index_groups=others)
        self.mine = mine
        self.back = swap(mine, "rep", ranks, 4)
        return mine

    def spread(self, *others):
        self.back = after(self.back, *others)
        held = jnp.concatenate([self.mine, self.back])
        self.held = held
        self.wide = swap(held, "rep", self.ranks, 2)
        return held

    def done(self, *others):
        self.wide = after(self.wide, *others)
        held = jnp.concatenate([self.held, self.wide])
        return held, swap(held, "rep", self.ranks, 1)


class SmallSum:
    def __init__(self, values, ranks):
        self.values = values
        self.steps = [("grp", GROUP, 1), ("grp", GROUP, 2)]
        mask = 1
        while mask < ranks:
            self.steps.append(("rep", ranks, mask))
            mask *= 2
        self.flight = None

    def step(self, *others):
        if self.flight is not None:
            self.values = self.values + after(self.flight, *others)
        if self.steps:
            self.flight = swap(self.values, *self.steps.pop(0))
        return self.values

    def finish(self):
        while self.steps:
            self.step()
        self.step()
        return self.values


def call(kernel, name, out_shape, *, grid=(1,), prefetch=0, in_specs, out_specs, scratch=(), micros=1, vmem=30):
    def lies(shape):
        return pltpu.HBM(shape.shape, shape.dtype)

    several = isinstance(out_shape, tuple)
    run = pl.pallas_call(
        kernel,
        name=name,
        out_shape=tuple(map(lies, out_shape)) if several else lies(out_shape),
        grid_spec=pltpu.PrefetchScalarGridSpec(
            num_scalar_prefetch=prefetch,
            grid=grid,
            in_specs=in_specs,
            out_specs=out_specs,
            scratch_shapes=list(scratch),
        ),
        compiler_params=pltpu.CompilerParams(vmem_limit_bytes=vmem << 20),
        cost_estimate=pl.CostEstimate(flops=int(micros * RATE), bytes_accessed=1 << 10, transcendentals=0),
    )

    def placed(*args):
        rest = [
            arg if spec is NEAR else pltpu.with_memory_space_constraint(arg, pltpu.HBM)
            for arg, spec in zip(args[prefetch:], in_specs, strict=True)
        ]
        return run(*args[:prefetch], *rest)

    return placed


def whole(shape):
    return pl.BlockSpec(shape, lambda *_: (0,) * len(shape))


ANY = pl.BlockSpec(memory_space=pl.ANY)
NEAR = pl.BlockSpec(memory_space=pltpu.VMEM)


def shape_of(shape, kind=LOW):
    return jax.ShapeDtypeStruct(shape, kind)


def turn(rows, cosine, sine_val, sign):
    one, two = rows[0 : HD // 2, :], rows[HD // 2 : HD, :]
    sine_val = sine_val * sign
    return one * cosine - two * sine_val, two * cosine + one * sine_val


def assemble(rank, blocks, scratch):
    rows = blocks[0].shape[0]
    for k in range(GROUP):
        start = pl.multiple_of((rank ^ k) * rows, 16)
        scratch[pl.ds(start, rows), :] = blocks[k][...]


def pack_kernel(wk_ref, wv_ref, gains_ref, out_ref):
    kw, shard = wk_ref.shape
    out_ref[:, 0:kw] = wk_ref[...].T
    out_ref[:, kw : 2 * kw] = wv_ref[...].T
    gains = jnp.concatenate([gains_ref[...], jnp.zeros((LANES - 2, shard), FULL)], axis=0)
    out_ref[:, 2 * kw :] = gains.T.astype(LOW)


def flip_two_kernel(wg_ref, wu_ref, wgut_ref, wgu_ref):
    ff = wg_ref.shape[1]
    wgut_ref[0:ff, :] = wg_ref[...].T
    wgut_ref[ff:, :] = wu_ref[...].T
    wgu_ref[:, 0:ff] = wg_ref[...]
    wgu_ref[:, ff:] = wu_ref[...]


def flip_one_kernel(wdt_ref, wd_ref):
    wd_ref[...] = wdt_ref[...].T


def keys_values_kernel(ranks, tok_ref, b0, b1, b2, b3, cos_ref, sin_ref, norm_ref, kv_a, kv_b, gain_ref, w_ref):
    span = tok_ref.shape[2]
    kw2 = kv_a.shape[0]
    kw = kw2 // 2
    assemble(ranks[0], (b0, b1, b2, b3), w_ref)
    gains = w_ref[:, kw2:]
    gain_ref[...] = gains
    gain_one = gains[:, 0:1].astype(FULL)
    for s, out in enumerate((kv_a, kv_b)):
        x = tok_ref[s].astype(FULL)
        inverse = lax.rsqrt(jnp.mean(x * x, axis=0, keepdims=True) + NORM_EPS)
        norm = (x * inverse * gain_one).astype(LOW)
        norm_ref[:, s * span : (s + 1) * span] = norm
        kv = dot(w_ref[:, 0:kw2], norm, TN)
        for h in range(kw // HD):
            one, two = turn(kv[h * HD : (h + 1) * HD, :], cos_ref[s], sin_ref[s], 1.0)
            top = h * 2 * HD
            out[top : top + HD // 2, :] = one.astype(LOW)
            out[top + HD // 2 : top + HD, :] = two.astype(LOW)
            out[top + HD : top + 2 * HD, :] = kv[kw + h * HD : kw + (h + 1) * HD, :].astype(LOW)


def queries_kernel(ranks, norm_ref, b0, b1, b2, b3, cos_ref, sin_ref, q_ref, w_ref):
    width = b0.shape[1]
    span = cos_ref.shape[2]
    assemble(ranks[0], (b0, b1, b2, b3), w_ref)
    for s in range(2):
        part = slice(s * span, (s + 1) * span)
        query = dot(w_ref[...], norm_ref[:, part], TN)
        for h in range(width // HD):
            one, two = turn(query[h * HD : (h + 1) * HD, :], cos_ref[s], sin_ref[s], 1.0)
            q_ref[h * HD : h * HD + HD // 2, part] = (one * SCALE).astype(LOW)
            q_ref[h * HD + HD // 2 : (h + 1) * HD, part] = (two * SCALE).astype(LOW)


def beside(ref):
    return jnp.concatenate([ref[i : i + HD, :] for i in range(0, ref.shape[0], HD)], axis=1)


def attend_kernel(seq, ranks, order, starts, q_ref, b0, b1, b2, b3, p_ref, o_ref, bias_ref):
    span = q_ref.shape[1]
    per = q_ref.shape[0] // HD
    rank = ranks[0]

    @pl.when(pl.program_id(0) == 0)
    def _():
        query_pos = order[seq, rank] * span + lax.broadcasted_iota(jnp.int32, (span, span), 1)
        query_in = []
        for m in range(2):
            start = starts[seq, m]
            query_in.append((query_pos >= start) & (query_pos < start + PIECE))
        for k in range(GROUP):
            key_pos = order[seq, rank ^ k] * span + lax.broadcasted_iota(jnp.int32, (span, span), 0)
            allowed = key_pos <= query_pos
            for m in range(2):
                start = starts[seq, m]
                key_in = (key_pos >= start) & (key_pos < start + PIECE)
                allowed = allowed | (query_in[m] & key_in)
            bias_ref[k * span : (k + 1) * span, :] = jnp.where(allowed, 0.0, MASKED_SCORE)

    kv_t = jnp.concatenate([b0[...], b1[...], b2[...], b3[...]], axis=1)
    keys = kv_t.T[:, 0:HD]
    values_t = kv_t[HD : 2 * HD, :]
    bias = jnp.concatenate([bias_ref[...]] * per, axis=1)
    scores = dot(keys, beside(q_ref)) + bias
    peak = jnp.max(scores, axis=0, keepdims=True)
    exponent = jnp.exp(scores - peak)
    total = jnp.sum(exponent, axis=0, keepdims=True)
    probs = (exponent * (1.0 / total)).astype(LOW)
    p_ref[0] = probs
    mixed = dot(values_t, probs).astype(LOW)
    for i in range(per):
        o_ref[i * HD : (i + 1) * HD, :] = mixed[:, i * span : (i + 1) * span]


def middle_kernel(ranks, att_ref, b0, b1, b2, b3, tok_ref, gain_ref, mid_ref, x_ref, w_ref):
    assemble(ranks[0], (b0, b1, b2, b3), w_ref)
    middle = tok_ref[0].astype(FULL) + dot(w_ref[...], att_ref[...], TN)
    mid_ref[...] = middle
    inverse = lax.rsqrt(jnp.mean(middle * middle, axis=0, keepdims=True) + NORM_EPS)
    x_ref[...] = (middle * inverse * gain_ref[:, 1:2].astype(FULL)).astype(LOW)


def forward_back_step(x, cot, wgut_ref, wgu_ref, wdt_ref, wd_ref, hid_ref, gg_ref, gu_ref, both):
    ff = wd_ref.shape[0]
    gate_up = dot(wgut_ref[...], x)
    grad_hidden = dot(wd_ref[...], cot)
    gate, up = gate_up[0:ff, :], gate_up[ff:, :]
    sig = 1.0 / (1.0 + jnp.exp(-gate))
    swish = gate * sig
    hidden = (swish * up).astype(LOW)
    grad_gate = (grad_hidden * up * sig * (1.0 + gate * (1.0 - sig))).astype(LOW)
    grad_up = (grad_hidden * swish).astype(LOW)
    hid_ref[...] = hidden
    gg_ref[...] = grad_gate
    gu_ref[...] = grad_up
    both[0:ff, :] = grad_gate
    both[ff:, :] = grad_up
    return dot(wgu_ref[...], both[...]).astype(LOW), dot(wdt_ref[...], hidden).astype(LOW)


def own_block_kernel(x_a, x_b, cot_ref, wgut_ref, wgu_ref, wdt_ref, wd_ref, out_ref, grad_ref, hid_ref, gg_ref, gu_ref, held, both):
    s = pl.program_id(0)
    for i, x in enumerate((x_a, x_b)):

        @pl.when(s == i)
        def _(x=x):
            held[...] = x[...]

    grad_x, out = forward_back_step(
        held[...], cot_ref[0], wgut_ref, wgu_ref, wdt_ref, wd_ref, hid_ref.at[0], gg_ref.at[0], gu_ref.at[0], both
    )
    grad_ref[0] = grad_x
    out_ref[0] = out


def other_blocks_kernel(*refs):
    blocks = refs[0:6]
    weights = refs[6:10]
    fo_ref, so_ref, fg_ref, sg_ref, hid_ref, gg_ref, gu_ref, held, both, sem = refs[10:]
    k = pl.program_id(0)
    copies = [pltpu.make_async_copy(block, held.at[i], sem.at[i]) for i, block in enumerate(blocks)]

    @pl.when(k == 0)
    def _():
        for i in range(3):
            copies[i].start()
            copies[3 + i].start()

    for i in range(3):

        @pl.when(k == i)
        def _(i=i):
            copies[i].wait()
            copies[3 + i].wait()

    grad_x, out = forward_back_step(held[k], held[3 + k], *weights, hid_ref, gg_ref, gu_ref, both)

    @pl.when(k == 1)
    def _():
        fg_ref[...] = grad_x
        fo_ref[...] = out

    @pl.when(k != 1)
    def _():
        sg_ref[0] = grad_x
        so_ref[0] = out


def weight_kernel(ranks, *refs):
    blocks = refs[0 : 2 * GROUP]
    own, *others = refs[2 * GROUP : 2 * GROUP + 3]
    outs = refs[2 * GROUP + 3 : 2 * GROUP + 7]
    left, right, acc, sem = refs[2 * GROUP + 7 :]
    span = left.shape[2] // GROUP
    copies = []
    for b, block in enumerate(blocks):
        s, k = divmod(b, GROUP)
        copies.append(pltpu.make_async_copy(block, left.at[s, :, pl.ds(k * span, span)], sem.at[b]))
    for s in range(2):
        for i, (source, part) in enumerate(((own.at[s], slice(0, span)), (others[s], slice(span, GROUP * span)))):
            copy = pltpu.make_async_copy(source, right.at[s, :, part], sem.at[2 * GROUP + 2 * s + i])
            copies.insert(s * (GROUP + 2), copy)
    for copy in copies:
        copy.start()
    for copy in copies[: GROUP + 2]:
        copy.wait()
    acc[...] = dot(left[0], right[0], NT)
    for copy in copies[GROUP + 2 :]:
        copy.wait()
    acc[...] += dot(left[1], right[1], NT)
    part = acc.shape[0] // PARTS
    places = [(outs[0], i) for i in range(4)] + [(outs[1], 0), (outs[1], 1), (outs[2], 0), (outs[3], 0)]
    for (out, i), slot in zip(places, SLOTS):
        start = pl.multiple_of((slot ^ ranks[1]) * part, 8)
        out[i] = acc[pl.ds(start, part), :].astype(LOW)


def branch_kernel(ranks, mid_ref, cot_ref, e0, e1, e2, gain_ref, b0, b1, b2, b3, att_ref, gm_ref, gb_ref, do_ref, delta_ref, gain_out, w_ref):
    width, span = mid_ref.shape
    assemble(ranks[0], (b0, b1, b2, b3), w_ref)
    middle = mid_ref[...]
    grad = e0[0].astype(FULL) + e1[0].astype(FULL) + e2[...].astype(FULL)
    inverse = lax.rsqrt(jnp.mean(middle * middle, axis=0, keepdims=True) + NORM_EPS)
    scaled = grad * gain_ref[:, 1:2].astype(FULL)
    turned = jnp.mean(scaled * middle, axis=0, keepdims=True)
    grad_middle = cot_ref[0].astype(FULL) + inverse * scaled - middle * (inverse * inverse * inverse * turned)
    gain_out[...] = dot(jnp.ones((8, span), LOW), (grad * middle * inverse).astype(LOW), NT)
    gm_ref[...] = grad_middle
    branch = grad_middle.astype(LOW)
    gb_ref[...] = branch
    grad_att = dot(w_ref[...], branch).astype(LOW)
    do_ref[...] = grad_att
    both = grad_att.astype(FULL) * att_ref[...].astype(FULL)
    heads = width // HD
    for h in range(heads):
        delta_ref[h : h + 1, :] = jnp.sum(both[h * HD : (h + 1) * HD, :], axis=0, keepdims=True)
    delta_ref[heads:, :] = jnp.zeros((delta_ref.shape[0] - heads, span), FULL)


def attend_back_kernel(seq, q_ref, b0, b1, b2, b3, p_ref, do_ref, delta_ref, cos_ref, sin_ref, gq_ref, own_ref, far_ref, send_ref):
    span = q_ref.shape[1]
    per = q_ref.shape[0] // HD
    h = pl.program_id(0)
    kv_t = jnp.concatenate([b0[...], b1[...], b2[...], b3[...]], axis=1)
    kv = kv_t.T
    query, out_grad = beside(q_ref), beside(do_ref)
    delta = jnp.concatenate([delta_ref[pl.ds(per * h + i, 1), :] for i in range(per)], axis=1)
    none = jnp.zeros(out_grad.shape, LOW)
    grad_probs = dot(kv, jnp.concatenate([none, out_grad], axis=0))
    grad_scores = (p_ref[0].astype(FULL) * (grad_probs - delta)).astype(LOW)
    grad_q = dot(kv_t[0:HD, :], grad_scores) * SCALE
    for i in range(per):
        one, two = turn(grad_q[:, i * span : (i + 1) * span], cos_ref[seq], sin_ref[seq], -1.0)
        gq_ref[i * HD : i * HD + HD // 2, :] = one.astype(LOW)
        gq_ref[i * HD + HD // 2 : (i + 1) * HD, :] = two.astype(LOW)
    keys = dot(query, grad_scores, NT).astype(LOW)
    values = dot(out_grad, p_ref[0], NT).astype(LOW)
    for k in range(GROUP):
        out = (own_ref, send_ref.at[0], far_ref, send_ref.at[1])[k]
        part = slice(k * span, (k + 1) * span)
        out[0:HD, :] = keys[:, part]
        out[HD:, :] = values[:, part]


def spread(ranks, acc, own_ref, far_ref, send_ref):
    part = acc.shape[1] // PARTS
    for k, out in enumerate((own_ref, send_ref.at[0], far_ref, send_ref.at[1])):
        for i, slot in enumerate(SLOTS):
            start = pl.multiple_of((slot ^ ranks[1]) * part, 8)
            out[i] = acc[ranks[0] ^ k, pl.ds(start, part), :].astype(LOW)


def query_weight_kernel(ranks, norm_ref, gq_a, gq_b, att_a, att_b, gb_a, gb_b, own_ref, far_ref, send_ref, acc):
    width, span = gq_a.shape
    shard = width // GROUP
    for b in range(GROUP):
        rows = slice(b * shard, (b + 1) * shard)
        acc[b, 0:shard, 0:width] = dot(norm_ref[rows, 0:span], gq_a[...], NT) + dot(norm_ref[rows, span:], gq_b[...], NT)
        acc[b, 0:shard, width:] = dot(att_a[rows, :], gb_a[...], NT) + dot(att_b[rows, :], gb_b[...], NT)
        acc[b, shard:, :] = jnp.zeros((acc.shape[1] - shard, acc.shape[2]), FULL)
    spread(ranks, acc, own_ref, far_ref, send_ref)


def key_weight_kernel(ranks, norm_ref, a0, a1, a2, b0, b1, b2, cos_ref, sin_ref, own_ref, far_ref, send_ref, gkv_ref, acc):
    width = norm_ref.shape[0]
    span = a2.shape[1]
    shard = width // GROUP
    kw2 = gkv_ref.shape[0]
    kw = kw2 // 2
    for s, (e0, e1, e2) in enumerate(((a0, a1, a2), (b0, b1, b2))):
        part = slice(s * span, (s + 1) * span)
        grad = e0[...].astype(FULL) + e1[0].astype(FULL) + e2[...].astype(FULL)
        for h in range(kw // HD):
            top = h * 2 * HD
            one, two = turn(grad[top : top + HD, :], cos_ref[s], sin_ref[s], -1.0)
            gkv_ref[h * HD : h * HD + HD // 2, part] = one.astype(LOW)
            gkv_ref[h * HD + HD // 2 : (h + 1) * HD, part] = two.astype(LOW)
            gkv_ref[kw + h * HD : kw + (h + 1) * HD, part] = grad[top + HD : top + 2 * HD, :].astype(LOW)
    for b in range(GROUP):
        rows = slice(b * shard, (b + 1) * shard)
        acc[b, 0:shard, :] = dot(norm_ref[rows, :], gkv_ref[...], NT)
        acc[b, shard:, :] = jnp.zeros((acc.shape[1] - shard, kw2), FULL)
    spread(ranks, acc, own_ref, far_ref, send_ref)


def query_grad_kernel(ranks, gq_a, gq_b, q0, q1, q2, q3, out_ref, wq_ref):
    assemble(ranks[0], (q0, q1, q2, q3), wq_ref)
    out_ref[0] = dot(wq_ref[...], gq_a[...])
    out_ref[1] = dot(wq_ref[...], gq_b[...])


def input_grad_kernel(ranks, part_ref, gkv_ref, k0, k1, k2, k3, tok_ref, gm_a, gm_b, gain_a, gain_b, out_ref, gain_out, wkv_ref):
    span = gm_a.shape[1]
    kw2 = gkv_ref.shape[0]
    assemble(ranks[0], (k0, k1, k2, k3), wkv_ref)
    gain_one = wkv_ref[:, kw2 : kw2 + 1].astype(FULL)
    total = None
    for s in range(2):
        part = slice(s * span, (s + 1) * span)
        grad_norm = part_ref[s] + dot(wkv_ref[:, 0:kw2], gkv_ref[:, part])
        x = tok_ref[s].astype(FULL)
        inverse = lax.rsqrt(jnp.mean(x * x, axis=0, keepdims=True) + NORM_EPS)
        scaled = grad_norm * gain_one
        turned = jnp.mean(scaled * x, axis=0, keepdims=True)
        out_ref[s] = (gm_a, gm_b)[s][...] + inverse * scaled - x * (inverse * inverse * inverse * turned)
        row = dot(jnp.ones((8, span), LOW), (grad_norm * x * inverse).astype(LOW), NT)
        total = row if total is None else total + row
    gain_out[0:1, :] = total[0:1, :]
    gain_out[1:2, :] = gain_a[0:1, :] + gain_b[0:1, :]
    gain_out[2:8, :] = total[2:8, :]


def place(slot):
    return ((slot >> 2) & 1) + ((slot >> 1) & 1) * 2


def gathered(ranks, pairs):
    for a in range(PARTS):
        slot = ranks[1] ^ a
        index = place(slot)
        for parity in range(2):

            @pl.when(slot % 2 == parity)
            def _(parity=parity, index=index, a=a):
                for pair in pairs:
                    part = pair[parity].shape[1]
                    pair[2][a * part : (a + 1) * part, :] = pair[parity][index].astype(FULL)


def forward_weights_kernel(ranks, even, odd, out_ref):
    gathered(ranks, [(even, odd, out_ref)])


def query_done_kernel(ranks, even, odd, q_ref, o_ref, scratch):
    shard, width = q_ref.shape
    gathered(ranks, [(even, odd, scratch)])
    q_ref[...] = scratch[0:shard, 0:width]
    o_ref[...] = scratch[0:shard, width:]


def key_done_kernel(ranks, even, odd, k_ref, v_ref, scratch):
    kw, shard = k_ref.shape
    gathered(ranks, [(even, odd, scratch)])
    k_ref[...] = scratch[0:shard, 0:kw].T
    v_ref[...] = scratch[0:shard, kw:].T


def tables(places):
    half = HD // 2
    frequency = ROPE_BASE ** (-2.0 * jnp.arange(half, dtype=FULL) / HD)
    angles = places.astype(FULL)[:, None, :] * frequency[None, :, None]
    return jnp.cos(angles), jnp.sin(angles)


def body(
    tokens,
    w_query,
    w_key,
    w_value,
    w_out,
    w_gate,
    w_up,
    w_down,
    gain_attn,
    gain_mlp,
    span_order,
    piece_starts,
    cotangent,
):
    ranks = lax.axis_size("rep")
    rank_grp = lax.axis_index("grp")
    seq_count, span, width = tokens.shape
    shard = w_query.shape[0]
    kw = w_key.shape[1]
    kw2 = 2 * kw
    kv_heads = kw // HD
    per = width // kw
    ff = w_gate.shape[1]
    rows = seq_count * span
    length = GROUP * span
    place_of = jnp.stack([rank_grp, lax.axis_index("rep") % PARTS]).astype(jnp.int32)
    tok_t = jnp.swapaxes(tokens, 1, 2)
    cot_t = jnp.swapaxes(cotangent, 1, 2)
    wd_t = w_down.T
    act = whole((width, span))
    seqs = whole((seq_count, width, span))
    one_seq = lambda s: pl.BlockSpec((1, width, span), lambda *_: (s, 0, 0))
    table = whole((seq_count, HD // 2, span))
    gain_spec = whole((width, LANES))
    head = pl.BlockSpec((2 * HD, span), lambda h, *_: (h, 0))
    probs_spec = pl.BlockSpec((1, length, per * span), lambda h, *_: (h, 0, 0))
    q_spec = lambda s: pl.BlockSpec((per * HD, span), lambda h, *_: (h, s))
    per_head = pl.BlockSpec((per * HD, span), lambda h, *_: (h, 0))

    kv_shard = call(
        pack_kernel,
        "pack",
        shape_of((shard, kw2 + LANES)),
        in_specs=[whole((kw, shard))] * 2 + [whole((2, shard))],
        out_specs=whole((shard, kw2 + LANES)),
        micros=2,
    )(w_key.T, w_value.T, jnp.stack([gain_attn, gain_mlp]).astype(FULL))
    kv_flight = Blocks(kv_shard)
    q_flight = Blocks(w_query, kv_shard)
    own_span = lax.dynamic_slice(span_order, (0, rank_grp), (seq_count, 1))
    places = own_span * span + jnp.arange(span, dtype=jnp.int32)[None, :]
    cos_cols, sin_cols = tables(places)
    kv_blocks = kv_flight.finish()
    norm_low, kv_a, kv_b, gain_cols = call(
        keys_values_kernel,
        "keys_values",
        (shape_of((width, rows)), shape_of((kw2, span)), shape_of((kw2, span)), shape_of((width, LANES))),
        prefetch=1,
        in_specs=[seqs] + [whole(kv_shard.shape)] * 4 + [table, table],
        out_specs=(whole((width, rows)), whole((kw2, span)), whole((kw2, span)), gain_spec),
        scratch=[pltpu.VMEM((width, kw2 + LANES), LOW)],
        micros=4.3,
    )(place_of, tok_t, *kv_blocks, cos_cols, sin_cols)
    kv_flight = [Blocks(kv_a), None]
    wgut, wgu = call(
        flip_two_kernel,
        "flip_two",
        (shape_of((2 * ff, width)), shape_of((width, 2 * ff))),
        in_specs=[whole((width, ff))] * 2,
        out_specs=(whole((2 * ff, width)), whole((width, 2 * ff))),
        micros=4,
    )(after(w_gate, norm_low), w_up)
    q_flight.arrive(wgut)
    wd = call(
        flip_one_kernel,
        "flip_one",
        shape_of((ff, width)),
        in_specs=[whole((width, ff))],
        out_specs=whole((ff, width)),
        micros=2,
    )(after(wd_t, *q_flight.ready))
    q_blocks = q_flight.finish(wd)
    queries = call(
        queries_kernel,
        "queries",
        shape_of((width, rows)),
        prefetch=1,
        in_specs=[whole((width, rows))] + [whole((shard, width))] * 4 + [table, table],
        out_specs=whole((width, rows)),
        scratch=[pltpu.VMEM((width, width), LOW)],
        micros=4.9,
    )(place_of, norm_low, *q_blocks, cos_cols, sin_cols)

    o_flight = Blocks(w_out, wgut)
    kv_flight[1] = Blocks(kv_b, o_flight.sent, wgut)
    cot_flight = [Blocks(cot_t[0], queries), None]
    cot_blocks = [None, None]
    kv_all = [kv_flight[0].finish(queries), None]

    def attend_of(s, query):
        return call(
            functools.partial(attend_kernel, s),
            "attend",
            (shape_of((kv_heads, length, per * span)), shape_of((width, span))),
            prefetch=3,
            grid=(kv_heads,),
            in_specs=[q_spec(s)] + [head] * 4,
            out_specs=(probs_spec, per_head),
            scratch=[pltpu.VMEM((length, span), FULL)],
            micros=10,
        )(place_of, span_order, piece_starts, query, *kv_all[s])

    def middle_of(s, att):
        return call(
            middle_kernel,
            "middle",
            (shape_of((width, span), FULL), shape_of((width, span))),
            prefetch=1,
            in_specs=[act] + [whole((shard, width))] * 4 + [one_seq(s), gain_spec],
            out_specs=(act, act),
            scratch=[pltpu.VMEM((width, width), LOW)],
            micros=3,
        )(place_of, att, *o_blocks, tok_t, gain_cols)

    probs_a, att_a = attend_of(0, queries)
    o_blocks = o_flight.finish(att_a)
    kv_all[1] = kv_flight[1].finish(att_a)
    middle_a, x_a = middle_of(0, att_a)
    x_flight = [Blocks(x_a), None]
    cot_flight[1] = Blocks(cot_t[1], x_flight[0].sent, x_a)
    probs_b, att_b = attend_of(1, after(queries, x_a))
    cot_flight[0].arrive(att_b)
    middle_b, x_b = middle_of(1, after(att_b, *cot_flight[0].ready))
    x_flight[1] = Blocks(x_b)
    x_flight[0].arrive(middle_b)
    cot_blocks[0] = cot_flight[0].finish(middle_b)
    stats, attended, middles = (probs_a, probs_b), (att_a, att_b), (middle_a, middle_b)

    each = pl.BlockSpec((1, width, span), lambda s, *_: (s, 0, 0))
    each_ff = pl.BlockSpec((1, ff, span), lambda s, *_: (s, 0, 0))
    two = shape_of((seq_count, width, span))
    two_ff = shape_of((seq_count, ff, span))
    own_out, own_grad, own_hid, own_gg, own_gu = call(
        own_block_kernel,
        "own_blocks",
        (two, two, two_ff, two_ff, two_ff),
        grid=(seq_count,),
        in_specs=[act, act, each] + [NEAR] * 4,
        out_specs=(each, each, each_ff, each_ff, each_ff),
        scratch=[pltpu.VMEM((width, span), LOW), pltpu.VMEM((2 * ff, span), LOW)],
        micros=8,
    )(after(x_a, *x_flight[0].ready, *cot_blocks[0]), x_b, cot_t, wgut, wgu, wd_t, wd)
    x_blocks = [x_flight[0].finish(own_out), None]
    cot_flight[1].arrive(own_out)

    def other_blocks(s, *others):
        half = pl.BlockSpec((1, width, span), lambda k, *_: (k // 2, 0, 0))
        per_block = pl.BlockSpec((ff, span), lambda k, *_: (0, k))
        act_shape, half_shape, ff_shape = shape_of((width, span)), shape_of((2, width, span)), shape_of((ff, 3 * span))
        return call(
            other_blocks_kernel,
            "other_blocks",
            (act_shape, half_shape, act_shape, half_shape, ff_shape, ff_shape, ff_shape),
            grid=(GROUP - 1,),
            in_specs=[ANY] * 6 + [NEAR] * 4,
            out_specs=(act, half, act, half) + (per_block,) * 3,
            scratch=[
                pltpu.VMEM((6, width, span), LOW),
                pltpu.VMEM((2 * ff, span), LOW),
                pltpu.SemaphoreType.DMA((6,)),
            ],
            micros=12,
        )(after(x_blocks[s][1], *others), *x_blocks[s][2:], *cot_blocks[s][1:], wgut, wgu, wd_t, wd)

    fo_a, so_a, fg_a, sg_a, hid_a, gg_a, gu_a = other_blocks(0, *cot_flight[1].ready)
    grad_a = Terms(own_grad[0], fg_a, sg_a)
    out_a = Terms(own_out[0], fo_a, so_a)
    x_flight[1].arrive(fg_a)
    x_blocks[1] = x_flight[1].finish()
    cot_blocks[1] = cot_flight[1].finish(fg_a)
    fo_b, so_b, fg_b, sg_b, hid_b, gg_b, gu_b = other_blocks(1, fg_a)
    grad_b = Terms(own_grad[1], fg_b, sg_b)
    out_b = Terms(own_out[1], fo_b, so_b)
    stage = (grad_a.cross(fg_b), out_a.cross(fg_b))
    grads = (grad_a, grad_b)

    part = width // PARTS

    def sums(name, blocks, rights, *others):
        pieces = call(
            weight_kernel,
            name,
            tuple(shape_of((n, part, ff)) for n in (4, 2, 1, 1)),
            prefetch=1,
            in_specs=[ANY] * (2 * GROUP + 3),
            out_specs=tuple(whole((n, part, ff)) for n in (4, 2, 1, 1)),
            scratch=[
                pltpu.VMEM((2, width, length), LOW),
                pltpu.VMEM((2, ff, length), LOW),
                pltpu.VMEM((width, ff), FULL),
                pltpu.SemaphoreType.DMA((2 * GROUP + 4,)),
            ],
            micros=8,
        )(place_of, after(blocks[0], *others), *blocks[1:], *rights)
        return RepSum(pieces, ranks)

    x_all = x_blocks[0] + x_blocks[1]
    down_sum = sums("down_weights", cot_blocks[0] + cot_blocks[1], (own_hid, hid_a, hid_b), *stage)
    done = down_sum.pieces[0]
    stage = (grad_b.cross(done), out_b.beside, done)
    gate_sum = sums("gate_weights", x_all, (own_gg, gg_a, gg_b), *stage)
    done = gate_sum.pieces[0]
    stage = (grad_a.across, out_b.cross(done), done)
    up_sum = sums("up_weights", x_all, (own_gu, gu_a, gu_b), *stage)
    done = up_sum.pieces[0]
    stage = (down_sum.second(done), out_a.across, done)

    def branch_of(s, middle):
        _, beside_term, across_term = grads[s].all()
        first = whole((1, width, span))
        return call(
            branch_kernel,
            "branch",
            (
                shape_of((width, span), FULL),
                shape_of((width, span)),
                shape_of((width, span)),
                shape_of((16, span), FULL),
                shape_of((8, width), FULL),
            ),
            prefetch=1,
            in_specs=[act, one_seq(s), one_seq(s), first, act, gain_spec] + [whole((shard, width))] * 4 + [act],
            out_specs=(act, act, act, whole((16, span)), whole((8, width))),
            scratch=[pltpu.VMEM((width, width), LOW)],
            micros=4,
        )(place_of, middle, cot_t, own_grad, beside_term, across_term, gain_cols, *o_blocks, attended[s])

    def attend_back_of(s, out_grad, delta):
        halves = pl.BlockSpec((2, 2 * HD, span), lambda h, *_: (0, h, 0))
        grad_q, *kv_parts = call(
            functools.partial(attend_back_kernel, s),
            "attend_back",
            (shape_of((width, span)), shape_of((kw2, span)), shape_of((kw2, span)), shape_of((2, kw2, span))),
            grid=(kv_heads,),
            in_specs=[q_spec(s)] + [head] * 4 + [probs_spec, per_head, whole((16, span)), table, table],
            out_specs=(per_head, head, head, halves),
            micros=11,
        )(queries, *kv_all[s], stats[s], out_grad, delta, cos_cols, sin_cols)
        return grad_q, Terms(*kv_parts)

    mid_a, branch_a, dout_a, delta_a, gain_a = branch_of(0, after(middles[0], *stage))
    gq_a, kv_grad_a = attend_back_of(0, after(dout_a, grad_b.across), delta_a)
    stage = (out_b.across, gate_sum.second(gq_a), down_sum.third(gq_a))
    mid_b, branch_b, dout_b, delta_b, gain_b = branch_of(1, after(middles[1], *stage))
    stage = (kv_grad_a.cross(branch_b), up_sum.second(branch_b))
    gq_b, kv_grad_b = attend_back_of(1, after(dout_b, *stage), delta_b)
    stage = (gate_sum.third(gq_b), down_sum.own(gq_b), up_sum.third(gq_b), kv_grad_a.across)

    grown = shard + GAIN_ROWS
    piece = grown // PARTS
    spread_out = lambda columns: (shape_of((PARTS, piece, columns)),) * 2 + (shape_of((2, PARTS, piece, columns)),)
    spread_spec = lambda columns: (whole((PARTS, piece, columns)),) * 2 + (whole((2, PARTS, piece, columns)),)
    query_parts = call(
        query_weight_kernel,
        "query_weights",
        spread_out(2 * width),
        prefetch=1,
        in_specs=[whole((width, rows))] + [act] * 6,
        out_specs=spread_spec(2 * width),
        scratch=[pltpu.VMEM((GROUP, grown, 2 * width), FULL)],
        micros=8,
    )(place_of, norm_low, after(gq_a, *stage), gq_b, *attended, branch_a, branch_b)
    done = query_parts[0]
    query_terms = Terms(*query_parts)
    stage = (kv_grad_b.cross(done), down_sum.spread(done))
    grad_part = call(
        query_grad_kernel,
        "query_grad",
        shape_of((seq_count, width, span), FULL),
        prefetch=1,
        in_specs=[act, act] + [whole((shard, width))] * 4,
        out_specs=seqs,
        scratch=[pltpu.VMEM((width, width), LOW)],
        micros=4,
    )(place_of, after(gq_a, *stage), gq_b, *q_blocks)
    stage = (query_terms.cross(grad_part), gate_sum.own(grad_part), up_sum.own(grad_part))
    block_out = jnp.stack(
        [middle + three(term.all()) for middle, term in zip(after(middles, *stage), (out_a, out_b))]
    )

    def owned(terms):
        own, beside_term, across = terms.all()
        cuts = (slice(0, 4), slice(4, 6), slice(6, 7), slice(7, 8))
        return [three((own[c], beside_term[:, c], across[c])).astype(LOW) for c in cuts]

    first = whole((1, kw2, span))
    terms = []
    for term in (kv_grad_a, kv_grad_b):
        terms += term.all()
    *key_parts, gkv = call(
        key_weight_kernel,
        "key_weights",
        spread_out(kw2) + (shape_of((kw2, rows)),),
        prefetch=1,
        in_specs=[whole((width, rows))] + [whole((kw2, span)), first, whole((kw2, span))] * 2 + [table, table],
        out_specs=spread_spec(kw2) + (whole((kw2, rows)),),
        scratch=[pltpu.VMEM((GROUP, grown, kw2), FULL)],
        micros=4,
    )(place_of, after(norm_low, block_out), *terms, cos_cols, sin_cols)
    key_terms = Terms(*key_parts)
    down_pair = down_sum.done(gkv)
    grad_tokens, gain_part = call(
        input_grad_kernel,
        "input_grad",
        (shape_of((seq_count, width, span), FULL), shape_of((8, width), FULL)),
        prefetch=1,
        in_specs=[seqs, whole((kw2, rows))]
        + [whole(kv_shard.shape)] * 4
        + [seqs, act, act]
        + [whole((8, width))] * 2,
        out_specs=(seqs, whole((8, width))),
        scratch=[pltpu.VMEM((width, kw2 + LANES), LOW)],
        micros=6,
    )(
        place_of,
        after(grad_part, down_pair[0]),
        gkv,
        *kv_blocks,
        tok_t,
        mid_a,
        mid_b,
        gain_a,
        gain_b,
    )
    small = SmallSum(gain_part, ranks)
    stage = (key_terms.cross(grad_tokens), gate_sum.spread(grad_tokens), up_sum.spread(grad_tokens))
    small.step()
    query_sum = RepSum(owned(query_terms), ranks)
    done = query_sum.pieces[0]
    gate_pair = gate_sum.done(done)
    small.step(done)

    def finished(name, pair, *others):
        return call(
            forward_weights_kernel,
            name,
            shape_of((width, ff), FULL),
            prefetch=1,
            in_specs=[whole((4, part, ff))] * 2,
            out_specs=whole((width, ff)),
            micros=3.5,
        )(place_of, after(pair[0], *others), pair[1])

    grad_down = finished("down_done", down_pair, gate_pair[0])
    key_sum = RepSum(owned(key_terms), ranks)
    stage = (query_sum.second(grad_down), up_sum.done(grad_down), small.step(grad_down))
    up_pair = stage[1]
    grad_gate = finished("gate_done", gate_pair, stage[0], up_pair[0])
    stage = (key_sum.second(grad_gate), query_sum.third(grad_gate))
    small.step(*stage)
    stage = (key_sum.third(*stage), query_sum.own(*stage))
    small.step(*stage)
    grad_up = finished("up_done", up_pair, *stage)
    stage = (key_sum.own(grad_up), query_sum.spread(grad_up))
    query_pair = query_sum.done(*stage)
    key_sum.spread(query_pair[0])
    key_pair = key_sum.done()
    grad_gains = small.finish()
    grad_down = grad_down.T
    grad_query, grad_out = call(
        query_done_kernel,
        "query_done",
        (shape_of((shard, width), FULL),) * 2,
        prefetch=1,
        in_specs=[whole((4, piece, 2 * width))] * 2,
        out_specs=(whole((shard, width)),) * 2,
        scratch=[pltpu.VMEM((grown, 2 * width), FULL)],
        micros=3,
    )(place_of, *query_pair)
    grad_key, grad_value = call(
        key_done_kernel,
        "key_done",
        (shape_of((kw, shard), FULL),) * 2,
        prefetch=1,
        in_specs=[whole((4, piece, kw2))] * 2,
        out_specs=(whole((kw, shard)),) * 2,
        scratch=[pltpu.VMEM((grown, kw2), FULL)],
        micros=2,
    )(place_of, *key_pair)
    own_gains = lax.dynamic_slice(grad_gains, (0, rank_grp * shard), (2, shard))
    return (
        jnp.swapaxes(block_out, 1, 2),
        jnp.swapaxes(grad_tokens, 1, 2),
        grad_query,
        grad_key.T,
        grad_value.T,
        grad_out,
        grad_gate,
        grad_up,
        grad_down,
        own_gains[0],
        own_gains[1],
    )


def solution(mesh):
    placed = (
        P("rep", "grp", None),
        P("grp", None),
        P("grp", None),
        P("grp", None),
        P("grp", None),
        P(None, "grp"),
        P(None, "grp"),
        P("grp", None),
        P("grp"),
        P("grp"),
        P("rep", None),
        P("rep", None),
        P("rep", "grp", None),
    )
    return jax.shard_map(
        body,
        mesh=mesh,
        in_specs=placed,
        out_specs=(
            P("rep", "grp", None),
            P("rep", "grp", None),
            P("grp", None),
            P("grp", None),
            P("grp", None),
            P("grp", None),
            P(None, "grp"),
            P(None, "grp"),
            P("grp", None),
            P("grp"),
            P("grp"),
        ),
        check_vma=False,
    )
```

```python
import functools

import jax
import jax.numpy as jnp
from jax import lax
from jax.experimental import pallas as pl
from jax.experimental.pallas import tpu as pltpu
from jax.sharding import PartitionSpec as P

HD = 64
PIECE = 256
LANES = 128
GROUP = 4
PARTS = 8
GAIN_ROWS = 16
RATE = 2.0e9
SLOTS = (7, 3, 5, 1, 6, 2, 4, 0)


NORM_EPS = 1e-05
ROPE_BASE = 10000.0
MASKED_SCORE = -1e30
SCALE = HD ** (-0.5)

LOW = jnp.bfloat16
FULL = jnp.float32
NN = (((1,), (0,)), ((), ()))
NT = (((1,), (1,)), ((), ()))
TN = (((0,), (0,)), ((), ()))


def dot(left_mat, right_mat, form=NN):
    return lax.dot_general(left_mat, right_mat, form, preferred_element_type=FULL)


def swap(values, axis, count, mask):
    return lax.ppermute(values, axis, [(i, i ^ mask) for i in range(count)])


def after(values, *others):
    return lax.optimization_barrier((values,) + others)[0] if others else values


class Blocks:
    def __init__(self, own, *others):
        self.own = own
        sent = after(own, *others)
        self.across = swap(sent, "grp", GROUP, 2)
        self.sent = sent

    def arrive(self, *others):
        pair = after((self.sent, self.across), *others)
        self.ready = pair
        self.core = swap(pair[0], "grp", GROUP, 1), swap(pair[1], "grp", GROUP, 1)

    def finish(self, *others):
        if not hasattr(self, "core"):
            self.arrive(*others)
        beside, corner = after(self.core, *others)
        return self.own, beside, self.across, corner


class Terms:
    def __init__(self, own, far, send, *others):
        self.own, self.far = own, far
        self.beside = swap(after(send, *others), "grp", GROUP, 1)

    def cross(self, *others):
        far, beside = after((self.far, self.beside), *others)
        across = (far.astype(FULL) + beside[1].astype(FULL)).astype(LOW)
        self.sent = across
        self.across = swap(across, "grp", GROUP, 2)
        return across

    def all(self):
        return self.own, self.beside, self.across


def three(terms):
    return terms[0].astype(FULL) + terms[1][0].astype(FULL) + terms[2].astype(FULL)


class RepSum:
    def __init__(self, pieces, ranks):
        self.pieces, self.ranks = pieces, ranks
        self.one = swap(pieces[0], "rep", ranks, 1)

    def second(self, *others):
        self.one = after(self.one, *others)
        two = (self.pieces[1].astype(FULL) + self.one[0:2].astype(FULL)).astype(LOW)
        self.held_two = two
        self.two = swap(two, "rep", self.ranks, 2)
        return two

    def third(self, *others):
        self.two = after(self.two, *others)
        four = self.pieces[2].astype(FULL) + self.one[2:3].astype(FULL) + self.two[0:1].astype(FULL)
        four = four.astype(LOW)
        self.four = swap(four, "rep", self.ranks, 4)
        return four

    def own(self, *others):
        ranks = self.ranks
        self.four = after(self.four, *others)
        mine = self.pieces[3].astype(FULL) + self.one[3:4].astype(FULL) + self.two[1:2].astype(FULL)
        mine = (mine + self.four.astype(FULL)).astype(LOW)
        if ranks > PARTS:
            others = [[j * PARTS + i for j in range(ranks // PARTS)] for i in range(PARTS)]
            mine = lax.psum(mine, "rep", axis_index_groups=others)
        self.mine = mine
        self.back = swap(mine, "rep", ranks, 4)
        return mine

    def spread(self, *others):
        self.back = after(self.back, *others)
        held = jnp.concatenate([self.mine, self.back])
        self.held = held
        self.wide = swap(held, "rep", self.ranks, 2)
        return held

    def done(self, *others):
        self.wide = after(self.wide, *others)
        held = jnp.concatenate([self.held, self.wide])
        return held, swap(held, "rep", self.ranks, 1)


def call(kernel, name, out_shape, *, grid=(1,), prefetch=0, in_specs, out_specs, scratch=(), micros=1, vmem=36):
    def lies(shape):
        return pltpu.HBM(shape.shape, shape.dtype)

    several = isinstance(out_shape, tuple)
    run = pl.pallas_call(
        kernel,
        name=name,
        out_shape=tuple(map(lies, out_shape)) if several else lies(out_shape),
        grid_spec=pltpu.PrefetchScalarGridSpec(
            num_scalar_prefetch=prefetch,
            grid=grid,
            in_specs=in_specs,
            out_specs=out_specs,
            scratch_shapes=list(scratch),
        ),
        compiler_params=pltpu.CompilerParams(vmem_limit_bytes=vmem << 20),
        cost_estimate=pl.CostEstimate(flops=int(micros * RATE), bytes_accessed=1 << 10, transcendentals=0),
    )

    def placed(*args):
        rest = [
            arg if spec is NEAR else pltpu.with_memory_space_constraint(arg, pltpu.HBM)
            for arg, spec in zip(args[prefetch:], in_specs, strict=True)
        ]
        return run(*args[:prefetch], *rest)

    return placed


def whole(shape):
    return pl.BlockSpec(shape, lambda *_: (0,) * len(shape))


ANY = pl.BlockSpec(memory_space=pl.ANY)
NEAR = pl.BlockSpec(memory_space=pltpu.VMEM)


def shape_of(shape, kind=LOW):
    return jax.ShapeDtypeStruct(shape, kind)


def turn(rows, cosine, sine_val, sign):
    one, two = rows[0 : HD // 2, :], rows[HD // 2 : HD, :]
    sine_val = sine_val * sign
    return one * cosine - two * sine_val, two * cosine + one * sine_val


def assemble(rank, blocks, scratch):
    rows = blocks[0].shape[0]
    for k in range(GROUP):
        start = pl.multiple_of((rank ^ k) * rows, 16)
        scratch[pl.ds(start, rows), :] = blocks[k][...]


def pack_kernel(wk_ref, wv_ref, gains_ref, out_ref):
    kw, shard = wk_ref.shape
    out_ref[:, 0:kw] = wk_ref[...].T
    out_ref[:, kw : 2 * kw] = wv_ref[...].T
    gains = jnp.concatenate([gains_ref[...], jnp.zeros((LANES - 2, shard), FULL)], axis=0)
    out_ref[:, 2 * kw :] = gains.T.astype(LOW)


def flip_two_kernel(wg_ref, wu_ref, wgut_ref, wgu_ref):
    ff = wg_ref.shape[1]
    wgut_ref[0:ff, :] = wg_ref[...].T
    wgut_ref[ff:, :] = wu_ref[...].T
    wgu_ref[:, 0:ff] = wg_ref[...]
    wgu_ref[:, ff:] = wu_ref[...]


def flip_one_kernel(wdt_ref, wd_ref):
    wd_ref[...] = wdt_ref[...].T


def keys_values_kernel(ranks, tok_ref, b0, b1, b2, b3, cos_ref, sin_ref, norm_ref, kv_a, kv_b, gain_ref, w_ref):
    span = tok_ref.shape[2]
    kw2 = kv_a.shape[0]
    kw = kw2 // 2
    assemble(ranks[0], (b0, b1, b2, b3), w_ref)
    gains = w_ref[:, kw2:]
    gain_ref[...] = gains
    gain_one = gains[:, 0:1].astype(FULL)
    for s, out in enumerate((kv_a, kv_b)):
        x = tok_ref[s].astype(FULL)
        inverse = lax.rsqrt(jnp.mean(x * x, axis=0, keepdims=True) + NORM_EPS)
        norm = (x * inverse * gain_one).astype(LOW)
        norm_ref[:, s * span : (s + 1) * span] = norm
        kv = dot(w_ref[:, 0:kw2], norm, TN)
        for h in range(kw // HD):
            one, two = turn(kv[h * HD : (h + 1) * HD, :], cos_ref[s], sin_ref[s], 1.0)
            top = h * 2 * HD
            out[top : top + HD // 2, :] = one.astype(LOW)
            out[top + HD // 2 : top + HD, :] = two.astype(LOW)
            out[top + HD : top + 2 * HD, :] = kv[kw + h * HD : kw + (h + 1) * HD, :].astype(LOW)


def queries_kernel(ranks, norm_ref, b0, b1, b2, b3, cos_ref, sin_ref, q_ref, w_ref):
    width = b0.shape[1]
    span = cos_ref.shape[2]
    assemble(ranks[0], (b0, b1, b2, b3), w_ref)
    for s in range(2):
        part = slice(s * span, (s + 1) * span)
        query = dot(w_ref[...], norm_ref[:, part], TN)
        for h in range(width // HD):
            one, two = turn(query[h * HD : (h + 1) * HD, :], cos_ref[s], sin_ref[s], 1.0)
            q_ref[h * HD : h * HD + HD // 2, part] = (one * SCALE).astype(LOW)
            q_ref[h * HD + HD // 2 : (h + 1) * HD, part] = (two * SCALE).astype(LOW)


def beside(ref):
    return jnp.concatenate([ref[i : i + HD, :] for i in range(0, ref.shape[0], HD)], axis=1)


def attend_kernel(seq, ranks, order, starts, q_ref, b0, b1, b2, b3, p_ref, o_ref, bias_ref):
    span = q_ref.shape[1]
    per = q_ref.shape[0] // HD
    rank = ranks[0]

    @pl.when(pl.program_id(0) == 0)
    def _():
        query_pos = order[seq, rank] * span + lax.broadcasted_iota(jnp.int32, (span, span), 1)
        query_in = []
        for m in range(2):
            start = starts[seq, m]
            query_in.append((query_pos >= start) & (query_pos < start + PIECE))
        for k in range(GROUP):
            key_pos = order[seq, rank ^ k] * span + lax.broadcasted_iota(jnp.int32, (span, span), 0)
            allowed = key_pos <= query_pos
            for m in range(2):
                start = starts[seq, m]
                key_in = (key_pos >= start) & (key_pos < start + PIECE)
                allowed = allowed | (query_in[m] & key_in)
            bias_ref[k * span : (k + 1) * span, :] = jnp.where(allowed, 0.0, MASKED_SCORE)

    kv_t = jnp.concatenate([b0[...], b1[...], b2[...], b3[...]], axis=1)
    keys = kv_t.T[:, 0:HD]
    values_t = kv_t[HD : 2 * HD, :]
    bias = jnp.concatenate([bias_ref[...]] * per, axis=1)
    scores = dot(keys, beside(q_ref)) + bias
    peak = jnp.max(scores, axis=0, keepdims=True)
    exponent = jnp.exp(scores - peak)
    total = jnp.sum(exponent, axis=0, keepdims=True)
    probs = (exponent * (1.0 / total)).astype(LOW)
    p_ref[0] = probs
    mixed = dot(values_t, probs).astype(LOW)
    for i in range(per):
        o_ref[i * HD : (i + 1) * HD, :] = mixed[:, i * span : (i + 1) * span]


def middle_kernel(ranks, att_ref, b0, b1, b2, b3, tok_ref, gain_ref, mid_ref, x_ref, w_ref):
    assemble(ranks[0], (b0, b1, b2, b3), w_ref)
    middle = tok_ref[0].astype(FULL) + dot(w_ref[...], att_ref[...], TN)
    mid_ref[...] = middle
    inverse = lax.rsqrt(jnp.mean(middle * middle, axis=0, keepdims=True) + NORM_EPS)
    x_ref[...] = (middle * inverse * gain_ref[:, 1:2].astype(FULL)).astype(LOW)


def forward_back_step(x, cot, wgut_ref, wgu_ref, wdt_ref, wd_ref, hid_ref, gg_ref, gu_ref, both):
    ff = wd_ref.shape[0]
    gate_up = dot(wgut_ref[...], x)
    grad_hidden = dot(wd_ref[...], cot)
    gate, up = gate_up[0:ff, :], gate_up[ff:, :]
    sig = 1.0 / (1.0 + jnp.exp(-gate))
    swish = gate * sig
    hidden = (swish * up).astype(LOW)
    grad_gate = (grad_hidden * up * sig * (1.0 + gate * (1.0 - sig))).astype(LOW)
    grad_up = (grad_hidden * swish).astype(LOW)
    hid_ref[...] = hidden
    gg_ref[...] = grad_gate
    gu_ref[...] = grad_up
    both[0:ff, :] = grad_gate
    both[ff:, :] = grad_up
    return dot(wgu_ref[...], both[...]).astype(LOW), dot(wdt_ref[...], hidden).astype(LOW)


def own_block_kernel(x_a, x_b, cot_ref, wgut_ref, wgu_ref, wdt_ref, wd_ref, out_ref, grad_ref, hid_ref, gg_ref, gu_ref, held, both):
    s = pl.program_id(0)
    for i, x in enumerate((x_a, x_b)):

        @pl.when(s == i)
        def _(x=x):
            held[...] = x[...]

    grad_x, out = forward_back_step(
        held[...], cot_ref[0], wgut_ref, wgu_ref, wdt_ref, wd_ref, hid_ref.at[0], gg_ref.at[0], gu_ref.at[0], both
    )
    grad_ref[0] = grad_x
    out_ref[0] = out


def other_blocks_kernel(*refs):
    blocks = refs[0:6]
    weights = refs[6:10]
    fo_ref, so_ref, fg_ref, sg_ref, hid_ref, gg_ref, gu_ref, held, both, sem = refs[10:]
    k = pl.program_id(0)
    copies = [pltpu.make_async_copy(block, held.at[i], sem.at[i]) for i, block in enumerate(blocks)]

    @pl.when(k == 0)
    def _():
        for i in range(3):
            copies[i].start()
            copies[3 + i].start()

    for i in range(3):

        @pl.when(k == i)
        def _(i=i):
            copies[i].wait()
            copies[3 + i].wait()

    grad_x, out = forward_back_step(held[k], held[3 + k], *weights, hid_ref, gg_ref, gu_ref, both)

    @pl.when(k == 1)
    def _():
        fg_ref[...] = grad_x
        fo_ref[...] = out

    @pl.when(k != 1)
    def _():
        sg_ref[0] = grad_x
        so_ref[0] = out


def weight_kernel(kinds, ranks, *refs):
    blocks = refs[0 : 2 * GROUP]
    rights = refs[2 * GROUP : 2 * GROUP + 3 * kinds]
    outs = refs[2 * GROUP + 3 * kinds : 2 * GROUP + 3 * kinds + 4]
    left, right, acc, sem = refs[2 * GROUP + 3 * kinds + 4 :]
    span = left.shape[2] // GROUP
    kind = pl.program_id(0)
    lefts, loads = [], []
    for b, block in enumerate(blocks):
        s, k = divmod(b, GROUP)
        lefts.append(pltpu.make_async_copy(block, left.at[s, :, pl.ds(k * span, span)], sem.at[b]))
    for n in range(kinds):
        own, *others = rights[3 * n : 3 * n + 3]
        for s in range(2):
            for i, (source, part) in enumerate(((own.at[s], slice(0, span)), (others[s], slice(span, GROUP * span)))):
                at = sem.at[2 * GROUP + 4 * n + 2 * s + i]
                loads.append(pltpu.make_async_copy(source, right.at[n, s, :, part], at))

    @pl.when(kind == 0)
    def _():
        for copy in loads[0:2] + lefts[:GROUP] + loads[2:4] + lefts[GROUP:] + loads[4:]:
            copy.start()
        for copy in loads[0:2] + lefts[:GROUP]:
            copy.wait()

    for n in range(1, kinds):

        @pl.when(kind == n)
        def _(n=n):
            for copy in loads[4 * n : 4 * n + 4]:
                copy.wait()

    acc[...] = dot(left[0], right[kind, 0], NT)

    @pl.when(kind == 0)
    def _():
        for copy in loads[2:4] + lefts[GROUP:]:
            copy.wait()

    acc[...] += dot(left[1], right[kind, 1], NT)
    part = acc.shape[0] // PARTS
    places = [(outs[0], i) for i in range(4)] + [(outs[1], 0), (outs[1], 1), (outs[2], 0), (outs[3], 0)]
    for (out, i), slot in zip(places, SLOTS):
        start = pl.multiple_of((slot ^ ranks[1]) * part, 8)
        out[i] = acc[pl.ds(start, part), :].astype(LOW)


def branch_kernel(seq, ranks, mid_ref, cot_ref, e0, e1, e2, gain_ref, b0, b1, b2, b3, att_ref, gm_ref, gb_ref, do_ref, delta_ref, gain_out, w_ref):
    width, span = mid_ref.shape
    assemble(ranks[0], (b0, b1, b2, b3), w_ref)
    middle = mid_ref[...]
    grad = e0[0].astype(FULL) + e1[0].astype(FULL) + e2[...].astype(FULL)
    inverse = lax.rsqrt(jnp.mean(middle * middle, axis=0, keepdims=True) + NORM_EPS)
    scaled = grad * gain_ref[:, 1:2].astype(FULL)
    turned = jnp.mean(scaled * middle, axis=0, keepdims=True)
    grad_middle = cot_ref[seq].astype(FULL) + inverse * scaled - middle * (inverse * inverse * inverse * turned)
    gain_out[...] = dot(jnp.ones((8, span), LOW), (grad * middle * inverse).astype(LOW), NT)
    gm_ref[...] = grad_middle
    branch = grad_middle.astype(LOW)
    gb_ref[...] = branch
    grad_att = dot(w_ref[...], branch).astype(LOW)
    do_ref[...] = grad_att
    both = grad_att.astype(FULL) * att_ref[...].astype(FULL)
    heads = width // HD
    for h in range(heads):
        delta_ref[h : h + 1, :] = jnp.sum(both[h * HD : (h + 1) * HD, :], axis=0, keepdims=True)
    delta_ref[heads:, :] = jnp.zeros((delta_ref.shape[0] - heads, span), FULL)


def attend_back_kernel(seq, q_ref, b0, b1, b2, b3, p_ref, do_ref, delta_ref, cos_ref, sin_ref, gq_ref, own_ref, far_ref, send_ref):
    span = q_ref.shape[1]
    per = q_ref.shape[0] // HD
    h = pl.program_id(0)
    kv_t = jnp.concatenate([b0[...], b1[...], b2[...], b3[...]], axis=1)
    kv = kv_t.T
    query, out_grad = beside(q_ref), beside(do_ref)
    delta = jnp.concatenate([delta_ref[pl.ds(per * h + i, 1), :] for i in range(per)], axis=1)
    none = jnp.zeros(out_grad.shape, LOW)
    grad_probs = dot(kv, jnp.concatenate([none, out_grad], axis=0))
    grad_scores = (p_ref[0].astype(FULL) * (grad_probs - delta)).astype(LOW)
    grad_q = dot(kv_t[0:HD, :], grad_scores) * SCALE
    for i in range(per):
        one, two = turn(grad_q[:, i * span : (i + 1) * span], cos_ref[seq], sin_ref[seq], -1.0)
        gq_ref[i * HD : i * HD + HD // 2, :] = one.astype(LOW)
        gq_ref[i * HD + HD // 2 : (i + 1) * HD, :] = two.astype(LOW)
    keys = dot(query, grad_scores, NT).astype(LOW)
    values = dot(out_grad, p_ref[0], NT).astype(LOW)
    for k in range(GROUP):
        out = (own_ref, send_ref.at[0], far_ref, send_ref.at[1])[k]
        part = slice(k * span, (k + 1) * span)
        out[0:HD, :] = keys[:, part]
        out[HD:, :] = values[:, part]


def spread(ranks, acc, own_ref, far_ref, send_ref):
    part = acc.shape[1] // PARTS
    for k, out in enumerate((own_ref, send_ref.at[0], far_ref, send_ref.at[1])):
        for i, slot in enumerate(SLOTS):
            start = pl.multiple_of((slot ^ ranks[1]) * part, 8)
            out[i] = acc[ranks[0] ^ k, pl.ds(start, part), :].astype(LOW)


def query_weight_kernel(ranks, norm_ref, gq_a, gq_b, att_a, att_b, gb_a, gb_b, own_ref, far_ref, send_ref, acc):
    width, span = gq_a.shape
    shard = width // GROUP
    for b in range(GROUP):
        rows = slice(b * shard, (b + 1) * shard)
        acc[b, 0:shard, 0:width] = dot(norm_ref[rows, 0:span], gq_a[...], NT) + dot(norm_ref[rows, span:], gq_b[...], NT)
        acc[b, 0:shard, width:] = dot(att_a[rows, :], gb_a[...], NT) + dot(att_b[rows, :], gb_b[...], NT)
        acc[b, shard:, :] = jnp.zeros((acc.shape[1] - shard, acc.shape[2]), FULL)
    spread(ranks, acc, own_ref, far_ref, send_ref)


def key_weight_kernel(ranks, *refs):
    norm_ref, *terms = refs[0:7]
    cos_ref, sin_ref, part_ref, k0, k1, k2, k3, tok_ref, gm_a, gm_b, gain_a, gain_b = refs[7:19]
    own_ref, far_ref, send_ref, out_ref, gkv_ref, wkv_ref, acc = refs[19:]
    width = norm_ref.shape[0]
    span = gm_a.shape[1]
    shard = width // GROUP
    kw2 = gkv_ref.shape[0]
    kw = kw2 // 2
    assemble(ranks[0], (k0, k1, k2, k3), wkv_ref)
    gain_one = wkv_ref[:, kw2 : kw2 + 1].astype(FULL)
    grad_gain = None
    for s in range(2):
        e0, e1, e2 = terms[3 * s : 3 * s + 3]
        part = slice(s * span, (s + 1) * span)
        grad = e0[...].astype(FULL) + e1[0].astype(FULL) + e2[...].astype(FULL)
        for h in range(kw // HD):
            top = h * 2 * HD
            one, two = turn(grad[top : top + HD, :], cos_ref[s], sin_ref[s], -1.0)
            gkv_ref[h * HD : h * HD + HD // 2, part] = one.astype(LOW)
            gkv_ref[h * HD + HD // 2 : (h + 1) * HD, part] = two.astype(LOW)
            gkv_ref[kw + h * HD : kw + (h + 1) * HD, part] = grad[top + HD : top + 2 * HD, :].astype(LOW)
        grad_norm = part_ref[s] + dot(wkv_ref[:, 0:kw2], gkv_ref[:, part])
        x = tok_ref[s].astype(FULL)
        inverse = lax.rsqrt(jnp.mean(x * x, axis=0, keepdims=True) + NORM_EPS)
        scaled = grad_norm * gain_one
        turned = jnp.mean(scaled * x, axis=0, keepdims=True)
        out_ref[s] = (gm_a, gm_b)[s][...] + inverse * scaled - x * (inverse * inverse * inverse * turned)
        row = dot(jnp.ones((8, span), LOW), (grad_norm * x * inverse).astype(LOW), NT)
        grad_gain = row if grad_gain is None else grad_gain + row
    gains = jnp.concatenate([grad_gain[0:1, :], gain_a[0:1, :] + gain_b[0:1, :], jnp.zeros((6, width), FULL)], axis=0)
    for b in range(GROUP):
        rows = slice(b * shard, (b + 1) * shard)
        acc[b, 0:shard, :] = dot(norm_ref[rows, :], gkv_ref[...], NT)
        acc[b, shard:, :] = jnp.zeros((acc.shape[1] - shard, kw2), FULL)
        acc[b, shard : shard + 8, 0:shard] = gains[:, rows]
    spread(ranks, acc, own_ref, far_ref, send_ref)


def query_grad_kernel(ranks, gq_a, gq_b, q0, q1, q2, q3, out_ref, wq_ref):
    assemble(ranks[0], (q0, q1, q2, q3), wq_ref)
    out_ref[0] = dot(wq_ref[...], gq_a[...])
    out_ref[1] = dot(wq_ref[...], gq_b[...])


def place(slot):
    return ((slot >> 2) & 1) + ((slot >> 1) & 1) * 2


def gathered(ranks, pairs):
    for a in range(PARTS):
        slot = ranks[1] ^ a
        index = place(slot)
        for parity in range(2):

            @pl.when(slot % 2 == parity)
            def _(parity=parity, index=index, a=a):
                for pair in pairs:
                    part = pair[parity].shape[1]
                    pair[2][a * part : (a + 1) * part, :] = pair[parity][index].astype(FULL)


def forward_weights_kernel(ranks, even, odd, *outs):
    columns = outs[0].shape[1]
    for i, out in enumerate(outs):
        part = slice(i * columns, (i + 1) * columns)
        gathered(ranks, [(even.at[:, :, part], odd.at[:, :, part], out)])


def attention_done_kernel(ranks, even, odd, q_ref, o_ref, k_ref, v_ref, gain_ref, scratch):
    shard, width = q_ref.shape
    kw = k_ref.shape[0]
    gathered(ranks, [(even, odd, scratch)])
    q_ref[...] = scratch[0:shard, 0:width]
    o_ref[...] = scratch[0:shard, width : 2 * width]
    k_ref[...] = scratch[0:shard, 2 * width : 2 * width + kw].T
    v_ref[...] = scratch[0:shard, 2 * width + kw :].T
    gain_ref[...] = scratch[shard : shard + 8, 2 * width : 2 * width + shard]


def tables(places):
    half = HD // 2
    frequency = ROPE_BASE ** (-2.0 * jnp.arange(half, dtype=FULL) / HD)
    angles = places.astype(FULL)[:, None, :] * frequency[None, :, None]
    return jnp.cos(angles), jnp.sin(angles)


def body(
    tokens,
    w_query,
    w_key,
    w_value,
    w_out,
    w_gate,
    w_up,
    w_down,
    gain_attn,
    gain_mlp,
    span_order,
    piece_starts,
    cotangent,
):
    ranks = lax.axis_size("rep")
    rank_grp = lax.axis_index("grp")
    seq_count, span, width = tokens.shape
    shard = w_query.shape[0]
    kw = w_key.shape[1]
    kw2 = 2 * kw
    kv_heads = kw // HD
    per = width // kw
    ff = w_gate.shape[1]
    rows = seq_count * span
    length = GROUP * span
    place_of = jnp.stack([rank_grp, lax.axis_index("rep") % PARTS]).astype(jnp.int32)
    tok_t = jnp.swapaxes(tokens, 1, 2)
    cot_t = jnp.swapaxes(cotangent, 1, 2)
    wd_t = w_down.T
    act = whole((width, span))
    seqs = whole((seq_count, width, span))
    one_seq = lambda s: pl.BlockSpec((1, width, span), lambda *_: (s, 0, 0))
    table = whole((seq_count, HD // 2, span))
    gain_spec = whole((width, LANES))
    head = pl.BlockSpec((2 * HD, span), lambda h, *_: (h, 0))
    probs_spec = pl.BlockSpec((1, length, per * span), lambda h, *_: (h, 0, 0))
    q_spec = lambda s: pl.BlockSpec((per * HD, span), lambda h, *_: (h, s))
    per_head = pl.BlockSpec((per * HD, span), lambda h, *_: (h, 0))

    kv_shard = call(
        pack_kernel,
        "pack",
        shape_of((shard, kw2 + LANES)),
        in_specs=[whole((kw, shard))] * 2 + [whole((2, shard))],
        out_specs=whole((shard, kw2 + LANES)),
        micros=2,
    )(w_key.T, w_value.T, jnp.stack([gain_attn, gain_mlp]).astype(FULL))
    kv_flight = Blocks(kv_shard)
    q_flight = Blocks(w_query, kv_shard)
    own_span = lax.dynamic_slice(span_order, (0, rank_grp), (seq_count, 1))
    places = own_span * span + jnp.arange(span, dtype=jnp.int32)[None, :]
    cos_cols, sin_cols = tables(places)
    wgut, wgu = call(
        flip_two_kernel,
        "flip_two",
        (shape_of((2 * ff, width)), shape_of((width, 2 * ff))),
        in_specs=[whole((width, ff))] * 2,
        out_specs=(whole((2 * ff, width)), whole((width, 2 * ff))),
        micros=4,
    )(after(w_gate, kv_flight.sent), w_up)
    wd = call(
        flip_one_kernel,
        "flip_one",
        shape_of((ff, width)),
        in_specs=[whole((width, ff))],
        out_specs=whole((ff, width)),
        micros=2,
    )(after(wd_t, wgut))
    kv_blocks = kv_flight.finish(wd)
    norm_low, kv_a, kv_b, gain_cols = call(
        keys_values_kernel,
        "keys_values",
        (shape_of((width, rows)), shape_of((kw2, span)), shape_of((kw2, span)), shape_of((width, LANES))),
        prefetch=1,
        in_specs=[NEAR] + [whole(kv_shard.shape)] * 4 + [table, table],
        out_specs=(whole((width, rows)), whole((kw2, span)), whole((kw2, span)), gain_spec),
        scratch=[pltpu.VMEM((width, kw2 + LANES), LOW)],
        micros=4.3,
    )(place_of, tok_t, *kv_blocks, cos_cols, sin_cols)
    kv_flight = [Blocks(kv_a), None]
    q_blocks = q_flight.finish(norm_low)
    queries = call(
        queries_kernel,
        "queries",
        shape_of((width, rows)),
        prefetch=1,
        in_specs=[whole((width, rows))] + [whole((shard, width))] * 4 + [table, table],
        out_specs=whole((width, rows)),
        scratch=[pltpu.VMEM((width, width), LOW)],
        micros=4.9,
    )(place_of, norm_low, *q_blocks, cos_cols, sin_cols)

    o_flight = Blocks(w_out, kv_a)
    kv_flight[1] = Blocks(kv_b, *q_blocks)
    cot_flight = [Blocks(cot_t[0], queries), None]
    cot_blocks = [None, None]
    kv_all = [kv_flight[0].finish(queries), None]

    def attend_of(s, query):
        return call(
            functools.partial(attend_kernel, s),
            "attend",
            (shape_of((kv_heads, length, per * span)), shape_of((width, span))),
            prefetch=3,
            grid=(kv_heads,),
            in_specs=[q_spec(s)] + [head] * 4,
            out_specs=(probs_spec, per_head),
            scratch=[pltpu.VMEM((length, span), FULL)],
            micros=10,
        )(place_of, span_order, piece_starts, query, *kv_all[s])

    def middle_of(s, att):
        return call(
            middle_kernel,
            "middle",
            (shape_of((width, span), FULL), shape_of((width, span))),
            prefetch=1,
            in_specs=[act] + [whole((shard, width))] * 4 + [one_seq(s), gain_spec],
            out_specs=(act, act),
            scratch=[pltpu.VMEM((width, width), LOW)],
            micros=3,
        )(place_of, att, *o_blocks, tok_t, gain_cols)

    probs_a, att_a = attend_of(0, queries)
    o_blocks = o_flight.finish(att_a)
    kv_all[1] = kv_flight[1].finish(att_a)
    middle_a, x_a = middle_of(0, att_a)
    x_flight = [Blocks(x_a), None]
    cot_flight[1] = Blocks(cot_t[1], x_flight[0].sent, x_a)
    probs_b, att_b = attend_of(1, after(queries, x_a))
    cot_flight[0].arrive(att_b)
    middle_b, x_b = middle_of(1, after(att_b, *cot_flight[0].ready))
    x_flight[1] = Blocks(x_b)
    x_flight[0].arrive(middle_b)
    cot_blocks[0] = cot_flight[0].finish(middle_b)
    stats, attended, middles = (probs_a, probs_b), (att_a, att_b), (middle_a, middle_b)

    each = pl.BlockSpec((1, width, span), lambda s, *_: (s, 0, 0))
    each_ff = pl.BlockSpec((1, ff, span), lambda s, *_: (s, 0, 0))
    two = shape_of((seq_count, width, span))
    two_ff = shape_of((seq_count, ff, span))
    own_out, own_grad, own_hid, own_gg, own_gu = call(
        own_block_kernel,
        "own_blocks",
        (two, two, two_ff, two_ff, two_ff),
        grid=(seq_count,),
        in_specs=[act, act, each] + [NEAR] * 4,
        out_specs=(each, each, each_ff, each_ff, each_ff),
        scratch=[pltpu.VMEM((width, span), LOW), pltpu.VMEM((2 * ff, span), LOW)],
        micros=8,
    )(after(x_a, *x_flight[0].ready, *cot_blocks[0]), x_b, cot_t, wgut, wgu, wd_t, wd)
    x_blocks = [x_flight[0].finish(own_out), None]
    cot_flight[1].arrive(own_out)

    def other_blocks(s, *others):
        half = pl.BlockSpec((1, width, span), lambda k, *_: (k // 2, 0, 0))
        per_block = pl.BlockSpec((ff, span), lambda k, *_: (0, k))
        act_shape, half_shape, ff_shape = shape_of((width, span)), shape_of((2, width, span)), shape_of((ff, 3 * span))
        return call(
            other_blocks_kernel,
            "other_blocks",
            (act_shape, half_shape, act_shape, half_shape, ff_shape, ff_shape, ff_shape),
            grid=(GROUP - 1,),
            in_specs=[ANY] * 6 + [NEAR] * 4,
            out_specs=(act, half, act, half) + (per_block,) * 3,
            scratch=[
                pltpu.VMEM((6, width, span), LOW),
                pltpu.VMEM((2 * ff, span), LOW),
                pltpu.SemaphoreType.DMA((6,)),
            ],
            micros=12,
        )(after(x_blocks[s][1], *others), *x_blocks[s][2:], *cot_blocks[s][1:], wgut, wgu, wd_t, wd)

    fo_a, so_a, fg_a, sg_a, hid_a, gg_a, gu_a = other_blocks(0, *cot_flight[1].ready)
    grad_a = Terms(own_grad[0], fg_a, sg_a)
    out_a = Terms(own_out[0], fo_a, so_a)
    x_flight[1].arrive(fg_a)
    x_blocks[1] = x_flight[1].finish()
    cot_blocks[1] = cot_flight[1].finish(fg_a)
    fo_b, so_b, fg_b, sg_b, hid_b, gg_b, gu_b = other_blocks(1, fg_a)
    grad_b = Terms(own_grad[1], fg_b, sg_b)
    out_b = Terms(own_out[1], fo_b, so_b)
    stage = (grad_a.cross(fg_b), out_a.cross(fg_b))
    grads = (grad_a, grad_b)

    part = width // PARTS

    def sums(name, blocks, kinds, *others):
        count = len(kinds)
        columns = count * ff
        pieces = call(
            functools.partial(weight_kernel, count),
            name,
            tuple(shape_of((n, part, columns)) for n in (4, 2, 1, 1)),
            prefetch=1,
            grid=(count,),
            in_specs=[ANY] * (2 * GROUP + 3 * count),
            out_specs=tuple(pl.BlockSpec((n, part, ff), lambda m, *_: (0, 0, m)) for n in (4, 2, 1, 1)),
            scratch=[
                pltpu.VMEM((2, width, length), LOW),
                pltpu.VMEM((count, 2, ff, length), LOW),
                pltpu.VMEM((width, ff), FULL),
                pltpu.SemaphoreType.DMA((2 * GROUP + 4 * count,)),
            ],
            micros=2 + 6 * count,
        )(place_of, after(blocks[0], *others), *blocks[1:], *sum(kinds, ()))
        return RepSum(pieces, ranks)

    x_all = x_blocks[0] + x_blocks[1]
    down_sum = sums("down_weights", cot_blocks[0] + cot_blocks[1], [(own_hid, hid_a, hid_b)], *stage)
    done = down_sum.pieces[0]
    stage = (grad_b.cross(done), out_b.beside, done)
    up_sum = sums("gate_up_weights", x_all, [(own_gg, gg_a, gg_b), (own_gu, gu_a, gu_b)], *stage)
    done = up_sum.pieces[0]
    stage = (grad_a.across, out_b.cross(done), down_sum.second(done), out_a.across, done)

    def branch_of(s, *others):
        _, beside_term, across_term = grads[s].all()
        first = whole((1, width, span))
        return call(
            functools.partial(branch_kernel, s),
            "branch",
            (
                shape_of((width, span), FULL),
                shape_of((width, span)),
                shape_of((width, span)),
                shape_of((16, span), FULL),
                shape_of((8, width), FULL),
            ),
            prefetch=1,
            in_specs=[NEAR, NEAR, one_seq(s), first, act, NEAR] + [NEAR] * 5,
            out_specs=(act, act, act, whole((16, span)), whole((8, width))),
            scratch=[pltpu.VMEM((width, width), LOW)],
            micros=4,
        )(place_of, middles[s], cot_t, own_grad, beside_term, after(across_term, *others), gain_cols, *o_blocks, attended[s])

    def attend_back_of(s, out_grad, delta):
        halves = pl.BlockSpec((2, 2 * HD, span), lambda h, *_: (0, h, 0))
        grad_q, *kv_parts = call(
            functools.partial(attend_back_kernel, s),
            "attend_back",
            (shape_of((width, span)), shape_of((kw2, span)), shape_of((kw2, span)), shape_of((2, kw2, span))),
            grid=(kv_heads,),
            in_specs=[q_spec(s)] + [head] * 4 + [probs_spec, per_head, whole((16, span)), table, table],
            out_specs=(per_head, head, head, halves),
            micros=11,
        )(queries, *kv_all[s], stats[s], out_grad, delta, cos_cols, sin_cols)
        return grad_q, Terms(*kv_parts)

    mid_a, branch_a, dout_a, delta_a, gain_a = branch_of(0, *stage)
    stage = (down_sum.third(branch_a), grad_b.across)
    gq_a, kv_grad_a = attend_back_of(0, after(dout_a, *stage), delta_a)
    stage = (out_b.across, down_sum.own(gq_a))
    mid_b, branch_b, dout_b, delta_b, gain_b = branch_of(1, *stage)
    stage = (kv_grad_a.cross(branch_b), up_sum.second(branch_b))
    gq_b, kv_grad_b = attend_back_of(1, after(dout_b, *stage), delta_b)
    stage = (down_sum.spread(gq_b), kv_grad_a.across)

    grown = shard + GAIN_ROWS
    piece = grown // PARTS
    spread_out = lambda columns: (shape_of((PARTS, piece, columns)),) * 2 + (shape_of((2, PARTS, piece, columns)),)
    spread_spec = lambda columns: (whole((PARTS, piece, columns)),) * 2 + (whole((2, PARTS, piece, columns)),)
    query_parts = call(
        query_weight_kernel,
        "query_weights",
        spread_out(2 * width),
        prefetch=1,
        in_specs=[NEAR, NEAR, act] + [NEAR] * 4,
        out_specs=spread_spec(2 * width),
        scratch=[pltpu.VMEM((GROUP, grown, 2 * width), FULL)],
        micros=8,
    )(place_of, norm_low, gq_a, after(gq_b, *stage), *attended, branch_a, branch_b)
    done = query_parts[0]
    stage = (kv_grad_b.cross(done), up_sum.third(done))
    query_terms = Terms(*query_parts, *stage)
    grad_part = call(
        query_grad_kernel,
        "query_grad",
        shape_of((seq_count, width, span), FULL),
        prefetch=1,
        in_specs=[NEAR, act] + [NEAR] * 4,
        out_specs=seqs,
        scratch=[pltpu.VMEM((width, width), LOW)],
        micros=4,
    )(place_of, gq_a, after(gq_b, *stage), *q_blocks)
    stage = (query_terms.cross(grad_part),)
    down_pair = down_sum.done(grad_part)
    block_out = jnp.stack(
        [middle + three(term.all()) for middle, term in zip(after(middles, *stage), (out_a, out_b))]
    )
    stage = (*stage, block_out, down_pair[0], kv_grad_b.across)

    def owned(terms):
        own, beside_term, across = terms.all()
        cuts = (slice(0, 4), slice(4, 6), slice(6, 7), slice(7, 8))
        return [three((own[c], beside_term[:, c], across[c])) for c in cuts]

    first = whole((1, kw2, span))
    terms = []
    for term in (kv_grad_a, kv_grad_b):
        terms += term.all()
    *key_parts, grad_tokens = call(
        key_weight_kernel,
        "key_weights",
        spread_out(kw2) + (shape_of((seq_count, width, span), FULL),),
        prefetch=1,
        in_specs=[NEAR]
        + [whole((kw2, span)), first, whole((kw2, span))] * 2
        + [table, table, seqs]
        + [NEAR] * 7
        + [whole((8, width))] * 2,
        out_specs=spread_spec(kw2) + (seqs,),
        scratch=[
            pltpu.VMEM((kw2, rows), LOW),
            pltpu.VMEM((width, kw2 + LANES), LOW),
            pltpu.VMEM((GROUP, grown, kw2), FULL),
        ],
        micros=10,
    )(
        place_of,
        norm_low,
        after(terms[0], *stage),
        *terms[1:],
        cos_cols,
        sin_cols,
        grad_part,
        *kv_blocks,
        tok_t,
        mid_a,
        mid_b,
        gain_a,
        gain_b,
    )
    stage = (up_sum.own(grad_tokens), down_pair[1])
    key_terms = Terms(*key_parts, *stage)

    def finished(name, kernel, pair, outs, *others):
        columns = pair[0].shape[2]
        return call(
            kernel,
            name,
            (shape_of((width, ff), FULL),) * outs,
            prefetch=1,
            in_specs=[whole((4, part, columns))] * 2,
            out_specs=(whole((width, ff)),) * outs,
            micros=3.5 * outs,
        )(place_of, after(pair[0], *others), pair[1])

    (grad_down,) = finished("down_done", forward_weights_kernel, down_pair, 1, *stage)
    key_terms.cross(grad_down)
    pieces = []
    for query_piece, key_piece in zip(owned(query_terms), owned(key_terms)):
        joint = jnp.concatenate([query_piece, key_piece], axis=-1)
        pieces.append(joint.astype(LOW))
    query_sum = RepSum(pieces, ranks)

    up_sum.spread(*pieces)
    step = query_sum.second()
    up_pair = up_sum.done(step)
    step = query_sum.third(step)
    step = query_sum.own(step)
    step = query_sum.spread(step, up_pair[1])
    grad_gate, grad_up = finished("gate_up_done", forward_weights_kernel, up_pair, 2, step)
    query_pair = query_sum.done(grad_up)
    grad_down = grad_down.T
    grad_query, grad_out, grad_key, grad_value, grad_gains = call(
        attention_done_kernel,
        "attention_done",
        (shape_of((shard, width), FULL),) * 2 + (shape_of((kw, shard), FULL),) * 2 + (shape_of((8, shard), FULL),),
        prefetch=1,
        in_specs=[whole((4, piece, 2 * width + kw2))] * 2,
        out_specs=(whole((shard, width)),) * 2 + (whole((kw, shard)),) * 2 + (whole((8, shard)),),
        scratch=[pltpu.VMEM((grown, 2 * width + kw2), FULL)],
        micros=5,
    )(place_of, *query_pair)
    return (
        jnp.swapaxes(block_out, 1, 2),
        jnp.swapaxes(grad_tokens, 1, 2),
        grad_query,
        grad_key.T,
        grad_value.T,
        grad_out,
        grad_gate,
        grad_up,
        grad_down,
        grad_gains[0],
        grad_gains[1],
    )


def solution(mesh):
    placed = (
        P("rep", "grp", None),
        P("grp", None),
        P("grp", None),
        P("grp", None),
        P("grp", None),
        P(None, "grp"),
        P(None, "grp"),
        P("grp", None),
        P("grp"),
        P("grp"),
        P("rep", None),
        P("rep", None),
        P("rep", "grp", None),
    )
    return jax.shard_map(
        body,
        mesh=mesh,
        in_specs=placed,
        out_specs=(
            P("rep", "grp", None),
            P("rep", "grp", None),
            P("grp", None),
            P("grp", None),
            P("grp", None),
            P("grp", None),
            P(None, "grp"),
            P(None, "grp"),
            P("grp", None),
            P("grp"),
            P("grp"),
        ),
        check_vma=False,
    )
```

```python
import functools

import jax
import jax.numpy as jnp
from jax import lax
from jax.experimental import pallas as pl
from jax.experimental.pallas import tpu as pltpu
from jax.sharding import PartitionSpec as P

HD = 64
PIECE = 256
LANES = 128
GROUP = 4
PARTS = 8
GAIN_ROWS = 16
RATE = 2.0e9
SLOTS = (7, 3, 5, 1, 6, 2, 4, 0)


NORM_EPS = 1e-05
ROPE_BASE = 10000.0
MASKED_SCORE = -1e30
SCALE = HD ** (-0.5)

LOW = jnp.bfloat16
FULL = jnp.float32
NN = (((1,), (0,)), ((), ()))
NT = (((1,), (1,)), ((), ()))
TN = (((0,), (0,)), ((), ()))


def dot(left_mat, right_mat, form=NN):
    return lax.dot_general(left_mat, right_mat, form, preferred_element_type=FULL)


def swap(values, axis, count, mask):
    return lax.ppermute(values, axis, [(i, i ^ mask) for i in range(count)])


def after(values, *others):
    return lax.optimization_barrier((values,) + others)[0] if others else values


class Blocks:
    def __init__(self, own, *others):
        self.own = own
        sent = after(own, *others)
        self.across = swap(sent, "grp", GROUP, 2)
        self.sent = sent

    def arrive(self, *others):
        pair = after((self.sent, self.across), *others)
        self.ready = pair
        self.core = swap(pair[0], "grp", GROUP, 1), swap(pair[1], "grp", GROUP, 1)

    def finish(self, *others):
        if not hasattr(self, "core"):
            self.arrive(*others)
        beside, corner = after(self.core, *others)
        return self.own, beside, self.across, corner


class Terms:
    def __init__(self, own, far, send, *others):
        self.own, self.far = own, far
        self.beside = swap(after(send, *others), "grp", GROUP, 1)

    def cross(self, *others):
        far, beside = after((self.far, self.beside), *others)
        across = (far.astype(FULL) + beside[1].astype(FULL)).astype(LOW)
        self.sent = across
        self.across = swap(across, "grp", GROUP, 2)
        return across

    def all(self):
        return self.own, self.beside, self.across


def three(terms):
    return terms[0].astype(FULL) + terms[1][0].astype(FULL) + terms[2].astype(FULL)


class RepSum:
    def __init__(self, pieces, ranks):
        self.pieces, self.ranks = pieces, ranks
        self.one = swap(pieces[0], "rep", ranks, 1)

    def second(self, *others):
        self.one = after(self.one, *others)
        two = (self.pieces[1].astype(FULL) + self.one[0:2].astype(FULL)).astype(LOW)
        self.held_two = two
        self.two = swap(two, "rep", self.ranks, 2)
        return two

    def third(self, *others):
        self.two = after(self.two, *others)
        four = self.pieces[2].astype(FULL) + self.one[2:3].astype(FULL) + self.two[0:1].astype(FULL)
        four = four.astype(LOW)
        self.four = swap(four, "rep", self.ranks, 4)
        return four

    def own(self, *others):
        ranks = self.ranks
        self.four = after(self.four, *others)
        mine = self.pieces[3].astype(FULL) + self.one[3:4].astype(FULL) + self.two[1:2].astype(FULL)
        mine = (mine + self.four.astype(FULL)).astype(LOW)
        if ranks > PARTS:
            others = [[j * PARTS + i for j in range(ranks // PARTS)] for i in range(PARTS)]
            mine = lax.psum(mine, "rep", axis_index_groups=others)
        self.mine = mine
        self.back = swap(mine, "rep", ranks, 4)
        return mine

    def spread(self, *others):
        self.back = after(self.back, *others)
        held = jnp.concatenate([self.mine, self.back])
        self.held = held
        self.wide = swap(held, "rep", self.ranks, 2)
        return held

    def done(self, *others):
        self.wide = after(self.wide, *others)
        held = jnp.concatenate([self.held, self.wide])
        return held, swap(held, "rep", self.ranks, 1)


class ShortSum(RepSum):
    def second(self, *others):
        one = after(self.one, *others)
        self.one = one
        six = (self.pieces[1][0:1].astype(FULL) + one[0:1].astype(FULL)).astype(LOW)
        two = (self.pieces[1][1:2].astype(FULL) + one[1:2].astype(FULL)).astype(LOW)
        four = (self.pieces[2].astype(FULL) + one[2:3].astype(FULL)).astype(LOW)
        self.terms = [swap(sent, "rep", self.ranks, mask) for sent, mask in ((six, 6), (two, 2), (four, 4))]
        return six, two, four

    def own(self, *others):
        ranks = self.ranks
        terms = after(self.terms, *others)
        mine = self.pieces[3].astype(FULL) + self.one[3:4].astype(FULL)
        mine = (mine + terms[0].astype(FULL) + terms[1].astype(FULL) + terms[2].astype(FULL)).astype(LOW)
        if ranks > PARTS:
            others = [[j * PARTS + i for j in range(ranks // PARTS)] for i in range(PARTS)]
            mine = lax.psum(mine, "rep", axis_index_groups=others)
        self.mine = mine
        self.back = [swap(mine, "rep", ranks, mask) for mask in (4, 2, 6)]
        return mine

    def done(self, *others):
        held = jnp.concatenate([self.mine, *after(self.back, *others)])
        return held, swap(held, "rep", self.ranks, 1)


def call(kernel, name, out_shape, *, grid=(1,), prefetch=0, in_specs, out_specs, scratch=(), micros=1, vmem=36):
    def lies(shape):
        return pltpu.HBM(shape.shape, shape.dtype)

    several = isinstance(out_shape, tuple)
    run = pl.pallas_call(
        kernel,
        name=name,
        out_shape=tuple(map(lies, out_shape)) if several else lies(out_shape),
        grid_spec=pltpu.PrefetchScalarGridSpec(
            num_scalar_prefetch=prefetch,
            grid=grid,
            in_specs=in_specs,
            out_specs=out_specs,
            scratch_shapes=list(scratch),
        ),
        compiler_params=pltpu.CompilerParams(vmem_limit_bytes=vmem << 20),
        cost_estimate=pl.CostEstimate(flops=int(micros * RATE), bytes_accessed=1 << 10, transcendentals=0),
    )

    def placed(*args):
        rest = [
            arg if spec is NEAR else pltpu.with_memory_space_constraint(arg, pltpu.HBM)
            for arg, spec in zip(args[prefetch:], in_specs, strict=True)
        ]
        return run(*args[:prefetch], *rest)

    return placed


def whole(shape):
    return pl.BlockSpec(shape, lambda *_: (0,) * len(shape))


ANY = pl.BlockSpec(memory_space=pl.ANY)
NEAR = pl.BlockSpec(memory_space=pltpu.VMEM)


def shape_of(shape, kind=LOW):
    return jax.ShapeDtypeStruct(shape, kind)


def turn(rows, cosine, sine_val, sign):
    one, two = rows[0 : HD // 2, :], rows[HD // 2 : HD, :]
    sine_val = sine_val * sign
    return one * cosine - two * sine_val, two * cosine + one * sine_val


def assemble(rank, blocks, scratch):
    rows = blocks[0].shape[0]
    for k in range(GROUP):
        start = pl.multiple_of((rank ^ k) * rows, 16)
        scratch[pl.ds(start, rows), :] = blocks[k][...]


def pack_kernel(wk_ref, wv_ref, gains_ref, out_ref):
    kw, shard = wk_ref.shape
    out_ref[:, 0:kw] = wk_ref[...].T
    out_ref[:, kw : 2 * kw] = wv_ref[...].T
    gains = jnp.concatenate([gains_ref[...], jnp.zeros((LANES - 2, shard), FULL)], axis=0)
    out_ref[:, 2 * kw :] = gains.T.astype(LOW)


def flip_two_kernel(wg_ref, wu_ref, wgut_ref, wgu_ref):
    ff = wg_ref.shape[1]
    wgut_ref[0:ff, :] = wg_ref[...].T
    wgut_ref[ff:, :] = wu_ref[...].T
    wgu_ref[:, 0:ff] = wg_ref[...]
    wgu_ref[:, ff:] = wu_ref[...]


def flip_one_kernel(wdt_ref, wd_ref):
    wd_ref[...] = wdt_ref[...].T


def keys_values_kernel(ranks, tok_ref, b0, b1, b2, b3, cos_ref, sin_ref, norm_ref, kv_a, kv_b, gain_ref, w_ref):
    span = tok_ref.shape[2]
    kw2 = kv_a.shape[0]
    kw = kw2 // 2
    assemble(ranks[0], (b0, b1, b2, b3), w_ref)
    gains = w_ref[:, kw2:]
    gain_ref[...] = gains
    gain_one = gains[:, 0:1].astype(FULL)
    for s, out in enumerate((kv_a, kv_b)):
        x = tok_ref[s].astype(FULL)
        inverse = lax.rsqrt(jnp.mean(x * x, axis=0, keepdims=True) + NORM_EPS)
        norm = (x * inverse * gain_one).astype(LOW)
        norm_ref[:, s * span : (s + 1) * span] = norm
        kv = dot(w_ref[:, 0:kw2], norm, TN)
        for h in range(kw // HD):
            one, two = turn(kv[h * HD : (h + 1) * HD, :], cos_ref[s], sin_ref[s], 1.0)
            top = h * 2 * HD
            out[top : top + HD // 2, :] = one.astype(LOW)
            out[top + HD // 2 : top + HD, :] = two.astype(LOW)
            out[top + HD : top + 2 * HD, :] = kv[kw + h * HD : kw + (h + 1) * HD, :].astype(LOW)


def queries_kernel(ranks, norm_ref, b0, b1, b2, b3, cos_ref, sin_ref, q_ref, w_ref):
    width = b0.shape[1]
    span = cos_ref.shape[2]
    assemble(ranks[0], (b0, b1, b2, b3), w_ref)
    for s in range(2):
        part = slice(s * span, (s + 1) * span)
        query = dot(w_ref[...], norm_ref[:, part], TN)
        for h in range(width // HD):
            one, two = turn(query[h * HD : (h + 1) * HD, :], cos_ref[s], sin_ref[s], 1.0)
            q_ref[h * HD : h * HD + HD // 2, part] = (one * SCALE).astype(LOW)
            q_ref[h * HD + HD // 2 : (h + 1) * HD, part] = (two * SCALE).astype(LOW)


def beside(ref):
    return jnp.concatenate([ref[i : i + HD, :] for i in range(0, ref.shape[0], HD)], axis=1)


def attend_kernel(seq, ranks, order, starts, q_ref, b0, b1, b2, b3, p_ref, o_ref, bias_ref):
    span = q_ref.shape[1]
    per = q_ref.shape[0] // HD
    rank = ranks[0]

    @pl.when(pl.program_id(0) == 0)
    def _():
        query_pos = order[seq, rank] * span + lax.broadcasted_iota(jnp.int32, (span, span), 1)
        query_in = []
        for m in range(2):
            start = starts[seq, m]
            query_in.append((query_pos >= start) & (query_pos < start + PIECE))
        for k in range(GROUP):
            key_pos = order[seq, rank ^ k] * span + lax.broadcasted_iota(jnp.int32, (span, span), 0)
            allowed = key_pos <= query_pos
            for m in range(2):
                start = starts[seq, m]
                key_in = (key_pos >= start) & (key_pos < start + PIECE)
                allowed = allowed | (query_in[m] & key_in)
            bias_ref[k * span : (k + 1) * span, :] = jnp.where(allowed, 0.0, MASKED_SCORE)

    kv_t = jnp.concatenate([b0[...], b1[...], b2[...], b3[...]], axis=1)
    keys = kv_t.T[:, 0:HD]
    values_t = kv_t[HD : 2 * HD, :]
    bias = jnp.concatenate([bias_ref[...]] * per, axis=1)
    scores = dot(keys, beside(q_ref)) + bias
    peak = jnp.max(scores, axis=0, keepdims=True)
    exponent = jnp.exp(scores - peak)
    total = jnp.sum(exponent, axis=0, keepdims=True)
    probs = (exponent * (1.0 / total)).astype(LOW)
    p_ref[0] = probs
    mixed = dot(values_t, probs).astype(LOW)
    for i in range(per):
        o_ref[i * HD : (i + 1) * HD, :] = mixed[:, i * span : (i + 1) * span]


def middle_kernel(ranks, att_ref, b0, b1, b2, b3, tok_ref, gain_ref, mid_ref, x_ref, w_ref):
    assemble(ranks[0], (b0, b1, b2, b3), w_ref)
    middle = tok_ref[0].astype(FULL) + dot(w_ref[...], att_ref[...], TN)
    mid_ref[...] = middle
    inverse = lax.rsqrt(jnp.mean(middle * middle, axis=0, keepdims=True) + NORM_EPS)
    x_ref[...] = (middle * inverse * gain_ref[:, 1:2].astype(FULL)).astype(LOW)


def forward_back_step(x, cot, wgut_ref, wgu_ref, wdt_ref, wd_ref, hid_ref, gg_ref, gu_ref, both):
    ff = wd_ref.shape[0]
    gate_up = dot(wgut_ref[...], x)
    grad_hidden = dot(wd_ref[...], cot)
    gate, up = gate_up[0:ff, :], gate_up[ff:, :]
    sig = 1.0 / (1.0 + jnp.exp(-gate))
    swish = gate * sig
    hidden = (swish * up).astype(LOW)
    grad_gate = (grad_hidden * up * sig * (1.0 + gate * (1.0 - sig))).astype(LOW)
    grad_up = (grad_hidden * swish).astype(LOW)
    hid_ref[...] = hidden
    gg_ref[...] = grad_gate
    gu_ref[...] = grad_up
    both[0:ff, :] = grad_gate
    both[ff:, :] = grad_up
    return dot(wgu_ref[...], both[...]).astype(LOW), dot(wdt_ref[...], hidden).astype(LOW)


def own_block_kernel(x_a, x_b, cot_ref, wgut_ref, wgu_ref, wdt_ref, wd_ref, out_ref, grad_ref, hid_ref, gg_ref, gu_ref, held, both):
    s = pl.program_id(0)
    for i, x in enumerate((x_a, x_b)):

        @pl.when(s == i)
        def _(x=x):
            held[...] = x[...]

    grad_x, out = forward_back_step(
        held[...], cot_ref[0], wgut_ref, wgu_ref, wdt_ref, wd_ref, hid_ref.at[0], gg_ref.at[0], gu_ref.at[0], both
    )
    grad_ref[0] = grad_x
    out_ref[0] = out


def other_blocks_kernel(*refs):
    blocks = refs[0:6]
    weights = refs[6:10]
    fo_ref, so_ref, fg_ref, sg_ref, hid_ref, gg_ref, gu_ref, held, both, sem = refs[10:]
    k = pl.program_id(0)
    copies = [pltpu.make_async_copy(block, held.at[i], sem.at[i]) for i, block in enumerate(blocks)]

    @pl.when(k == 0)
    def _():
        for i in range(3):
            copies[i].start()
            copies[3 + i].start()

    for i in range(3):

        @pl.when(k == i)
        def _(i=i):
            copies[i].wait()
            copies[3 + i].wait()

    grad_x, out = forward_back_step(held[k], held[3 + k], *weights, hid_ref, gg_ref, gu_ref, both)

    @pl.when(k == 1)
    def _():
        fg_ref[...] = grad_x
        fo_ref[...] = out

    @pl.when(k != 1)
    def _():
        sg_ref[0] = grad_x
        so_ref[0] = out


def weight_kernel(kinds, ranks, *refs):
    blocks = refs[0 : 2 * GROUP]
    rights = refs[2 * GROUP : 2 * GROUP + 3 * kinds]
    outs = refs[2 * GROUP + 3 * kinds : 2 * GROUP + 3 * kinds + 4]
    left, right, acc, sem = refs[2 * GROUP + 3 * kinds + 4 :]
    span = left.shape[2] // GROUP
    kind = pl.program_id(0)
    lefts, loads = [], []
    for b, block in enumerate(blocks):
        s, k = divmod(b, GROUP)
        lefts.append(pltpu.make_async_copy(block, left.at[s, :, pl.ds(k * span, span)], sem.at[b]))
    for n in range(kinds):
        own, *others = rights[3 * n : 3 * n + 3]
        for s in range(2):
            for i, (source, part) in enumerate(((own.at[s], slice(0, span)), (others[s], slice(span, GROUP * span)))):
                at = sem.at[2 * GROUP + 4 * n + 2 * s + i]
                loads.append(pltpu.make_async_copy(source, right.at[n, s, :, part], at))

    @pl.when(kind == 0)
    def _():
        for copy in loads[0:2] + lefts[:GROUP] + loads[2:4] + lefts[GROUP:] + loads[4:]:
            copy.start()
        for copy in loads[0:2] + lefts[:GROUP]:
            copy.wait()

    for n in range(1, kinds):

        @pl.when(kind == n)
        def _(n=n):
            for copy in loads[4 * n : 4 * n + 4]:
                copy.wait()

    acc[...] = dot(left[0], right[kind, 0], NT)

    @pl.when(kind == 0)
    def _():
        for copy in loads[2:4] + lefts[GROUP:]:
            copy.wait()

    acc[...] += dot(left[1], right[kind, 1], NT)
    part = acc.shape[0] // PARTS
    places = [(outs[0], i) for i in range(4)] + [(outs[1], 0), (outs[1], 1), (outs[2], 0), (outs[3], 0)]
    for (out, i), slot in zip(places, SLOTS):
        start = pl.multiple_of((slot ^ ranks[1]) * part, 8)
        out[i] = acc[pl.ds(start, part), :].astype(LOW)


def branch_kernel(seq, ranks, mid_ref, cot_ref, e0, e1, e2, gain_ref, b0, b1, b2, b3, att_ref, gm_ref, gb_ref, do_ref, delta_ref, gain_out, w_ref):
    width, span = mid_ref.shape
    assemble(ranks[0], (b0, b1, b2, b3), w_ref)
    middle = mid_ref[...]
    grad = e0[0].astype(FULL) + e1[0].astype(FULL) + e2[...].astype(FULL)
    inverse = lax.rsqrt(jnp.mean(middle * middle, axis=0, keepdims=True) + NORM_EPS)
    scaled = grad * gain_ref[:, 1:2].astype(FULL)
    turned = jnp.mean(scaled * middle, axis=0, keepdims=True)
    grad_middle = cot_ref[seq].astype(FULL) + inverse * scaled - middle * (inverse * inverse * inverse * turned)
    gain_out[...] = dot(jnp.ones((8, span), LOW), (grad * middle * inverse).astype(LOW), NT)
    gm_ref[...] = grad_middle
    branch = grad_middle.astype(LOW)
    gb_ref[...] = branch
    grad_att = dot(w_ref[...], branch).astype(LOW)
    do_ref[...] = grad_att
    both = grad_att.astype(FULL) * att_ref[...].astype(FULL)
    heads = width // HD
    for h in range(heads):
        delta_ref[h : h + 1, :] = jnp.sum(both[h * HD : (h + 1) * HD, :], axis=0, keepdims=True)
    delta_ref[heads:, :] = jnp.zeros((delta_ref.shape[0] - heads, span), FULL)


def attend_back_kernel(seq, q_ref, b0, b1, b2, b3, p_ref, do_ref, delta_ref, cos_ref, sin_ref, gq_ref, own_ref, far_ref, send_ref):
    span = q_ref.shape[1]
    per = q_ref.shape[0] // HD
    h = pl.program_id(0)
    kv_t = jnp.concatenate([b0[...], b1[...], b2[...], b3[...]], axis=1)
    kv = kv_t.T
    query, out_grad = beside(q_ref), beside(do_ref)
    delta = jnp.concatenate([delta_ref[pl.ds(per * h + i, 1), :] for i in range(per)], axis=1)
    none = jnp.zeros(out_grad.shape, LOW)
    grad_probs = dot(kv, jnp.concatenate([none, out_grad], axis=0))
    grad_scores = (p_ref[0].astype(FULL) * (grad_probs - delta)).astype(LOW)
    grad_q = dot(kv_t[0:HD, :], grad_scores) * SCALE
    for i in range(per):
        one, two = turn(grad_q[:, i * span : (i + 1) * span], cos_ref[seq], sin_ref[seq], -1.0)
        gq_ref[i * HD : i * HD + HD // 2, :] = one.astype(LOW)
        gq_ref[i * HD + HD // 2 : (i + 1) * HD, :] = two.astype(LOW)
    keys = dot(query, grad_scores, NT).astype(LOW)
    values = dot(out_grad, p_ref[0], NT).astype(LOW)
    for k in range(GROUP):
        out = (own_ref, send_ref.at[0], far_ref, send_ref.at[1])[k]
        part = slice(k * span, (k + 1) * span)
        out[0:HD, :] = keys[:, part]
        out[HD:, :] = values[:, part]


def spread(ranks, acc, own_ref, far_ref, send_ref):
    part = acc.shape[1] // PARTS
    for k, out in enumerate((own_ref, send_ref.at[0], far_ref, send_ref.at[1])):
        for i, slot in enumerate(SLOTS):
            start = pl.multiple_of((slot ^ ranks[1]) * part, 8)
            out[i] = acc[ranks[0] ^ k, pl.ds(start, part), :].astype(LOW)


def query_weight_kernel(ranks, norm_ref, gq_a, gq_b, att_a, att_b, gb_a, gb_b, own_ref, far_ref, send_ref, acc):
    width, span = gq_a.shape
    shard = width // GROUP
    for b in range(GROUP):
        rows = slice(b * shard, (b + 1) * shard)
        acc[b, 0:shard, 0:width] = dot(norm_ref[rows, 0:span], gq_a[...], NT) + dot(norm_ref[rows, span:], gq_b[...], NT)
        acc[b, 0:shard, width:] = dot(att_a[rows, :], gb_a[...], NT) + dot(att_b[rows, :], gb_b[...], NT)
        acc[b, shard:, :] = jnp.zeros((acc.shape[1] - shard, acc.shape[2]), FULL)
    spread(ranks, acc, own_ref, far_ref, send_ref)


def key_weight_kernel(ranks, *refs):
    norm_ref, *terms = refs[0:7]
    cos_ref, sin_ref, part_ref, k0, k1, k2, k3, tok_ref, gm_a, gm_b, gain_a, gain_b = refs[7:19]
    own_ref, far_ref, send_ref, out_ref, gkv_ref, wkv_ref, acc = refs[19:]
    width = norm_ref.shape[0]
    span = gm_a.shape[1]
    shard = width // GROUP
    kw2 = gkv_ref.shape[0]
    kw = kw2 // 2
    assemble(ranks[0], (k0, k1, k2, k3), wkv_ref)
    gain_one = wkv_ref[:, kw2 : kw2 + 1].astype(FULL)
    grad_gain = None
    for s in range(2):
        e0, e1, e2 = terms[3 * s : 3 * s + 3]
        part = slice(s * span, (s + 1) * span)
        grad = e0[...].astype(FULL) + e1[0].astype(FULL) + e2[...].astype(FULL)
        for h in range(kw // HD):
            top = h * 2 * HD
            one, two = turn(grad[top : top + HD, :], cos_ref[s], sin_ref[s], -1.0)
            gkv_ref[h * HD : h * HD + HD // 2, part] = one.astype(LOW)
            gkv_ref[h * HD + HD // 2 : (h + 1) * HD, part] = two.astype(LOW)
            gkv_ref[kw + h * HD : kw + (h + 1) * HD, part] = grad[top + HD : top + 2 * HD, :].astype(LOW)
        grad_norm = part_ref[s] + dot(wkv_ref[:, 0:kw2], gkv_ref[:, part])
        x = tok_ref[s].astype(FULL)
        inverse = lax.rsqrt(jnp.mean(x * x, axis=0, keepdims=True) + NORM_EPS)
        scaled = grad_norm * gain_one
        turned = jnp.mean(scaled * x, axis=0, keepdims=True)
        out_ref[s] = (gm_a, gm_b)[s][...] + inverse * scaled - x * (inverse * inverse * inverse * turned)
        row = dot(jnp.ones((8, span), LOW), (grad_norm * x * inverse).astype(LOW), NT)
        grad_gain = row if grad_gain is None else grad_gain + row
    gains = jnp.concatenate([grad_gain[0:1, :], gain_a[0:1, :] + gain_b[0:1, :], jnp.zeros((6, width), FULL)], axis=0)
    for b in range(GROUP):
        rows = slice(b * shard, (b + 1) * shard)
        acc[b, 0:shard, :] = dot(norm_ref[rows, :], gkv_ref[...], NT)
        acc[b, shard:, :] = jnp.zeros((acc.shape[1] - shard, kw2), FULL)
        acc[b, shard : shard + 8, 0:shard] = gains[:, rows]
    spread(ranks, acc, own_ref, far_ref, send_ref)


def query_grad_kernel(ranks, gq_a, gq_b, q0, q1, q2, q3, out_ref, wq_ref):
    assemble(ranks[0], (q0, q1, q2, q3), wq_ref)
    out_ref[0] = dot(wq_ref[...], gq_a[...])
    out_ref[1] = dot(wq_ref[...], gq_b[...])


def place(slot):
    return ((slot >> 2) & 1) + ((slot >> 1) & 1) * 2


def gathered(ranks, pairs):
    for a in range(PARTS):
        slot = ranks[1] ^ a
        index = place(slot)
        for parity in range(2):

            @pl.when(slot % 2 == parity)
            def _(parity=parity, index=index, a=a):
                for pair in pairs:
                    part = pair[parity].shape[1]
                    pair[2][a * part : (a + 1) * part, :] = pair[parity][index].astype(FULL)


def forward_weights_kernel(ranks, even, odd, *outs):
    columns = outs[0].shape[1]
    for i, out in enumerate(outs):
        part = slice(i * columns, (i + 1) * columns)
        gathered(ranks, [(even.at[:, :, part], odd.at[:, :, part], out)])


def attention_done_kernel(ranks, even, odd, q_ref, o_ref, k_ref, v_ref, gain_ref, scratch):
    shard, width = q_ref.shape
    kw = k_ref.shape[0]
    gathered(ranks, [(even, odd, scratch)])
    q_ref[...] = scratch[0:shard, 0:width]
    o_ref[...] = scratch[0:shard, width : 2 * width]
    k_ref[...] = scratch[0:shard, 2 * width : 2 * width + kw].T
    v_ref[...] = scratch[0:shard, 2 * width + kw :].T
    gain_ref[...] = scratch[shard : shard + 8, 2 * width : 2 * width + shard]


def tables(places):
    half = HD // 2
    frequency = ROPE_BASE ** (-2.0 * jnp.arange(half, dtype=FULL) / HD)
    angles = places.astype(FULL)[:, None, :] * frequency[None, :, None]
    return jnp.cos(angles), jnp.sin(angles)


def body(
    tokens,
    w_query,
    w_key,
    w_value,
    w_out,
    w_gate,
    w_up,
    w_down,
    gain_attn,
    gain_mlp,
    span_order,
    piece_starts,
    cotangent,
):
    ranks = lax.axis_size("rep")
    rank_grp = lax.axis_index("grp")
    seq_count, span, width = tokens.shape
    shard = w_query.shape[0]
    kw = w_key.shape[1]
    kw2 = 2 * kw
    kv_heads = kw // HD
    per = width // kw
    ff = w_gate.shape[1]
    rows = seq_count * span
    length = GROUP * span
    place_of = jnp.stack([rank_grp, lax.axis_index("rep") % PARTS]).astype(jnp.int32)
    tok_t = jnp.swapaxes(tokens, 1, 2)
    cot_t = jnp.swapaxes(cotangent, 1, 2)
    wd_t = w_down.T
    act = whole((width, span))
    seqs = whole((seq_count, width, span))
    one_seq = lambda s: pl.BlockSpec((1, width, span), lambda *_: (s, 0, 0))
    table = whole((seq_count, HD // 2, span))
    gain_spec = whole((width, LANES))
    head = pl.BlockSpec((2 * HD, span), lambda h, *_: (h, 0))
    probs_spec = pl.BlockSpec((1, length, per * span), lambda h, *_: (h, 0, 0))
    q_spec = lambda s: pl.BlockSpec((per * HD, span), lambda h, *_: (h, s))
    per_head = pl.BlockSpec((per * HD, span), lambda h, *_: (h, 0))

    kv_shard = call(
        pack_kernel,
        "pack",
        shape_of((shard, kw2 + LANES)),
        in_specs=[whole((kw, shard))] * 2 + [whole((2, shard))],
        out_specs=whole((shard, kw2 + LANES)),
        micros=2,
    )(w_key.T, w_value.T, jnp.stack([gain_attn, gain_mlp]).astype(FULL))
    kv_flight = Blocks(kv_shard)
    q_flight = Blocks(w_query, kv_shard)
    own_span = lax.dynamic_slice(span_order, (0, rank_grp), (seq_count, 1))
    places = own_span * span + jnp.arange(span, dtype=jnp.int32)[None, :]
    cos_cols, sin_cols = tables(places)
    wgut, wgu = call(
        flip_two_kernel,
        "flip_two",
        (shape_of((2 * ff, width)), shape_of((width, 2 * ff))),
        in_specs=[whole((width, ff))] * 2,
        out_specs=(whole((2 * ff, width)), whole((width, 2 * ff))),
        micros=4,
    )(after(w_gate, kv_flight.sent), w_up)
    wd = call(
        flip_one_kernel,
        "flip_one",
        shape_of((ff, width)),
        in_specs=[whole((width, ff))],
        out_specs=whole((ff, width)),
        micros=2,
    )(after(wd_t, wgut))
    kv_blocks = kv_flight.finish(wd)
    norm_low, kv_a, kv_b, gain_cols = call(
        keys_values_kernel,
        "keys_values",
        (shape_of((width, rows)), shape_of((kw2, span)), shape_of((kw2, span)), shape_of((width, LANES))),
        prefetch=1,
        in_specs=[NEAR] + [whole(kv_shard.shape)] * 4 + [table, table],
        out_specs=(whole((width, rows)), whole((kw2, span)), whole((kw2, span)), gain_spec),
        scratch=[pltpu.VMEM((width, kw2 + LANES), LOW)],
        micros=4.3,
    )(place_of, tok_t, *kv_blocks, cos_cols, sin_cols)
    kv_flight = [Blocks(kv_a), None]
    q_blocks = q_flight.finish(norm_low)
    queries = call(
        queries_kernel,
        "queries",
        shape_of((width, rows)),
        prefetch=1,
        in_specs=[whole((width, rows))] + [whole((shard, width))] * 4 + [table, table],
        out_specs=whole((width, rows)),
        scratch=[pltpu.VMEM((width, width), LOW)],
        micros=0.1,
    )(place_of, norm_low, *q_blocks, cos_cols, sin_cols)

    o_flight = Blocks(w_out, kv_a)
    kv_flight[1] = Blocks(kv_b, *q_blocks)
    cot_flight = [Blocks(cot_t[0], queries), None]
    cot_blocks = [None, None]
    kv_all = [kv_flight[0].finish(queries), None]

    def attend_of(s, query):
        return call(
            functools.partial(attend_kernel, s),
            "attend",
            (shape_of((kv_heads, length, per * span)), shape_of((width, span))),
            prefetch=3,
            grid=(kv_heads,),
            in_specs=[q_spec(s)] + [head] * 4,
            out_specs=(probs_spec, per_head),
            scratch=[pltpu.VMEM((length, span), FULL)],
            micros=0.1,
        )(place_of, span_order, piece_starts, query, *kv_all[s])

    def middle_of(s, att):
        return call(
            middle_kernel,
            "middle",
            (shape_of((width, span), FULL), shape_of((width, span))),
            prefetch=1,
            in_specs=[act] + [whole((shard, width))] * 4 + [one_seq(s), gain_spec],
            out_specs=(act, act),
            scratch=[pltpu.VMEM((width, width), LOW)],
            micros=3,
        )(place_of, att, *o_blocks, tok_t, gain_cols)

    probs_a, att_a = attend_of(0, queries)
    o_blocks = o_flight.finish(att_a)
    kv_all[1] = kv_flight[1].finish(att_a)
    middle_a, x_a = middle_of(0, att_a)
    x_flight = [Blocks(x_a), None]
    cot_flight[1] = Blocks(cot_t[1], x_flight[0].sent, x_a)
    probs_b, att_b = attend_of(1, after(queries, x_a))
    cot_flight[0].arrive(att_b)
    middle_b, x_b = middle_of(1, after(att_b, *cot_flight[0].ready))
    x_flight[1] = Blocks(x_b)
    x_flight[0].arrive(middle_b)
    cot_blocks[0] = cot_flight[0].finish(middle_b)
    stats, attended, middles = (probs_a, probs_b), (att_a, att_b), (middle_a, middle_b)

    each = pl.BlockSpec((1, width, span), lambda s, *_: (s, 0, 0))
    each_ff = pl.BlockSpec((1, ff, span), lambda s, *_: (s, 0, 0))
    two = shape_of((seq_count, width, span))
    two_ff = shape_of((seq_count, ff, span))
    own_out, own_grad, own_hid, own_gg, own_gu = call(
        own_block_kernel,
        "own_blocks",
        (two, two, two_ff, two_ff, two_ff),
        grid=(seq_count,),
        in_specs=[act, act, each] + [NEAR] * 4,
        out_specs=(each, each, each_ff, each_ff, each_ff),
        scratch=[pltpu.VMEM((width, span), LOW), pltpu.VMEM((2 * ff, span), LOW)],
        micros=8,
    )(after(x_a, *x_flight[0].ready, *cot_blocks[0]), x_b, cot_t, wgut, wgu, wd_t, wd)
    x_blocks = [x_flight[0].finish(own_out), None]
    cot_flight[1].arrive(own_out)

    def other_blocks(s, *others):
        half = pl.BlockSpec((1, width, span), lambda k, *_: (k // 2, 0, 0))
        per_block = pl.BlockSpec((ff, span), lambda k, *_: (0, k))
        act_shape, half_shape, ff_shape = shape_of((width, span)), shape_of((2, width, span)), shape_of((ff, 3 * span))
        return call(
            other_blocks_kernel,
            "other_blocks",
            (act_shape, half_shape, act_shape, half_shape, ff_shape, ff_shape, ff_shape),
            grid=(GROUP - 1,),
            in_specs=[ANY] * 6 + [NEAR] * 4,
            out_specs=(act, half, act, half) + (per_block,) * 3,
            scratch=[
                pltpu.VMEM((6, width, span), LOW),
                pltpu.VMEM((2 * ff, span), LOW),
                pltpu.SemaphoreType.DMA((6,)),
            ],
            micros=12,
        )(after(x_blocks[s][1], *others), *x_blocks[s][2:], *cot_blocks[s][1:], wgut, wgu, wd_t, wd)

    fo_a, so_a, fg_a, sg_a, hid_a, gg_a, gu_a = other_blocks(0, *cot_flight[1].ready)
    grad_a = Terms(own_grad[0], fg_a, sg_a)
    out_a = Terms(own_out[0], fo_a, so_a)
    x_flight[1].arrive(fg_a)
    x_blocks[1] = x_flight[1].finish()
    cot_blocks[1] = cot_flight[1].finish(fg_a)
    fo_b, so_b, fg_b, sg_b, hid_b, gg_b, gu_b = other_blocks(1, fg_a)
    grad_b = Terms(own_grad[1], fg_b, sg_b)
    out_b = Terms(own_out[1], fo_b, so_b)
    stage = (grad_a.cross(fg_b), out_a.cross(fg_b))
    grads = (grad_a, grad_b)

    part = width // PARTS

    def sums(name, blocks, kinds, *others):
        count = len(kinds)
        columns = count * ff
        pieces = call(
            functools.partial(weight_kernel, count),
            name,
            tuple(shape_of((n, part, columns)) for n in (4, 2, 1, 1)),
            prefetch=1,
            grid=(count,),
            in_specs=[ANY] * (2 * GROUP + 3 * count),
            out_specs=tuple(pl.BlockSpec((n, part, ff), lambda m, *_: (0, 0, m)) for n in (4, 2, 1, 1)),
            scratch=[
                pltpu.VMEM((2, width, length), LOW),
                pltpu.VMEM((count, 2, ff, length), LOW),
                pltpu.VMEM((width, ff), FULL),
                pltpu.SemaphoreType.DMA((2 * GROUP + 4 * count,)),
            ],
            micros=2 + 6 * count,
        )(place_of, after(blocks[0], *others), *blocks[1:], *sum(kinds, ()))
        return RepSum(pieces, ranks)

    x_all = x_blocks[0] + x_blocks[1]
    down_sum = sums("down_weights", cot_blocks[0] + cot_blocks[1], [(own_hid, hid_a, hid_b)], *stage)
    done = down_sum.pieces[0]
    stage = (grad_b.cross(done), out_b.beside, done)
    up_sum = sums("gate_up_weights", x_all, [(own_gg, gg_a, gg_b), (own_gu, gu_a, gu_b)], *stage)
    done = up_sum.pieces[0]
    stage = (grad_a.across, out_b.cross(done), down_sum.second(done), out_a.across, done)

    def branch_of(s, *others):
        _, beside_term, across_term = grads[s].all()
        first = whole((1, width, span))
        return call(
            functools.partial(branch_kernel, s),
            "branch",
            (
                shape_of((width, span), FULL),
                shape_of((width, span)),
                shape_of((width, span)),
                shape_of((16, span), FULL),
                shape_of((8, width), FULL),
            ),
            prefetch=1,
            in_specs=[NEAR, NEAR, one_seq(s), first, act, NEAR] + [NEAR] * 5,
            out_specs=(act, act, act, whole((16, span)), whole((8, width))),
            scratch=[pltpu.VMEM((width, width), LOW)],
            micros=4,
        )(place_of, middles[s], cot_t, own_grad, beside_term, after(across_term, *others), gain_cols, *o_blocks, attended[s])

    def attend_back_of(s, out_grad, delta):
        halves = pl.BlockSpec((2, 2 * HD, span), lambda h, *_: (0, h, 0))
        grad_q, *kv_parts = call(
            functools.partial(attend_back_kernel, s),
            "attend_back",
            (shape_of((width, span)), shape_of((kw2, span)), shape_of((kw2, span)), shape_of((2, kw2, span))),
            grid=(kv_heads,),
            in_specs=[q_spec(s)] + [head] * 4 + [probs_spec, per_head, whole((16, span)), table, table],
            out_specs=(per_head, head, head, halves),
            micros=11,
        )(queries, *kv_all[s], stats[s], out_grad, delta, cos_cols, sin_cols)
        return grad_q, Terms(*kv_parts)

    mid_a, branch_a, dout_a, delta_a, gain_a = branch_of(0, *stage)
    stage = (down_sum.third(branch_a), grad_b.across)
    gq_a, kv_grad_a = attend_back_of(0, after(dout_a, *stage), delta_a)
    stage = (out_b.across, down_sum.own(gq_a))
    mid_b, branch_b, dout_b, delta_b, gain_b = branch_of(1, *stage)
    stage = (kv_grad_a.cross(branch_b), up_sum.second(branch_b))
    gq_b, kv_grad_b = attend_back_of(1, after(dout_b, *stage), delta_b)
    stage = (down_sum.spread(gq_b), kv_grad_a.across)

    grown = shard + GAIN_ROWS
    piece = grown // PARTS
    spread_out = lambda columns: (shape_of((PARTS, piece, columns)),) * 2 + (shape_of((2, PARTS, piece, columns)),)
    spread_spec = lambda columns: (whole((PARTS, piece, columns)),) * 2 + (whole((2, PARTS, piece, columns)),)
    query_parts = call(
        query_weight_kernel,
        "query_weights",
        spread_out(2 * width),
        prefetch=1,
        in_specs=[NEAR, NEAR, act] + [NEAR] * 4,
        out_specs=spread_spec(2 * width),
        scratch=[pltpu.VMEM((GROUP, grown, 2 * width), FULL)],
        micros=8,
    )(place_of, norm_low, gq_a, after(gq_b, *stage), *attended, branch_a, branch_b)
    done = query_parts[0]
    stage = (kv_grad_b.cross(done), up_sum.third(done))
    query_terms = Terms(*query_parts, *stage)
    grad_part = call(
        query_grad_kernel,
        "query_grad",
        shape_of((seq_count, width, span), FULL),
        prefetch=1,
        in_specs=[NEAR, act] + [NEAR] * 4,
        out_specs=seqs,
        scratch=[pltpu.VMEM((width, width), LOW)],
        micros=4,
    )(place_of, gq_a, after(gq_b, *stage), *q_blocks)
    stage = (query_terms.cross(grad_part),)
    stage = (*stage, kv_grad_b.across)

    def owned(terms):
        own, beside_term, across = terms.all()
        cuts = (slice(0, 4), slice(4, 6), slice(6, 7), slice(7, 8))
        return [three((own[c], beside_term[:, c], across[c])) for c in cuts]

    first = whole((1, kw2, span))
    terms = []
    for term in (kv_grad_a, kv_grad_b):
        terms += term.all()
    *key_parts, grad_tokens = call(
        key_weight_kernel,
        "key_weights",
        spread_out(kw2) + (shape_of((seq_count, width, span), FULL),),
        prefetch=1,
        in_specs=[NEAR]
        + [whole((kw2, span)), first, whole((kw2, span))] * 2
        + [table, table, seqs]
        + [NEAR] * 7
        + [whole((8, width))] * 2,
        out_specs=spread_spec(kw2) + (seqs,),
        scratch=[
            pltpu.VMEM((kw2, rows), LOW),
            pltpu.VMEM((width, kw2 + LANES), LOW),
            pltpu.VMEM((GROUP, grown, kw2), FULL),
        ],
        micros=10,
    )(
        place_of,
        norm_low,
        after(terms[0], *stage),
        *terms[1:],
        cos_cols,
        sin_cols,
        grad_part,
        *kv_blocks,
        tok_t,
        mid_a,
        mid_b,
        gain_a,
        gain_b,
    )
    down_pair = down_sum.done(grad_tokens)
    stage = (up_sum.own(grad_tokens), down_pair[0])
    key_terms = Terms(*key_parts)

    def finished(name, kernel, pair, outs, *others):
        columns = pair[0].shape[2]
        return call(
            kernel,
            name,
            (shape_of((width, ff), FULL),) * outs,
            prefetch=1,
            in_specs=[whole((4, part, columns))] * 2,
            out_specs=(whole((width, ff)),) * outs,
            micros=3.5 * outs,
        )(place_of, after(pair[0], *others), pair[1])

    block_out = jnp.stack(
        [middle + three(term.all()) for middle, term in zip(after(middles, *stage), (out_a, out_b))]
    )
    key_terms.cross(block_out)
    pieces = []
    for query_piece, key_piece in zip(owned(query_terms), owned(key_terms)):
        joint = jnp.concatenate([query_piece, key_piece], axis=-1)
        pieces.append(joint.astype(LOW))
    query_sum = ShortSum(pieces, ranks)

    up_sum.spread(*pieces)
    (grad_down,) = finished("down_done", forward_weights_kernel, down_pair, 1, *pieces)
    step = query_sum.second(grad_down)
    up_pair = up_sum.done(*step)
    step = query_sum.own(up_pair[0])
    query_pair = query_sum.done(step, up_pair[1])
    grad_gate, grad_up = finished("gate_up_done", forward_weights_kernel, up_pair, 2, query_pair[0])
    grad_down = grad_down.T
    grad_query, grad_out, grad_key, grad_value, grad_gains = call(
        attention_done_kernel,
        "attention_done",
        (shape_of((shard, width), FULL),) * 2 + (shape_of((kw, shard), FULL),) * 2 + (shape_of((8, shard), FULL),),
        prefetch=1,
        in_specs=[whole((4, piece, 2 * width + kw2))] * 2,
        out_specs=(whole((shard, width)),) * 2 + (whole((kw, shard)),) * 2 + (whole((8, shard)),),
        scratch=[pltpu.VMEM((grown, 2 * width + kw2), FULL)],
        micros=5,
    )(place_of, *query_pair)
    return (
        jnp.swapaxes(block_out, 1, 2),
        jnp.swapaxes(grad_tokens, 1, 2),
        grad_query,
        grad_key.T,
        grad_value.T,
        grad_out,
        grad_gate,
        grad_up,
        grad_down,
        grad_gains[0],
        grad_gains[1],
    )


def solution(mesh):
    placed = (
        P("rep", "grp", None),
        P("grp", None),
        P("grp", None),
        P("grp", None),
        P("grp", None),
        P(None, "grp"),
        P(None, "grp"),
        P("grp", None),
        P("grp"),
        P("grp"),
        P("rep", None),
        P("rep", None),
        P("rep", "grp", None),
    )
    return jax.shard_map(
        body,
        mesh=mesh,
        in_specs=placed,
        out_specs=(
            P("rep", "grp", None),
            P("rep", "grp", None),
            P("grp", None),
            P("grp", None),
            P("grp", None),
            P("grp", None),
            P(None, "grp"),
            P(None, "grp"),
            P("grp", None),
            P("grp"),
            P("grp"),
        ),
        check_vma=False,
    )
```

```python
import functools

import jax
import jax.numpy as jnp
from jax import lax
from jax.experimental import pallas as pl
from jax.experimental.pallas import tpu as pltpu
from jax.sharding import PartitionSpec as P

HD = 64
PIECE = 256
LANES = 128
GROUP = 4
PARTS = 8
GAIN_ROWS = 16
RATE = 2.0e9
SLOTS = (7, 3, 5, 1, 6, 2, 4, 0)


NORM_EPS = 1e-05
ROPE_BASE = 10000.0
MASKED_SCORE = -1e30
SCALE = HD ** (-0.5)

LOW = jnp.bfloat16
FULL = jnp.float32
NN = (((1,), (0,)), ((), ()))
NT = (((1,), (1,)), ((), ()))
TN = (((0,), (0,)), ((), ()))


def dot(left_mat, right_mat, form=NN):
    return lax.dot_general(left_mat, right_mat, form, preferred_element_type=FULL)


def swap(values, axis, count, mask):
    return lax.ppermute(values, axis, [(i, i ^ mask) for i in range(count)])


def after(values, *others):
    return lax.optimization_barrier((values,) + others)[0] if others else values


class Blocks:
    def __init__(self, own, *others):
        self.own = own
        sent = after(own, *others)
        self.across = swap(sent, "grp", GROUP, 2)
        self.sent = sent

    def arrive(self, *others):
        pair = after((self.sent, self.across), *others)
        self.ready = pair
        self.core = swap(pair[0], "grp", GROUP, 1), swap(pair[1], "grp", GROUP, 1)

    def finish(self, *others):
        if not hasattr(self, "core"):
            self.arrive(*others)
        beside, corner = after(self.core, *others)
        return self.own, beside, self.across, corner


class Terms:
    def __init__(self, own, far, send, *others):
        self.own, self.far = own, far
        self.beside = swap(after(send, *others), "grp", GROUP, 1)

    def cross(self, *others):
        far, beside = after((self.far, self.beside), *others)
        across = (far.astype(FULL) + beside[1].astype(FULL)).astype(LOW)
        self.sent = across
        self.across = swap(across, "grp", GROUP, 2)
        return across

    def all(self):
        return self.own, self.beside, self.across


def three(terms):
    return terms[0].astype(FULL) + terms[1][0].astype(FULL) + terms[2].astype(FULL)


class RepSum:
    def __init__(self, pieces, ranks):
        self.pieces, self.ranks = pieces, ranks
        self.one = swap(pieces[0], "rep", ranks, 1)

    def second(self, *others):
        self.one = after(self.one, *others)
        two = (self.pieces[1].astype(FULL) + self.one[0:2].astype(FULL)).astype(LOW)
        self.held_two = two
        self.two = swap(two, "rep", self.ranks, 2)
        return two

    def third(self, *others):
        self.two = after(self.two, *others)
        four = self.pieces[2].astype(FULL) + self.one[2:3].astype(FULL) + self.two[0:1].astype(FULL)
        four = four.astype(LOW)
        self.four = swap(four, "rep", self.ranks, 4)
        return four

    def own(self, *others):
        ranks = self.ranks
        self.four = after(self.four, *others)
        mine = self.pieces[3].astype(FULL) + self.one[3:4].astype(FULL) + self.two[1:2].astype(FULL)
        mine = (mine + self.four.astype(FULL)).astype(LOW)
        if ranks > PARTS:
            others = [[j * PARTS + i for j in range(ranks // PARTS)] for i in range(PARTS)]
            mine = lax.psum(mine, "rep", axis_index_groups=others)
        self.mine = mine
        self.back = swap(mine, "rep", ranks, 4)
        return mine

    def spread(self, *others):
        self.back = after(self.back, *others)
        held = jnp.concatenate([self.mine, self.back])
        self.held = held
        self.wide = swap(held, "rep", self.ranks, 2)
        return held

    def done(self, *others):
        self.wide = after(self.wide, *others)
        held = jnp.concatenate([self.held, self.wide])
        return held, swap(held, "rep", self.ranks, 1)


class ShortSum(RepSum):
    def second(self, *others):
        one = after(self.one, *others)
        self.one = one
        six = (self.pieces[1][0:1].astype(FULL) + one[0:1].astype(FULL)).astype(LOW)
        two = (self.pieces[1][1:2].astype(FULL) + one[1:2].astype(FULL)).astype(LOW)
        four = (self.pieces[2].astype(FULL) + one[2:3].astype(FULL)).astype(LOW)
        self.terms = [swap(sent, "rep", self.ranks, mask) for sent, mask in ((six, 6), (two, 2), (four, 4))]
        return six, two, four

    def own(self, *others):
        ranks = self.ranks
        terms = after(self.terms, *others)
        mine = self.pieces[3].astype(FULL) + self.one[3:4].astype(FULL)
        mine = (mine + terms[0].astype(FULL) + terms[1].astype(FULL) + terms[2].astype(FULL)).astype(LOW)
        if ranks > PARTS:
            others = [[j * PARTS + i for j in range(ranks // PARTS)] for i in range(PARTS)]
            mine = lax.psum(mine, "rep", axis_index_groups=others)
        self.mine = mine
        self.back = [swap(mine, "rep", ranks, mask) for mask in (4, 2, 6)]
        return mine

    def done(self, *others):
        held = jnp.concatenate([self.mine, *after(self.back, *others)])
        return held, swap(held, "rep", self.ranks, 1)


def call(kernel, name, out_shape, *, grid=(1,), prefetch=0, in_specs, out_specs, scratch=(), micros=1, vmem=36, free=()):
    def lies(shape):
        return pltpu.HBM(shape.shape, shape.dtype)

    several = isinstance(out_shape, tuple)
    run = pl.pallas_call(
        kernel,
        name=name,
        out_shape=tuple(map(lies, out_shape)) if several else lies(out_shape),
        grid_spec=pltpu.PrefetchScalarGridSpec(
            num_scalar_prefetch=prefetch,
            grid=grid,
            in_specs=in_specs,
            out_specs=out_specs,
            scratch_shapes=list(scratch),
        ),
        compiler_params=pltpu.CompilerParams(vmem_limit_bytes=vmem << 20),
        cost_estimate=pl.CostEstimate(flops=int(micros * RATE), bytes_accessed=1 << 10, transcendentals=0),
    )

    def placed(*args):
        rest = [
            arg if spec is NEAR or i in free else pltpu.with_memory_space_constraint(arg, pltpu.HBM)
            for i, (arg, spec) in enumerate(zip(args[prefetch:], in_specs, strict=True))
        ]
        return run(*args[:prefetch], *rest)

    return placed


def whole(shape):
    return pl.BlockSpec(shape, lambda *_: (0,) * len(shape))


ANY = pl.BlockSpec(memory_space=pl.ANY)
NEAR = pl.BlockSpec(memory_space=pltpu.VMEM)


def shape_of(shape, kind=LOW):
    return jax.ShapeDtypeStruct(shape, kind)


def turn(rows, cosine, sine_val, sign):
    one, two = rows[0 : HD // 2, :], rows[HD // 2 : HD, :]
    sine_val = sine_val * sign
    return one * cosine - two * sine_val, two * cosine + one * sine_val


def assemble(rank, blocks, scratch):
    rows = blocks[0].shape[0]
    for k in range(GROUP):
        start = pl.multiple_of((rank ^ k) * rows, 16)
        scratch[pl.ds(start, rows), :] = blocks[k][...]


def pack_kernel(wk_ref, wv_ref, gains_ref, out_ref):
    kw, shard = wk_ref.shape
    out_ref[:, 0:kw] = wk_ref[...].T
    out_ref[:, kw : 2 * kw] = wv_ref[...].T
    gains = jnp.concatenate([gains_ref[...], jnp.zeros((LANES - 2, shard), FULL)], axis=0)
    out_ref[:, 2 * kw :] = gains.T.astype(LOW)


def flip_two_kernel(wg_ref, wu_ref, wgut_ref, wgu_ref):
    ff = wg_ref.shape[1]
    wgut_ref[0:ff, :] = wg_ref[...].T
    wgut_ref[ff:, :] = wu_ref[...].T
    wgu_ref[:, 0:ff] = wg_ref[...]
    wgu_ref[:, ff:] = wu_ref[...]


def flip_one_kernel(wdt_ref, wd_ref):
    wd_ref[...] = wdt_ref[...].T


def keys_values_kernel(ranks, tok_ref, b0, b1, b2, b3, cos_ref, sin_ref, norm_ref, kv_a, kv_b, gain_ref, w_ref):
    span = tok_ref.shape[2]
    kw2 = kv_a.shape[0]
    kw = kw2 // 2
    assemble(ranks[0], (b0, b1, b2, b3), w_ref)
    gains = w_ref[:, kw2:]
    gain_ref[...] = gains
    gain_one = gains[:, 0:1].astype(FULL)
    for s, out in enumerate((kv_a, kv_b)):
        x = tok_ref[s].astype(FULL)
        inverse = lax.rsqrt(jnp.mean(x * x, axis=0, keepdims=True) + NORM_EPS)
        norm = (x * inverse * gain_one).astype(LOW)
        norm_ref[:, s * span : (s + 1) * span] = norm
        kv = dot(w_ref[:, 0:kw2], norm, TN)
        for h in range(kw // HD):
            one, two = turn(kv[h * HD : (h + 1) * HD, :], cos_ref[s], sin_ref[s], 1.0)
            top = h * 2 * HD
            out[top : top + HD // 2, :] = one.astype(LOW)
            out[top + HD // 2 : top + HD, :] = two.astype(LOW)
            out[top + HD : top + 2 * HD, :] = kv[kw + h * HD : kw + (h + 1) * HD, :].astype(LOW)


def queries_kernel(ranks, norm_ref, b0, b1, b2, b3, cos_ref, sin_ref, q_ref, w_ref):
    width = b0.shape[1]
    span = cos_ref.shape[2]
    assemble(ranks[0], (b0, b1, b2, b3), w_ref)
    for s in range(2):
        part = slice(s * span, (s + 1) * span)
        query = dot(w_ref[...], norm_ref[:, part], TN)
        for h in range(width // HD):
            one, two = turn(query[h * HD : (h + 1) * HD, :], cos_ref[s], sin_ref[s], 1.0)
            q_ref[h * HD : h * HD + HD // 2, part] = (one * SCALE).astype(LOW)
            q_ref[h * HD + HD // 2 : (h + 1) * HD, part] = (two * SCALE).astype(LOW)


def beside(ref):
    return jnp.concatenate([ref[i : i + HD, :] for i in range(0, ref.shape[0], HD)], axis=1)


def attend_kernel(seq, ranks, order, starts, q_ref, b0, b1, b2, b3, p_ref, o_ref, bias_ref):
    span = q_ref.shape[1]
    per = q_ref.shape[0] // HD
    rank = ranks[0]

    @pl.when(pl.program_id(0) == 0)
    def _():
        query_pos = order[seq, rank] * span + lax.broadcasted_iota(jnp.int32, (span, span), 1)
        query_in = []
        for m in range(2):
            start = starts[seq, m]
            query_in.append((query_pos >= start) & (query_pos < start + PIECE))
        for k in range(GROUP):
            key_pos = order[seq, rank ^ k] * span + lax.broadcasted_iota(jnp.int32, (span, span), 0)
            allowed = key_pos <= query_pos
            for m in range(2):
                start = starts[seq, m]
                key_in = (key_pos >= start) & (key_pos < start + PIECE)
                allowed = allowed | (query_in[m] & key_in)
            bias_ref[k * span : (k + 1) * span, :] = jnp.where(allowed, 0.0, MASKED_SCORE)

    kv_t = jnp.concatenate([b0[...], b1[...], b2[...], b3[...]], axis=1)
    keys = kv_t.T[:, 0:HD]
    values_t = kv_t[HD : 2 * HD, :]
    bias = jnp.concatenate([bias_ref[...]] * per, axis=1)
    scores = dot(keys, beside(q_ref)) + bias
    peak = jnp.max(scores, axis=0, keepdims=True)
    exponent = jnp.exp(scores - peak)
    total = jnp.sum(exponent, axis=0, keepdims=True)
    probs = (exponent * (1.0 / total)).astype(LOW)
    p_ref[0] = probs
    mixed = dot(values_t, probs).astype(LOW)
    for i in range(per):
        o_ref[i * HD : (i + 1) * HD, :] = mixed[:, i * span : (i + 1) * span]


def middle_kernel(ranks, att_ref, b0, b1, b2, b3, tok_ref, gain_ref, mid_ref, x_ref, w_ref):
    assemble(ranks[0], (b0, b1, b2, b3), w_ref)
    middle = tok_ref[0].astype(FULL) + dot(w_ref[...], att_ref[...], TN)
    mid_ref[...] = middle
    inverse = lax.rsqrt(jnp.mean(middle * middle, axis=0, keepdims=True) + NORM_EPS)
    x_ref[...] = (middle * inverse * gain_ref[:, 1:2].astype(FULL)).astype(LOW)


def forward_back_step(x, cot, wgut_ref, wgu_ref, wdt_ref, wd_ref, hid_ref, gg_ref, gu_ref, both):
    ff = wd_ref.shape[0]
    gate_up = dot(wgut_ref[...], x)
    grad_hidden = dot(wd_ref[...], cot)
    gate, up = gate_up[0:ff, :], gate_up[ff:, :]
    sig = 1.0 / (1.0 + jnp.exp(-gate))
    swish = gate * sig
    hidden = (swish * up).astype(LOW)
    grad_gate = (grad_hidden * up * sig * (1.0 + gate * (1.0 - sig))).astype(LOW)
    grad_up = (grad_hidden * swish).astype(LOW)
    hid_ref[...] = hidden
    gg_ref[...] = grad_gate
    gu_ref[...] = grad_up
    both[0:ff, :] = grad_gate
    both[ff:, :] = grad_up
    return dot(wgu_ref[...], both[...]).astype(LOW), dot(wdt_ref[...], hidden).astype(LOW)


def own_block_kernel(x_a, x_b, cot_ref, wgut_ref, wgu_ref, wdt_ref, wd_ref, out_ref, grad_ref, hid_ref, gg_ref, gu_ref, held, both):
    s = pl.program_id(0)
    for i, x in enumerate((x_a, x_b)):

        @pl.when(s == i)
        def _(x=x):
            held[...] = x[...]

    grad_x, out = forward_back_step(
        held[...], cot_ref[0], wgut_ref, wgu_ref, wdt_ref, wd_ref, hid_ref.at[0], gg_ref.at[0], gu_ref.at[0], both
    )
    grad_ref[0] = grad_x
    out_ref[0] = out


def other_blocks_kernel(*refs):
    blocks = refs[0:6]
    weights = refs[6:10]
    fo_ref, so_ref, fg_ref, sg_ref, hid_ref, gg_ref, gu_ref, held, both, sem = refs[10:]
    k = pl.program_id(0)
    copies = [pltpu.make_async_copy(block, held.at[i], sem.at[i]) for i, block in enumerate(blocks)]

    @pl.when(k == 0)
    def _():
        for i in range(3):
            copies[i].start()
            copies[3 + i].start()

    for i in range(3):

        @pl.when(k == i)
        def _(i=i):
            copies[i].wait()
            copies[3 + i].wait()

    grad_x, out = forward_back_step(held[k], held[3 + k], *weights, hid_ref, gg_ref, gu_ref, both)

    @pl.when(k == 1)
    def _():
        fg_ref[...] = grad_x
        fo_ref[...] = out

    @pl.when(k != 1)
    def _():
        sg_ref[0] = grad_x
        so_ref[0] = out


def weight_kernel(kinds, ranks, *refs):
    blocks = refs[0 : 2 * GROUP]
    rights = refs[2 * GROUP : 2 * GROUP + 3 * kinds]
    outs = refs[2 * GROUP + 3 * kinds : 2 * GROUP + 3 * kinds + 4]
    left, right, acc, sem = refs[2 * GROUP + 3 * kinds + 4 :]
    span = left.shape[2] // GROUP
    kind = pl.program_id(0)
    lefts, loads = [], []
    for b, block in enumerate(blocks):
        s, k = divmod(b, GROUP)
        lefts.append(pltpu.make_async_copy(block, left.at[s, :, pl.ds(k * span, span)], sem.at[b]))
    for n in range(kinds):
        own, *others = rights[3 * n : 3 * n + 3]
        for s in range(2):
            for i, (source, part) in enumerate(((own.at[s], slice(0, span)), (others[s], slice(span, GROUP * span)))):
                at = sem.at[2 * GROUP + 4 * n + 2 * s + i]
                loads.append(pltpu.make_async_copy(source, right.at[n, s, :, part], at))

    @pl.when(kind == 0)
    def _():
        for copy in loads[0:2] + lefts[:GROUP] + loads[2:4] + lefts[GROUP:] + loads[4:]:
            copy.start()
        for copy in loads[0:2] + lefts[:GROUP]:
            copy.wait()

    for n in range(1, kinds):

        @pl.when(kind == n)
        def _(n=n):
            for copy in loads[4 * n : 4 * n + 4]:
                copy.wait()

    acc[...] = dot(left[0], right[kind, 0], NT)

    @pl.when(kind == 0)
    def _():
        for copy in loads[2:4] + lefts[GROUP:]:
            copy.wait()

    acc[...] += dot(left[1], right[kind, 1], NT)
    part = acc.shape[0] // PARTS
    places = [(outs[0], i) for i in range(4)] + [(outs[1], 0), (outs[1], 1), (outs[2], 0), (outs[3], 0)]
    for (out, i), slot in zip(places, SLOTS):
        start = pl.multiple_of((slot ^ ranks[1]) * part, 8)
        out[i] = acc[pl.ds(start, part), :].astype(LOW)


def branch_kernel(seq, ranks, mid_ref, cot_ref, e0, e1, e2, gain_ref, b0, b1, b2, b3, att_ref, gm_ref, gb_ref, do_ref, delta_ref, gain_out, w_ref):
    width, span = mid_ref.shape
    assemble(ranks[0], (b0, b1, b2, b3), w_ref)
    middle = mid_ref[...]
    grad = e0[0].astype(FULL) + e1[0].astype(FULL) + e2[...].astype(FULL)
    inverse = lax.rsqrt(jnp.mean(middle * middle, axis=0, keepdims=True) + NORM_EPS)
    scaled = grad * gain_ref[:, 1:2].astype(FULL)
    turned = jnp.mean(scaled * middle, axis=0, keepdims=True)
    grad_middle = cot_ref[seq].astype(FULL) + inverse * scaled - middle * (inverse * inverse * inverse * turned)
    gain_out[...] = dot(jnp.ones((8, span), LOW), (grad * middle * inverse).astype(LOW), NT)
    gm_ref[...] = grad_middle
    branch = grad_middle.astype(LOW)
    gb_ref[...] = branch
    grad_att = dot(w_ref[...], branch).astype(LOW)
    do_ref[...] = grad_att
    both = grad_att.astype(FULL) * att_ref[...].astype(FULL)
    heads = width // HD
    for h in range(heads):
        delta_ref[h : h + 1, :] = jnp.sum(both[h * HD : (h + 1) * HD, :], axis=0, keepdims=True)
    delta_ref[heads:, :] = jnp.zeros((delta_ref.shape[0] - heads, span), FULL)


def attend_back_kernel(seq, q_ref, b0, b1, b2, b3, p_ref, do_ref, delta_ref, cos_ref, sin_ref, gq_ref, own_ref, far_ref, send_ref):
    span = q_ref.shape[1]
    per = q_ref.shape[0] // HD
    h = pl.program_id(0)
    kv_t = jnp.concatenate([b0[...], b1[...], b2[...], b3[...]], axis=1)
    kv = kv_t.T
    query, out_grad = beside(q_ref), beside(do_ref)
    delta = jnp.concatenate([delta_ref[pl.ds(per * h + i, 1), :] for i in range(per)], axis=1)
    none = jnp.zeros(out_grad.shape, LOW)
    grad_probs = dot(kv, jnp.concatenate([none, out_grad], axis=0))
    grad_scores = (p_ref[0].astype(FULL) * (grad_probs - delta)).astype(LOW)
    grad_q = dot(kv_t[0:HD, :], grad_scores) * SCALE
    for i in range(per):
        one, two = turn(grad_q[:, i * span : (i + 1) * span], cos_ref[seq], sin_ref[seq], -1.0)
        gq_ref[i * HD : i * HD + HD // 2, :] = one.astype(LOW)
        gq_ref[i * HD + HD // 2 : (i + 1) * HD, :] = two.astype(LOW)
    keys = dot(query, grad_scores, NT).astype(LOW)
    values = dot(out_grad, p_ref[0], NT).astype(LOW)
    for k in range(GROUP):
        out = (own_ref, send_ref.at[0], far_ref, send_ref.at[1])[k]
        part = slice(k * span, (k + 1) * span)
        out[0:HD, :] = keys[:, part]
        out[HD:, :] = values[:, part]


def spread(ranks, acc, own_ref, far_ref, send_ref):
    part = acc.shape[1] // PARTS
    for k, out in enumerate((own_ref, send_ref.at[0], far_ref, send_ref.at[1])):
        for i, slot in enumerate(SLOTS):
            start = pl.multiple_of((slot ^ ranks[1]) * part, 8)
            out[i] = acc[ranks[0] ^ k, pl.ds(start, part), :].astype(LOW)


def query_weight_kernel(ranks, norm_ref, gq_a, gq_b, att_a, att_b, gb_a, gb_b, own_ref, far_ref, send_ref, acc):
    width, span = gq_a.shape
    shard = width // GROUP
    for b in range(GROUP):
        rows = slice(b * shard, (b + 1) * shard)
        acc[b, 0:shard, 0:width] = dot(norm_ref[rows, 0:span], gq_a[...], NT) + dot(norm_ref[rows, span:], gq_b[...], NT)
        acc[b, 0:shard, width:] = dot(att_a[rows, :], gb_a[...], NT) + dot(att_b[rows, :], gb_b[...], NT)
        acc[b, shard:, :] = jnp.zeros((acc.shape[1] - shard, acc.shape[2]), FULL)
    spread(ranks, acc, own_ref, far_ref, send_ref)


def key_weight_kernel(ranks, *refs):
    norm_ref, *terms = refs[0:7]
    cos_ref, sin_ref, part_ref, k0, k1, k2, k3, tok_ref, gm_a, gm_b, gain_a, gain_b = refs[7:19]
    own_ref, far_ref, send_ref, out_ref, gkv_ref, wkv_ref, acc = refs[19:]
    width = norm_ref.shape[0]
    span = gm_a.shape[1]
    shard = width // GROUP
    kw2 = gkv_ref.shape[0]
    kw = kw2 // 2
    assemble(ranks[0], (k0, k1, k2, k3), wkv_ref)
    gain_one = wkv_ref[:, kw2 : kw2 + 1].astype(FULL)
    grad_gain = None
    for s in range(2):
        e0, e1, e2 = terms[3 * s : 3 * s + 3]
        part = slice(s * span, (s + 1) * span)
        grad = e0[...].astype(FULL) + e1[0].astype(FULL) + e2[...].astype(FULL)
        for h in range(kw // HD):
            top = h * 2 * HD
            one, two = turn(grad[top : top + HD, :], cos_ref[s], sin_ref[s], -1.0)
            gkv_ref[h * HD : h * HD + HD // 2, part] = one.astype(LOW)
            gkv_ref[h * HD + HD // 2 : (h + 1) * HD, part] = two.astype(LOW)
            gkv_ref[kw + h * HD : kw + (h + 1) * HD, part] = grad[top + HD : top + 2 * HD, :].astype(LOW)
        grad_norm = part_ref[s] + dot(wkv_ref[:, 0:kw2], gkv_ref[:, part])
        x = tok_ref[s].astype(FULL)
        inverse = lax.rsqrt(jnp.mean(x * x, axis=0, keepdims=True) + NORM_EPS)
        scaled = grad_norm * gain_one
        turned = jnp.mean(scaled * x, axis=0, keepdims=True)
        out_ref[s] = (gm_a, gm_b)[s][...] + inverse * scaled - x * (inverse * inverse * inverse * turned)
        row = dot(jnp.ones((8, span), LOW), (grad_norm * x * inverse).astype(LOW), NT)
        grad_gain = row if grad_gain is None else grad_gain + row
    gains = jnp.concatenate([grad_gain[0:1, :], gain_a[0:1, :] + gain_b[0:1, :], jnp.zeros((6, width), FULL)], axis=0)
    for b in range(GROUP):
        rows = slice(b * shard, (b + 1) * shard)
        acc[b, 0:shard, :] = dot(norm_ref[rows, :], gkv_ref[...], NT)
        acc[b, shard:, :] = jnp.zeros((acc.shape[1] - shard, kw2), FULL)
        acc[b, shard : shard + 8, 0:shard] = gains[:, rows]
    spread(ranks, acc, own_ref, far_ref, send_ref)


def query_grad_kernel(ranks, gq_a, gq_b, q0, q1, q2, q3, out_ref, wq_ref):
    assemble(ranks[0], (q0, q1, q2, q3), wq_ref)
    out_ref[0] = dot(wq_ref[...], gq_a[...])
    out_ref[1] = dot(wq_ref[...], gq_b[...])


def place(slot):
    return ((slot >> 2) & 1) + ((slot >> 1) & 1) * 2


def gathered(ranks, pairs):
    for a in range(PARTS):
        slot = ranks[1] ^ a
        index = place(slot)
        for parity in range(2):

            @pl.when(slot % 2 == parity)
            def _(parity=parity, index=index, a=a):
                for pair in pairs:
                    part = pair[parity].shape[1]
                    pair[2][a * part : (a + 1) * part, :] = pair[parity][index].astype(FULL)


def forward_weights_kernel(ranks, even, odd, *outs):
    columns = outs[0].shape[1]
    for i, out in enumerate(outs):
        part = slice(i * columns, (i + 1) * columns)
        gathered(ranks, [(even.at[:, :, part], odd.at[:, :, part], out)])


def attention_done_kernel(ranks, even, odd, q_ref, o_ref, k_ref, v_ref, gain_ref, scratch):
    shard, width = q_ref.shape
    kw = k_ref.shape[0]
    gathered(ranks, [(even, odd, scratch)])
    q_ref[...] = scratch[0:shard, 0:width]
    o_ref[...] = scratch[0:shard, width : 2 * width]
    k_ref[...] = scratch[0:shard, 2 * width : 2 * width + kw].T
    v_ref[...] = scratch[0:shard, 2 * width + kw :].T
    gain_ref[...] = scratch[shard : shard + 8, 2 * width : 2 * width + shard]


def tables(places):
    half = HD // 2
    frequency = ROPE_BASE ** (-2.0 * jnp.arange(half, dtype=FULL) / HD)
    angles = places.astype(FULL)[:, None, :] * frequency[None, :, None]
    return jnp.cos(angles), jnp.sin(angles)


def body(
    tokens,
    w_query,
    w_key,
    w_value,
    w_out,
    w_gate,
    w_up,
    w_down,
    gain_attn,
    gain_mlp,
    span_order,
    piece_starts,
    cotangent,
):
    ranks = lax.axis_size("rep")
    rank_grp = lax.axis_index("grp")
    seq_count, span, width = tokens.shape
    shard = w_query.shape[0]
    kw = w_key.shape[1]
    kw2 = 2 * kw
    kv_heads = kw // HD
    per = width // kw
    ff = w_gate.shape[1]
    rows = seq_count * span
    length = GROUP * span
    place_of = jnp.stack([rank_grp, lax.axis_index("rep") % PARTS]).astype(jnp.int32)
    tok_t = jnp.swapaxes(tokens, 1, 2)
    cot_t = jnp.swapaxes(cotangent, 1, 2)
    wd_t = w_down.T
    act = whole((width, span))
    seqs = whole((seq_count, width, span))
    one_seq = lambda s: pl.BlockSpec((1, width, span), lambda *_: (s, 0, 0))
    table = whole((seq_count, HD // 2, span))
    gain_spec = whole((width, LANES))
    head = pl.BlockSpec((2 * HD, span), lambda h, *_: (h, 0))
    probs_spec = pl.BlockSpec((1, length, per * span), lambda h, *_: (h, 0, 0))
    q_spec = lambda s: pl.BlockSpec((per * HD, span), lambda h, *_: (h, s))
    per_head = pl.BlockSpec((per * HD, span), lambda h, *_: (h, 0))

    kv_shard = call(
        pack_kernel,
        "pack",
        shape_of((shard, kw2 + LANES)),
        in_specs=[whole((kw, shard))] * 2 + [whole((2, shard))],
        out_specs=whole((shard, kw2 + LANES)),
        micros=2,
    )(w_key.T, w_value.T, jnp.stack([gain_attn, gain_mlp]).astype(FULL))
    kv_flight = Blocks(kv_shard)
    q_flight = Blocks(w_query, kv_shard)
    own_span = lax.dynamic_slice(span_order, (0, rank_grp), (seq_count, 1))
    places = own_span * span + jnp.arange(span, dtype=jnp.int32)[None, :]
    cos_cols, sin_cols = tables(places)
    wgut, wgu = call(
        flip_two_kernel,
        "flip_two",
        (shape_of((2 * ff, width)), shape_of((width, 2 * ff))),
        in_specs=[whole((width, ff))] * 2,
        out_specs=(whole((2 * ff, width)), whole((width, 2 * ff))),
        micros=4,
    )(after(w_gate, kv_flight.sent), w_up)
    wd = call(
        flip_one_kernel,
        "flip_one",
        shape_of((ff, width)),
        in_specs=[whole((width, ff))],
        out_specs=whole((ff, width)),
        micros=2,
    )(after(wd_t, wgut))
    kv_blocks = kv_flight.finish(wd)
    norm_low, kv_a, kv_b, gain_cols = call(
        keys_values_kernel,
        "keys_values",
        (shape_of((width, rows)), shape_of((kw2, span)), shape_of((kw2, span)), shape_of((width, LANES))),
        free=range(1, 5),
            prefetch=1,
        in_specs=[NEAR] + [whole(kv_shard.shape)] * 4 + [table, table],
        out_specs=(whole((width, rows)), whole((kw2, span)), whole((kw2, span)), gain_spec),
        scratch=[pltpu.VMEM((width, kw2 + LANES), LOW)],
        micros=4.3,
    )(place_of, tok_t, *kv_blocks, cos_cols, sin_cols)
    kv_flight = [Blocks(kv_a), None]
    q_blocks = q_flight.finish(norm_low)
    queries = call(
        queries_kernel,
        "queries",
        shape_of((width, rows)),
        free=range(1, 5),
            prefetch=1,
        in_specs=[whole((width, rows))] + [whole((shard, width))] * 4 + [table, table],
        out_specs=whole((width, rows)),
        scratch=[pltpu.VMEM((width, width), LOW)],
        micros=0.1,
    )(place_of, norm_low, *q_blocks, cos_cols, sin_cols)

    o_flight = Blocks(w_out, kv_a)
    kv_flight[1] = Blocks(kv_b, *q_blocks)
    cot_flight = [Blocks(cot_t[0], queries), None]
    cot_blocks = [None, None]
    kv_all = [kv_flight[0].finish(queries), None]

    def attend_of(s, query):
        return call(
            functools.partial(attend_kernel, s),
            "attend",
            (shape_of((kv_heads, length, per * span)), shape_of((width, span))),
            free=range(1, 5),
            prefetch=3,
            grid=(kv_heads,),
            in_specs=[q_spec(s)] + [head] * 4,
            out_specs=(probs_spec, per_head),
            scratch=[pltpu.VMEM((length, span), FULL)],
            micros=0.1,
        )(place_of, span_order, piece_starts, query, *kv_all[s])

    def middle_of(s, att):
        return call(
            middle_kernel,
            "middle",
            (shape_of((width, span), FULL), shape_of((width, span))),
            free=range(1, 5),
            prefetch=1,
            in_specs=[act] + [whole((shard, width))] * 4 + [one_seq(s), gain_spec],
            out_specs=(act, act),
            scratch=[pltpu.VMEM((width, width), LOW)],
            micros=3,
        )(place_of, att, *o_blocks, tok_t, gain_cols)

    probs_a, att_a = attend_of(0, queries)
    o_blocks = o_flight.finish(att_a)
    kv_all[1] = kv_flight[1].finish(att_a)
    middle_a, x_a = middle_of(0, att_a)
    x_flight = [Blocks(x_a), None]
    cot_flight[1] = Blocks(cot_t[1], x_flight[0].sent, x_a)
    probs_b, att_b = attend_of(1, after(queries, x_a))
    cot_flight[0].arrive(att_b)
    middle_b, x_b = middle_of(1, after(att_b, *cot_flight[0].ready))
    x_flight[1] = Blocks(x_b)
    x_flight[0].arrive(middle_b)
    cot_blocks[0] = cot_flight[0].finish(middle_b)
    stats, attended, middles = (probs_a, probs_b), (att_a, att_b), (middle_a, middle_b)

    each = pl.BlockSpec((1, width, span), lambda s, *_: (s, 0, 0))
    each_ff = pl.BlockSpec((1, ff, span), lambda s, *_: (s, 0, 0))
    two = shape_of((seq_count, width, span))
    two_ff = shape_of((seq_count, ff, span))
    own_out, own_grad, own_hid, own_gg, own_gu = call(
        own_block_kernel,
        "own_blocks",
        (two, two, two_ff, two_ff, two_ff),
        grid=(seq_count,),
        in_specs=[act, act, each] + [NEAR] * 4,
        out_specs=(each, each, each_ff, each_ff, each_ff),
        scratch=[pltpu.VMEM((width, span), LOW), pltpu.VMEM((2 * ff, span), LOW)],
        micros=8,
    )(after(x_a, *x_flight[0].ready, *cot_blocks[0]), x_b, cot_t, wgut, wgu, wd_t, wd)
    x_blocks = [x_flight[0].finish(own_out), None]
    cot_flight[1].arrive(own_out)

    def other_blocks(s, *others):
        half = pl.BlockSpec((1, width, span), lambda k, *_: (k // 2, 0, 0))
        per_block = pl.BlockSpec((ff, span), lambda k, *_: (0, k))
        act_shape, half_shape, ff_shape = shape_of((width, span)), shape_of((2, width, span)), shape_of((ff, 3 * span))
        return call(
            other_blocks_kernel,
            "other_blocks",
            (act_shape, half_shape, act_shape, half_shape, ff_shape, ff_shape, ff_shape),
            free=range(6),
            grid=(GROUP - 1,),
            in_specs=[ANY] * 6 + [NEAR] * 4,
            out_specs=(act, half, act, half) + (per_block,) * 3,
            scratch=[
                pltpu.VMEM((6, width, span), LOW),
                pltpu.VMEM((2 * ff, span), LOW),
                pltpu.SemaphoreType.DMA((6,)),
            ],
            micros=12,
        )(after(x_blocks[s][1], *others), *x_blocks[s][2:], *cot_blocks[s][1:], wgut, wgu, wd_t, wd)

    fo_a, so_a, fg_a, sg_a, hid_a, gg_a, gu_a = other_blocks(0, *cot_flight[1].ready)
    grad_a = Terms(own_grad[0], fg_a, sg_a)
    out_a = Terms(own_out[0], fo_a, so_a)
    x_flight[1].arrive(fg_a)
    x_blocks[1] = x_flight[1].finish()
    cot_blocks[1] = cot_flight[1].finish(fg_a)
    fo_b, so_b, fg_b, sg_b, hid_b, gg_b, gu_b = other_blocks(1, fg_a)
    grad_b = Terms(own_grad[1], fg_b, sg_b)
    out_b = Terms(own_out[1], fo_b, so_b)
    stage = (grad_a.cross(fg_b), out_a.cross(fg_b))
    grads = (grad_a, grad_b)

    part = width // PARTS

    def sums(name, blocks, kinds, *others):
        count = len(kinds)
        columns = count * ff
        pieces = call(
            functools.partial(weight_kernel, count),
            name,
            tuple(shape_of((n, part, columns)) for n in (4, 2, 1, 1)),
            prefetch=1,
            grid=(count,),
            in_specs=[ANY] * (2 * GROUP + 3 * count),
            out_specs=tuple(pl.BlockSpec((n, part, ff), lambda m, *_: (0, 0, m)) for n in (4, 2, 1, 1)),
            scratch=[
                pltpu.VMEM((2, width, length), LOW),
                pltpu.VMEM((count, 2, ff, length), LOW),
                pltpu.VMEM((width, ff), FULL),
                pltpu.SemaphoreType.DMA((2 * GROUP + 4 * count,)),
            ],
            micros=2 + 6 * count,
        )(place_of, after(blocks[0], *others), *blocks[1:], *sum(kinds, ()))
        return RepSum(pieces, ranks)

    x_all = x_blocks[0] + x_blocks[1]
    down_sum = sums("down_weights", cot_blocks[0] + cot_blocks[1], [(own_hid, hid_a, hid_b)], *stage)
    done = down_sum.pieces[0]
    stage = (grad_b.cross(done), out_b.beside, done)
    up_sum = sums("gate_up_weights", x_all, [(own_gg, gg_a, gg_b), (own_gu, gu_a, gu_b)], *stage)
    done = up_sum.pieces[0]
    stage = (grad_a.across, out_b.cross(done), down_sum.second(done), out_a.across, done)

    def branch_of(s, *others):
        _, beside_term, across_term = grads[s].all()
        first = whole((1, width, span))
        return call(
            functools.partial(branch_kernel, s),
            "branch",
            (
                shape_of((width, span), FULL),
                shape_of((width, span)),
                shape_of((width, span)),
                shape_of((16, span), FULL),
                shape_of((8, width), FULL),
            ),
            free=(3, 4),
            prefetch=1,
            in_specs=[NEAR, NEAR, one_seq(s), first, act, NEAR] + [NEAR] * 5,
            out_specs=(act, act, act, whole((16, span)), whole((8, width))),
            scratch=[pltpu.VMEM((width, width), LOW)],
            micros=4,
        )(place_of, middles[s], cot_t, own_grad, beside_term, after(across_term, *others), gain_cols, *o_blocks, attended[s])

    def attend_back_of(s, out_grad, delta):
        halves = pl.BlockSpec((2, 2 * HD, span), lambda h, *_: (0, h, 0))
        grad_q, *kv_parts = call(
            functools.partial(attend_back_kernel, s),
            "attend_back",
            (shape_of((width, span)), shape_of((kw2, span)), shape_of((kw2, span)), shape_of((2, kw2, span))),
            grid=(kv_heads,),
            in_specs=[q_spec(s)] + [head] * 4 + [probs_spec, per_head, whole((16, span)), table, table],
            out_specs=(per_head, head, head, halves),
            micros=11,
        )(queries, *kv_all[s], stats[s], out_grad, delta, cos_cols, sin_cols)
        return grad_q, Terms(*kv_parts)

    mid_a, branch_a, dout_a, delta_a, gain_a = branch_of(0, *stage)
    stage = (down_sum.third(branch_a), grad_b.across)
    gq_a, kv_grad_a = attend_back_of(0, after(dout_a, *stage), delta_a)
    stage = (out_b.across, down_sum.own(gq_a))
    mid_b, branch_b, dout_b, delta_b, gain_b = branch_of(1, *stage)
    stage = (kv_grad_a.cross(branch_b), up_sum.second(branch_b))
    gq_b, kv_grad_b = attend_back_of(1, after(dout_b, *stage), delta_b)
    stage = (down_sum.spread(gq_b), kv_grad_a.across)

    grown = shard + GAIN_ROWS
    piece = grown // PARTS
    spread_out = lambda columns: (shape_of((PARTS, piece, columns)),) * 2 + (shape_of((2, PARTS, piece, columns)),)
    spread_spec = lambda columns: (whole((PARTS, piece, columns)),) * 2 + (whole((2, PARTS, piece, columns)),)
    query_parts = call(
        query_weight_kernel,
        "query_weights",
        spread_out(2 * width),
        prefetch=1,
        in_specs=[NEAR, NEAR, act] + [NEAR] * 4,
        out_specs=spread_spec(2 * width),
        scratch=[pltpu.VMEM((GROUP, grown, 2 * width), FULL)],
        micros=8,
    )(place_of, norm_low, gq_a, after(gq_b, *stage), *attended, branch_a, branch_b)
    done = query_parts[0]
    stage = (kv_grad_b.cross(done), up_sum.third(done))
    query_terms = Terms(*query_parts, *stage)
    grad_part = call(
        query_grad_kernel,
        "query_grad",
        shape_of((seq_count, width, span), FULL),
        prefetch=1,
        in_specs=[NEAR, act] + [NEAR] * 4,
        out_specs=seqs,
        scratch=[pltpu.VMEM((width, width), LOW)],
        micros=4,
    )(place_of, gq_a, after(gq_b, *stage), *q_blocks)
    stage = (query_terms.cross(grad_part),)
    stage = (*stage, kv_grad_b.across)

    def owned(terms):
        own, beside_term, across = terms.all()
        cuts = (slice(0, 4), slice(4, 6), slice(6, 7), slice(7, 8))
        return [three((own[c], beside_term[:, c], across[c])) for c in cuts]

    first = whole((1, kw2, span))
    terms = []
    for term in (kv_grad_a, kv_grad_b):
        terms += term.all()
    *key_parts, grad_tokens = call(
        key_weight_kernel,
        "key_weights",
        spread_out(kw2) + (shape_of((seq_count, width, span), FULL),),
        free=range(1, 7),
            prefetch=1,
        in_specs=[NEAR]
        + [whole((kw2, span)), first, whole((kw2, span))] * 2
        + [table, table, seqs]
        + [NEAR] * 7
        + [whole((8, width))] * 2,
        out_specs=spread_spec(kw2) + (seqs,),
        scratch=[
            pltpu.VMEM((kw2, rows), LOW),
            pltpu.VMEM((width, kw2 + LANES), LOW),
            pltpu.VMEM((GROUP, grown, kw2), FULL),
        ],
        micros=10,
    )(
        place_of,
        norm_low,
        after(terms[0], *stage),
        *terms[1:],
        cos_cols,
        sin_cols,
        grad_part,
        *kv_blocks,
        tok_t,
        mid_a,
        mid_b,
        gain_a,
        gain_b,
    )
    down_pair = down_sum.done(grad_tokens)
    stage = (up_sum.own(grad_tokens), down_pair[0])
    key_terms = Terms(*key_parts)

    def finished(name, kernel, pair, outs, *others):
        columns = pair[0].shape[2]
        return call(
            kernel,
            name,
            (shape_of((width, ff), FULL),) * outs,
            free=range(2),
            prefetch=1,
            in_specs=[whole((4, part, columns))] * 2,
            out_specs=(whole((width, ff)),) * outs,
            micros=3.5 * outs,
        )(place_of, after(pair[0], *others), pair[1])

    block_out = jnp.stack(
        [middle + three(term.all()) for middle, term in zip(after(middles, *stage), (out_a, out_b))]
    )
    key_terms.cross(block_out)
    pieces = []
    for query_piece, key_piece in zip(owned(query_terms), owned(key_terms)):
        joint = jnp.concatenate([query_piece, key_piece], axis=-1)
        pieces.append(joint.astype(LOW))
    query_sum = ShortSum(pieces, ranks)

    up_sum.spread(*pieces)
    (grad_down,) = finished("down_done", forward_weights_kernel, down_pair, 1, *pieces)
    step = query_sum.second(grad_down)
    up_pair = up_sum.done(*step)
    step = query_sum.own(up_pair[0])
    query_pair = query_sum.done(step, up_pair[1])
    grad_gate, grad_up = finished("gate_up_done", forward_weights_kernel, up_pair, 2, query_pair[0])
    grad_down = grad_down.T
    grad_query, grad_out, grad_key, grad_value, grad_gains = call(
        attention_done_kernel,
        "attention_done",
        (shape_of((shard, width), FULL),) * 2 + (shape_of((kw, shard), FULL),) * 2 + (shape_of((8, shard), FULL),),
        free=range(2),
            prefetch=1,
        in_specs=[whole((4, piece, 2 * width + kw2))] * 2,
        out_specs=(whole((shard, width)),) * 2 + (whole((kw, shard)),) * 2 + (whole((8, shard)),),
        scratch=[pltpu.VMEM((grown, 2 * width + kw2), FULL)],
        micros=5,
    )(place_of, *query_pair)
    return (
        jnp.swapaxes(block_out, 1, 2),
        jnp.swapaxes(grad_tokens, 1, 2),
        grad_query,
        grad_key.T,
        grad_value.T,
        grad_out,
        grad_gate,
        grad_up,
        grad_down,
        grad_gains[0],
        grad_gains[1],
    )


def solution(mesh):
    placed = (
        P("rep", "grp", None),
        P("grp", None),
        P("grp", None),
        P("grp", None),
        P("grp", None),
        P(None, "grp"),
        P(None, "grp"),
        P("grp", None),
        P("grp"),
        P("grp"),
        P("rep", None),
        P("rep", None),
        P("rep", "grp", None),
    )
    return jax.shard_map(
        body,
        mesh=mesh,
        in_specs=placed,
        out_specs=(
            P("rep", "grp", None),
            P("rep", "grp", None),
            P("grp", None),
            P("grp", None),
            P("grp", None),
            P("grp", None),
            P(None, "grp"),
            P(None, "grp"),
            P("grp", None),
            P("grp"),
            P("grp"),
        ),
        check_vma=False,
    )
```

```python
import functools

import jax
import jax.numpy as jnp
from jax import lax
from jax.experimental import pallas as pl
from jax.experimental.pallas import tpu as pltpu
from jax.sharding import PartitionSpec as P

HD = 64
PIECE = 256
LANES = 128
GROUP = 4
PARTS = 8
GAIN_ROWS = 16
RATE = 2.0e9
SLOTS = (7, 3, 5, 1, 6, 2, 4, 0)


NORM_EPS = 1e-05
ROPE_BASE = 10000.0
MASKED_SCORE = -1e30
SCALE = HD ** (-0.5)

LOW = jnp.bfloat16
FULL = jnp.float32
NN = (((1,), (0,)), ((), ()))
NT = (((1,), (1,)), ((), ()))
TN = (((0,), (0,)), ((), ()))


def dot(left_mat, right_mat, form=NN):
    return lax.dot_general(left_mat, right_mat, form, preferred_element_type=FULL)


def swap(values, axis, count, mask):
    return lax.ppermute(values, axis, [(i, i ^ mask) for i in range(count)])


def after(values, *others):
    return lax.optimization_barrier((values,) + others)[0] if others else values


class Blocks:
    def __init__(self, own, *others):
        self.own = own
        sent = after(own, *others)
        self.across = swap(sent, "grp", GROUP, 2)
        self.sent = sent

    def arrive(self, *others):
        pair = after((self.sent, self.across), *others)
        self.ready = pair
        self.core = swap(pair[0], "grp", GROUP, 1), swap(pair[1], "grp", GROUP, 1)

    def finish(self, *others):
        if not hasattr(self, "core"):
            self.arrive(*others)
        beside, corner = after(self.core, *others)
        return self.own, beside, self.across, corner


class Terms:
    def __init__(self, own, far, send, *others):
        self.own, self.far = own, far
        self.beside = swap(after(send, *others), "grp", GROUP, 1)

    def cross(self, *others):
        far, beside = after((self.far, self.beside), *others)
        across = (far.astype(FULL) + beside[1].astype(FULL)).astype(LOW)
        self.sent = across
        self.across = swap(across, "grp", GROUP, 2)
        return across

    def all(self):
        return self.own, self.beside, self.across


def three(terms):
    return terms[0].astype(FULL) + terms[1][0].astype(FULL) + terms[2].astype(FULL)


class RepSum:
    def __init__(self, pieces, ranks):
        self.pieces, self.ranks = pieces, ranks
        self.one = swap(pieces[0], "rep", ranks, 1)

    def second(self, *others):
        self.one = after(self.one, *others)
        two = (self.pieces[1].astype(FULL) + self.one[0:2].astype(FULL)).astype(LOW)
        self.held_two = two
        self.two = swap(two, "rep", self.ranks, 2)
        return two

    def third(self, *others):
        self.two = after(self.two, *others)
        four = self.pieces[2].astype(FULL) + self.one[2:3].astype(FULL) + self.two[0:1].astype(FULL)
        four = four.astype(LOW)
        self.four = swap(four, "rep", self.ranks, 4)
        return four

    def own(self, *others):
        ranks = self.ranks
        self.four = after(self.four, *others)
        mine = self.pieces[3].astype(FULL) + self.one[3:4].astype(FULL) + self.two[1:2].astype(FULL)
        mine = (mine + self.four.astype(FULL)).astype(LOW)
        if ranks > PARTS:
            others = [[j * PARTS + i for j in range(ranks // PARTS)] for i in range(PARTS)]
            mine = lax.psum(mine, "rep", axis_index_groups=others)
        self.mine = mine
        self.back = swap(mine, "rep", ranks, 4)
        return mine

    def spread(self, *others):
        self.back = after(self.back, *others)
        held = jnp.concatenate([self.mine, self.back])
        self.held = held
        self.wide = swap(held, "rep", self.ranks, 2)
        return held

    def done(self, *others):
        self.wide = after(self.wide, *others)
        held = jnp.concatenate([self.held, self.wide])
        return held, swap(held, "rep", self.ranks, 1)


class ShortSum(RepSum):
    def second(self, *others):
        one = after(self.one, *others)
        self.one = one
        six = (self.pieces[1][0:1].astype(FULL) + one[0:1].astype(FULL)).astype(LOW)
        two = (self.pieces[1][1:2].astype(FULL) + one[1:2].astype(FULL)).astype(LOW)
        four = (self.pieces[2].astype(FULL) + one[2:3].astype(FULL)).astype(LOW)
        self.terms = [swap(sent, "rep", self.ranks, mask) for sent, mask in ((six, 6), (two, 2), (four, 4))]
        return six, two, four

    def own(self, *others):
        ranks = self.ranks
        terms = after(self.terms, *others)
        mine = self.pieces[3].astype(FULL) + self.one[3:4].astype(FULL)
        mine = (mine + terms[0].astype(FULL) + terms[1].astype(FULL) + terms[2].astype(FULL)).astype(LOW)
        if ranks > PARTS:
            others = [[j * PARTS + i for j in range(ranks // PARTS)] for i in range(PARTS)]
            mine = lax.psum(mine, "rep", axis_index_groups=others)
        self.mine = mine
        self.back = [swap(mine, "rep", ranks, mask) for mask in (4, 2, 6)]
        return mine

    def done(self, *others):
        held = jnp.concatenate([self.mine, *after(self.back, *others)])
        return held, swap(held, "rep", self.ranks, 1)


def call(kernel, name, out_shape, *, grid=(1,), prefetch=0, in_specs, out_specs, scratch=(), micros=1, vmem=36, free=()):
    def lies(shape):
        return pltpu.HBM(shape.shape, shape.dtype)

    several = isinstance(out_shape, tuple)
    run = pl.pallas_call(
        kernel,
        name=name,
        out_shape=tuple(map(lies, out_shape)) if several else lies(out_shape),
        grid_spec=pltpu.PrefetchScalarGridSpec(
            num_scalar_prefetch=prefetch,
            grid=grid,
            in_specs=in_specs,
            out_specs=out_specs,
            scratch_shapes=list(scratch),
        ),
        compiler_params=pltpu.CompilerParams(vmem_limit_bytes=vmem << 20),
        cost_estimate=pl.CostEstimate(flops=int(micros * RATE), bytes_accessed=1 << 10, transcendentals=0),
    )

    def placed(*args):
        rest = [
            arg if spec is NEAR or i in free else pltpu.with_memory_space_constraint(arg, pltpu.HBM)
            for i, (arg, spec) in enumerate(zip(args[prefetch:], in_specs, strict=True))
        ]
        return run(*args[:prefetch], *rest)

    return placed


def whole(shape):
    return pl.BlockSpec(shape, lambda *_: (0,) * len(shape))


ANY = pl.BlockSpec(memory_space=pl.ANY)
NEAR = pl.BlockSpec(memory_space=pltpu.VMEM)


def shape_of(shape, kind=LOW):
    return jax.ShapeDtypeStruct(shape, kind)


def turn(rows, cosine, sine_val, sign):
    one, two = rows[0 : HD // 2, :], rows[HD // 2 : HD, :]
    sine_val = sine_val * sign
    return one * cosine - two * sine_val, two * cosine + one * sine_val


def assemble(rank, blocks, scratch):
    rows = blocks[0].shape[0]
    for k in range(GROUP):
        start = pl.multiple_of((rank ^ k) * rows, 16)
        scratch[pl.ds(start, rows), :] = blocks[k][...]


def pack_kernel(wk_ref, wv_ref, gains_ref, out_ref):
    kw, shard = wk_ref.shape
    out_ref[:, 0:kw] = wk_ref[...].T
    out_ref[:, kw : 2 * kw] = wv_ref[...].T
    gains = jnp.concatenate([gains_ref[...], jnp.zeros((LANES - 2, shard), FULL)], axis=0)
    out_ref[:, 2 * kw :] = gains.T.astype(LOW)


def flip_two_kernel(wg_ref, wu_ref, wgut_ref, wgu_ref):
    ff = wg_ref.shape[1]
    wgut_ref[0:ff, :] = wg_ref[...].T
    wgut_ref[ff:, :] = wu_ref[...].T
    wgu_ref[:, 0:ff] = wg_ref[...]
    wgu_ref[:, ff:] = wu_ref[...]


def flip_one_kernel(wdt_ref, wd_ref):
    wd_ref[...] = wdt_ref[...].T


def keys_values_kernel(ranks, tok_ref, b0, b1, b2, b3, cos_ref, sin_ref, norm_ref, kv_a, kv_b, gain_ref, w_ref):
    span = tok_ref.shape[2]
    kw2 = kv_a.shape[0]
    kw = kw2 // 2
    assemble(ranks[0], (b0, b1, b2, b3), w_ref)
    gains = w_ref[:, kw2:]
    gain_ref[...] = gains
    gain_one = gains[:, 0:1].astype(FULL)
    for s, out in enumerate((kv_a, kv_b)):
        x = tok_ref[s].astype(FULL)
        inverse = lax.rsqrt(jnp.mean(x * x, axis=0, keepdims=True) + NORM_EPS)
        norm = (x * inverse * gain_one).astype(LOW)
        norm_ref[:, s * span : (s + 1) * span] = norm
        kv = dot(w_ref[:, 0:kw2], norm, TN)
        for h in range(kw // HD):
            one, two = turn(kv[h * HD : (h + 1) * HD, :], cos_ref[s], sin_ref[s], 1.0)
            top = h * 2 * HD
            out[top : top + HD // 2, :] = one.astype(LOW)
            out[top + HD // 2 : top + HD, :] = two.astype(LOW)
            out[top + HD : top + 2 * HD, :] = kv[kw + h * HD : kw + (h + 1) * HD, :].astype(LOW)


def queries_kernel(ranks, norm_ref, b0, b1, b2, b3, cos_ref, sin_ref, q_ref, w_ref):
    width = b0.shape[1]
    span = cos_ref.shape[2]
    assemble(ranks[0], (b0, b1, b2, b3), w_ref)
    for s in range(2):
        part = slice(s * span, (s + 1) * span)
        query = dot(w_ref[...], norm_ref[:, part], TN)
        for h in range(width // HD):
            one, two = turn(query[h * HD : (h + 1) * HD, :], cos_ref[s], sin_ref[s], 1.0)
            q_ref[h * HD : h * HD + HD // 2, part] = (one * SCALE).astype(LOW)
            q_ref[h * HD + HD // 2 : (h + 1) * HD, part] = (two * SCALE).astype(LOW)


def beside(ref):
    return jnp.concatenate([ref[i : i + HD, :] for i in range(0, ref.shape[0], HD)], axis=1)


def attend_kernel(seq, ranks, order, starts, q_ref, b0, b1, b2, b3, p_ref, o_ref, bias_ref):
    span = q_ref.shape[1]
    per = q_ref.shape[0] // HD
    rank = ranks[0]

    @pl.when(pl.program_id(0) == 0)
    def _():
        query_pos = order[seq, rank] * span + lax.broadcasted_iota(jnp.int32, (span, span), 1)
        query_in = []
        for m in range(2):
            start = starts[seq, m]
            query_in.append((query_pos >= start) & (query_pos < start + PIECE))
        for k in range(GROUP):
            key_pos = order[seq, rank ^ k] * span + lax.broadcasted_iota(jnp.int32, (span, span), 0)
            allowed = key_pos <= query_pos
            for m in range(2):
                start = starts[seq, m]
                key_in = (key_pos >= start) & (key_pos < start + PIECE)
                allowed = allowed | (query_in[m] & key_in)
            bias_ref[k * span : (k + 1) * span, :] = jnp.where(allowed, 0.0, MASKED_SCORE)

    kv_t = jnp.concatenate([b0[...], b1[...], b2[...], b3[...]], axis=1)
    keys = kv_t.T[:, 0:HD]
    values_t = kv_t[HD : 2 * HD, :]
    bias = jnp.concatenate([bias_ref[...]] * per, axis=1)
    scores = dot(keys, beside(q_ref)) + bias
    peak = jnp.max(scores, axis=0, keepdims=True)
    exponent = jnp.exp(scores - peak)
    total = jnp.sum(exponent, axis=0, keepdims=True)
    probs = (exponent * (1.0 / total)).astype(LOW)
    p_ref[0] = probs
    mixed = dot(values_t, probs).astype(LOW)
    for i in range(per):
        o_ref[i * HD : (i + 1) * HD, :] = mixed[:, i * span : (i + 1) * span]


def middle_kernel(ranks, att_ref, b0, b1, b2, b3, tok_ref, gain_ref, mid_ref, x_ref, w_ref):
    assemble(ranks[0], (b0, b1, b2, b3), w_ref)
    middle = tok_ref[0].astype(FULL) + dot(w_ref[...], att_ref[...], TN)
    mid_ref[...] = middle
    inverse = lax.rsqrt(jnp.mean(middle * middle, axis=0, keepdims=True) + NORM_EPS)
    x_ref[...] = (middle * inverse * gain_ref[:, 1:2].astype(FULL)).astype(LOW)


def forward_back_step(x, cot, wgut_ref, wgu_ref, wdt_ref, wd_ref, hid_ref, gg_ref, gu_ref, both):
    ff = wd_ref.shape[0]
    gate_up = dot(wgut_ref[...], x)
    grad_hidden = dot(wd_ref[...], cot)
    gate, up = gate_up[0:ff, :], gate_up[ff:, :]
    sig = 1.0 / (1.0 + jnp.exp(-gate))
    swish = gate * sig
    hidden = (swish * up).astype(LOW)
    grad_gate = (grad_hidden * up * sig * (1.0 + gate * (1.0 - sig))).astype(LOW)
    grad_up = (grad_hidden * swish).astype(LOW)
    hid_ref[...] = hidden
    gg_ref[...] = grad_gate
    gu_ref[...] = grad_up
    both[0:ff, :] = grad_gate
    both[ff:, :] = grad_up
    return dot(wgu_ref[...], both[...]).astype(LOW), dot(wdt_ref[...], hidden).astype(LOW)


def own_block_kernel(x_a, x_b, cot_ref, wgut_ref, wgu_ref, wdt_ref, wd_ref, out_ref, grad_ref, hid_ref, gg_ref, gu_ref, held, both):
    s = pl.program_id(0)
    for i, x in enumerate((x_a, x_b)):

        @pl.when(s == i)
        def _(x=x):
            held[...] = x[...]

    grad_x, out = forward_back_step(
        held[...], cot_ref[0], wgut_ref, wgu_ref, wdt_ref, wd_ref, hid_ref.at[0], gg_ref.at[0], gu_ref.at[0], both
    )
    grad_ref[0] = grad_x
    out_ref[0] = out


def other_blocks_kernel(*refs):
    blocks = refs[0:6]
    weights = refs[6:10]
    fo_ref, so_ref, fg_ref, sg_ref, hid_ref, gg_ref, gu_ref, held, both, sem = refs[10:]
    k = pl.program_id(0)
    copies = [pltpu.make_async_copy(block, held.at[i], sem.at[i]) for i, block in enumerate(blocks)]

    @pl.when(k == 0)
    def _():
        for i in range(3):
            copies[i].start()
            copies[3 + i].start()

    for i in range(3):

        @pl.when(k == i)
        def _(i=i):
            copies[i].wait()
            copies[3 + i].wait()

    grad_x, out = forward_back_step(held[k], held[3 + k], *weights, hid_ref, gg_ref, gu_ref, both)

    @pl.when(k == 1)
    def _():
        fg_ref[...] = grad_x
        fo_ref[...] = out

    @pl.when(k != 1)
    def _():
        sg_ref[0] = grad_x
        so_ref[0] = out


def weight_kernel(kinds, ranks, *refs):
    blocks = refs[0 : 2 * GROUP]
    rights = refs[2 * GROUP : 2 * GROUP + 3 * kinds]
    outs = refs[2 * GROUP + 3 * kinds : 2 * GROUP + 3 * kinds + 4]
    left, right, acc, sem = refs[2 * GROUP + 3 * kinds + 4 :]
    span = left.shape[2] // GROUP
    kind = pl.program_id(0)
    lefts, loads = [], []
    for b, block in enumerate(blocks):
        s, k = divmod(b, GROUP)
        lefts.append(pltpu.make_async_copy(block, left.at[s, :, pl.ds(k * span, span)], sem.at[b]))
    for n in range(kinds):
        own, *others = rights[3 * n : 3 * n + 3]
        for s in range(2):
            for i, (source, part) in enumerate(((own.at[s], slice(0, span)), (others[s], slice(span, GROUP * span)))):
                at = sem.at[2 * GROUP + 4 * n + 2 * s + i]
                loads.append(pltpu.make_async_copy(source, right.at[n, s, :, part], at))

    @pl.when(kind == 0)
    def _():
        for copy in loads[0:2] + lefts[:GROUP] + loads[2:4] + lefts[GROUP:] + loads[4:]:
            copy.start()
        for copy in loads[0:2] + lefts[:GROUP]:
            copy.wait()

    for n in range(1, kinds):

        @pl.when(kind == n)
        def _(n=n):
            for copy in loads[4 * n : 4 * n + 4]:
                copy.wait()

    acc[...] = dot(left[0], right[kind, 0], NT)

    @pl.when(kind == 0)
    def _():
        for copy in loads[2:4] + lefts[GROUP:]:
            copy.wait()

    acc[...] += dot(left[1], right[kind, 1], NT)
    part = acc.shape[0] // PARTS
    places = [(outs[0], i) for i in range(4)] + [(outs[1], 0), (outs[1], 1), (outs[2], 0), (outs[3], 0)]
    for (out, i), slot in zip(places, SLOTS):
        start = pl.multiple_of((slot ^ ranks[1]) * part, 8)
        out[i] = acc[pl.ds(start, part), :].astype(LOW)


def branch_kernel(seq, ranks, mid_ref, cot_ref, e0, e1, e2, gain_ref, b0, b1, b2, b3, att_ref, gm_ref, gb_ref, do_ref, delta_ref, gain_out, w_ref):
    width, span = mid_ref.shape
    assemble(ranks[0], (b0, b1, b2, b3), w_ref)
    middle = mid_ref[...]
    grad = e0[0].astype(FULL) + e1[0].astype(FULL) + e2[...].astype(FULL)
    inverse = lax.rsqrt(jnp.mean(middle * middle, axis=0, keepdims=True) + NORM_EPS)
    scaled = grad * gain_ref[:, 1:2].astype(FULL)
    turned = jnp.mean(scaled * middle, axis=0, keepdims=True)
    grad_middle = cot_ref[seq].astype(FULL) + inverse * scaled - middle * (inverse * inverse * inverse * turned)
    gain_out[...] = dot(jnp.ones((8, span), LOW), (grad * middle * inverse).astype(LOW), NT)
    gm_ref[...] = grad_middle
    branch = grad_middle.astype(LOW)
    gb_ref[...] = branch
    grad_att = dot(w_ref[...], branch).astype(LOW)
    do_ref[...] = grad_att
    both = grad_att.astype(FULL) * att_ref[...].astype(FULL)
    heads = width // HD
    for h in range(heads):
        delta_ref[h : h + 1, :] = jnp.sum(both[h * HD : (h + 1) * HD, :], axis=0, keepdims=True)
    delta_ref[heads:, :] = jnp.zeros((delta_ref.shape[0] - heads, span), FULL)


def attend_back_kernel(seq, q_ref, b0, b1, b2, b3, p_ref, do_ref, delta_ref, cos_ref, sin_ref, gq_ref, own_ref, far_ref, send_ref):
    span = q_ref.shape[1]
    per = q_ref.shape[0] // HD
    h = pl.program_id(0)
    kv_t = jnp.concatenate([b0[...], b1[...], b2[...], b3[...]], axis=1)
    kv = kv_t.T
    query, out_grad = beside(q_ref), beside(do_ref)
    delta = jnp.concatenate([delta_ref[pl.ds(per * h + i, 1), :] for i in range(per)], axis=1)
    none = jnp.zeros(out_grad.shape, LOW)
    grad_probs = dot(kv, jnp.concatenate([none, out_grad], axis=0))
    grad_scores = (p_ref[0].astype(FULL) * (grad_probs - delta)).astype(LOW)
    grad_q = dot(kv_t[0:HD, :], grad_scores) * SCALE
    for i in range(per):
        one, two = turn(grad_q[:, i * span : (i + 1) * span], cos_ref[seq], sin_ref[seq], -1.0)
        gq_ref[i * HD : i * HD + HD // 2, :] = one.astype(LOW)
        gq_ref[i * HD + HD // 2 : (i + 1) * HD, :] = two.astype(LOW)
    keys = dot(query, grad_scores, NT).astype(LOW)
    values = dot(out_grad, p_ref[0], NT).astype(LOW)
    for k in range(GROUP):
        out = (own_ref, send_ref.at[0], far_ref, send_ref.at[1])[k]
        part = slice(k * span, (k + 1) * span)
        out[0:HD, :] = keys[:, part]
        out[HD:, :] = values[:, part]


def slot_at(i):
    n = PARTS - 1 - i
    return ((n & 1) << 2) | (n & 2) | ((n >> 2) & 1)


def spread(ranks, acc, own_ref, far_ref, send_ref):
    part = acc.shape[1] // PARTS
    outs = (own_ref, send_ref.at[0], far_ref, send_ref.at[1])

    def move(i, carry):
        start = pl.multiple_of((slot_at(i) ^ ranks[1]) * part, 8)
        for k, out in enumerate(outs):
            out[i] = acc[ranks[0] ^ k, pl.ds(start, part), :].astype(LOW)
        return carry

    lax.fori_loop(0, PARTS, move, 0)


def query_weight_kernel(ranks, norm_ref, gq_a, gq_b, att_a, att_b, gb_a, gb_b, own_ref, far_ref, send_ref, acc):
    width, span = gq_a.shape
    shard = width // GROUP
    for b in range(GROUP):
        rows = slice(b * shard, (b + 1) * shard)
        acc[b, 0:shard, 0:width] = dot(norm_ref[rows, 0:span], gq_a[...], NT) + dot(norm_ref[rows, span:], gq_b[...], NT)
        acc[b, 0:shard, width:] = dot(att_a[rows, :], gb_a[...], NT) + dot(att_b[rows, :], gb_b[...], NT)
        acc[b, shard:, :] = jnp.zeros((acc.shape[1] - shard, acc.shape[2]), FULL)
    spread(ranks, acc, own_ref, far_ref, send_ref)


def key_weight_kernel(ranks, *refs):
    norm_ref, *terms = refs[0:7]
    cos_ref, sin_ref, part_ref, k0, k1, k2, k3, tok_ref, gm_a, gm_b, gain_a, gain_b = refs[7:19]
    own_ref, far_ref, send_ref, out_ref, gkv_ref, wkv_ref, acc = refs[19:]
    width = norm_ref.shape[0]
    span = gm_a.shape[1]
    shard = width // GROUP
    kw2 = gkv_ref.shape[0]
    kw = kw2 // 2
    assemble(ranks[0], (k0, k1, k2, k3), wkv_ref)
    gain_one = wkv_ref[:, kw2 : kw2 + 1].astype(FULL)
    grad_gain = None
    for s in range(2):
        e0, e1, e2 = terms[3 * s : 3 * s + 3]
        part = slice(s * span, (s + 1) * span)
        grad = e0[...].astype(FULL) + e1[0].astype(FULL) + e2[...].astype(FULL)
        for h in range(kw // HD):
            top = h * 2 * HD
            one, two = turn(grad[top : top + HD, :], cos_ref[s], sin_ref[s], -1.0)
            gkv_ref[h * HD : h * HD + HD // 2, part] = one.astype(LOW)
            gkv_ref[h * HD + HD // 2 : (h + 1) * HD, part] = two.astype(LOW)
            gkv_ref[kw + h * HD : kw + (h + 1) * HD, part] = grad[top + HD : top + 2 * HD, :].astype(LOW)
        grad_norm = part_ref[s] + dot(wkv_ref[:, 0:kw2], gkv_ref[:, part])
        x = tok_ref[s].astype(FULL)
        inverse = lax.rsqrt(jnp.mean(x * x, axis=0, keepdims=True) + NORM_EPS)
        scaled = grad_norm * gain_one
        turned = jnp.mean(scaled * x, axis=0, keepdims=True)
        out_ref[s] = (gm_a, gm_b)[s][...] + inverse * scaled - x * (inverse * inverse * inverse * turned)
        row = dot(jnp.ones((8, span), LOW), (grad_norm * x * inverse).astype(LOW), NT)
        grad_gain = row if grad_gain is None else grad_gain + row
    gains = jnp.concatenate([grad_gain[0:1, :], gain_a[0:1, :] + gain_b[0:1, :], jnp.zeros((6, width), FULL)], axis=0)
    for b in range(GROUP):
        rows = slice(b * shard, (b + 1) * shard)
        acc[b, 0:shard, :] = dot(norm_ref[rows, :], gkv_ref[...], NT)
        acc[b, shard:, :] = jnp.zeros((acc.shape[1] - shard, kw2), FULL)
        acc[b, shard : shard + 8, 0:shard] = gains[:, rows]
    spread(ranks, acc, own_ref, far_ref, send_ref)


def query_grad_kernel(ranks, gq_a, gq_b, q0, q1, q2, q3, out_ref, wq_ref):
    assemble(ranks[0], (q0, q1, q2, q3), wq_ref)
    out_ref[0] = dot(wq_ref[...], gq_a[...])
    out_ref[1] = dot(wq_ref[...], gq_b[...])


def place(slot):
    return ((slot >> 2) & 1) + ((slot >> 1) & 1) * 2


def gathered(ranks, pairs):
    def move(a, carry):
        slot = ranks[1] ^ a
        index = place(slot)
        for parity in range(2):

            @pl.when(slot % 2 == parity)
            def _(parity=parity):
                for pair in pairs:
                    part = pair[parity].shape[1]
                    rows = pl.ds(pl.multiple_of(a * part, 8), part)
                    pair[2][rows, :] = pair[parity][index].astype(FULL)

        return carry

    lax.fori_loop(0, PARTS, move, 0)


def forward_weights_kernel(ranks, even, odd, *outs):
    columns = outs[0].shape[1]
    for i, out in enumerate(outs):
        part = slice(i * columns, (i + 1) * columns)
        gathered(ranks, [(even.at[:, :, part], odd.at[:, :, part], out)])


def attention_done_kernel(ranks, even, odd, q_ref, o_ref, k_ref, v_ref, gain_ref, scratch):
    shard, width = q_ref.shape
    kw = k_ref.shape[0]
    gathered(ranks, [(even, odd, scratch)])
    q_ref[...] = scratch[0:shard, 0:width]
    o_ref[...] = scratch[0:shard, width : 2 * width]
    k_ref[...] = scratch[0:shard, 2 * width : 2 * width + kw].T
    v_ref[...] = scratch[0:shard, 2 * width + kw :].T
    gain_ref[...] = scratch[shard : shard + 8, 2 * width : 2 * width + shard]


def tables(places):
    half = HD // 2
    frequency = ROPE_BASE ** (-2.0 * jnp.arange(half, dtype=FULL) / HD)
    angles = places.astype(FULL)[:, None, :] * frequency[None, :, None]
    return jnp.cos(angles), jnp.sin(angles)


def body(
    tokens,
    w_query,
    w_key,
    w_value,
    w_out,
    w_gate,
    w_up,
    w_down,
    gain_attn,
    gain_mlp,
    span_order,
    piece_starts,
    cotangent,
):
    ranks = lax.axis_size("rep")
    rank_grp = lax.axis_index("grp")
    seq_count, span, width = tokens.shape
    shard = w_query.shape[0]
    kw = w_key.shape[1]
    kw2 = 2 * kw
    kv_heads = kw // HD
    per = width // kw
    ff = w_gate.shape[1]
    rows = seq_count * span
    length = GROUP * span
    place_of = jnp.stack([rank_grp, lax.axis_index("rep") % PARTS]).astype(jnp.int32)
    tok_t = jnp.swapaxes(tokens, 1, 2)
    cot_t = jnp.swapaxes(cotangent, 1, 2)
    wd_t = w_down.T
    act = whole((width, span))
    seqs = whole((seq_count, width, span))
    one_seq = lambda s: pl.BlockSpec((1, width, span), lambda *_: (s, 0, 0))
    table = whole((seq_count, HD // 2, span))
    gain_spec = whole((width, LANES))
    head = pl.BlockSpec((2 * HD, span), lambda h, *_: (h, 0))
    probs_spec = pl.BlockSpec((1, length, per * span), lambda h, *_: (h, 0, 0))
    q_spec = lambda s: pl.BlockSpec((per * HD, span), lambda h, *_: (h, s))
    per_head = pl.BlockSpec((per * HD, span), lambda h, *_: (h, 0))

    kv_shard = call(
        pack_kernel,
        "pack",
        shape_of((shard, kw2 + LANES)),
        in_specs=[whole((kw, shard))] * 2 + [whole((2, shard))],
        out_specs=whole((shard, kw2 + LANES)),
        micros=2,
    )(w_key.T, w_value.T, jnp.stack([gain_attn, gain_mlp]).astype(FULL))
    kv_flight = Blocks(kv_shard)
    q_flight = Blocks(w_query, kv_shard)
    own_span = lax.dynamic_slice(span_order, (0, rank_grp), (seq_count, 1))
    places = own_span * span + jnp.arange(span, dtype=jnp.int32)[None, :]
    cos_cols, sin_cols = tables(places)
    wgut, wgu = call(
        flip_two_kernel,
        "flip_two",
        (shape_of((2 * ff, width)), shape_of((width, 2 * ff))),
        in_specs=[whole((width, ff))] * 2,
        out_specs=(whole((2 * ff, width)), whole((width, 2 * ff))),
        micros=4,
    )(after(w_gate, kv_flight.sent), w_up)
    wd = call(
        flip_one_kernel,
        "flip_one",
        shape_of((ff, width)),
        in_specs=[whole((width, ff))],
        out_specs=whole((ff, width)),
        micros=2,
    )(after(wd_t, wgut))
    kv_blocks = kv_flight.finish(wd)
    norm_low, kv_a, kv_b, gain_cols = call(
        keys_values_kernel,
        "keys_values",
        (shape_of((width, rows)), shape_of((kw2, span)), shape_of((kw2, span)), shape_of((width, LANES))),
        free=range(1, 5),
            prefetch=1,
        in_specs=[NEAR] + [whole(kv_shard.shape)] * 4 + [table, table],
        out_specs=(whole((width, rows)), whole((kw2, span)), whole((kw2, span)), gain_spec),
        scratch=[pltpu.VMEM((width, kw2 + LANES), LOW)],
        micros=4.3,
    )(place_of, tok_t, *kv_blocks, cos_cols, sin_cols)
    kv_flight = [Blocks(kv_a), None]
    q_blocks = q_flight.finish(norm_low)
    queries = call(
        queries_kernel,
        "queries",
        shape_of((width, rows)),
        free=range(1, 5),
            prefetch=1,
        in_specs=[whole((width, rows))] + [whole((shard, width))] * 4 + [table, table],
        out_specs=whole((width, rows)),
        scratch=[pltpu.VMEM((width, width), LOW)],
        micros=0.1,
    )(place_of, norm_low, *q_blocks, cos_cols, sin_cols)

    o_flight = Blocks(w_out, kv_a)
    kv_flight[1] = Blocks(kv_b, *q_blocks)
    cot_flight = [Blocks(cot_t[0], queries), None]
    cot_blocks = [None, None]
    kv_all = [kv_flight[0].finish(queries), None]

    def attend_of(s, query):
        return call(
            functools.partial(attend_kernel, s),
            "attend",
            (shape_of((kv_heads, length, per * span)), shape_of((width, span))),
            free=range(1, 5),
            prefetch=3,
            grid=(kv_heads,),
            in_specs=[q_spec(s)] + [head] * 4,
            out_specs=(probs_spec, per_head),
            scratch=[pltpu.VMEM((length, span), FULL)],
            micros=0.1,
        )(place_of, span_order, piece_starts, query, *kv_all[s])

    def middle_of(s, att):
        return call(
            middle_kernel,
            "middle",
            (shape_of((width, span), FULL), shape_of((width, span))),
            free=range(1, 5),
            prefetch=1,
            in_specs=[act] + [whole((shard, width))] * 4 + [one_seq(s), gain_spec],
            out_specs=(act, act),
            scratch=[pltpu.VMEM((width, width), LOW)],
            micros=3,
        )(place_of, att, *o_blocks, tok_t, gain_cols)

    probs_a, att_a = attend_of(0, queries)
    o_blocks = o_flight.finish(att_a)
    kv_all[1] = kv_flight[1].finish(att_a)
    middle_a, x_a = middle_of(0, att_a)
    x_flight = [Blocks(x_a), None]
    cot_flight[1] = Blocks(cot_t[1], x_flight[0].sent, x_a)
    probs_b, att_b = attend_of(1, after(queries, x_a))
    cot_flight[0].arrive(att_b)
    middle_b, x_b = middle_of(1, after(att_b, *cot_flight[0].ready))
    x_flight[1] = Blocks(x_b)
    x_flight[0].arrive(middle_b)
    cot_blocks[0] = cot_flight[0].finish(middle_b)
    stats, attended, middles = (probs_a, probs_b), (att_a, att_b), (middle_a, middle_b)

    each = pl.BlockSpec((1, width, span), lambda s, *_: (s, 0, 0))
    each_ff = pl.BlockSpec((1, ff, span), lambda s, *_: (s, 0, 0))
    two = shape_of((seq_count, width, span))
    two_ff = shape_of((seq_count, ff, span))
    own_out, own_grad, own_hid, own_gg, own_gu = call(
        own_block_kernel,
        "own_blocks",
        (two, two, two_ff, two_ff, two_ff),
        grid=(seq_count,),
        in_specs=[act, act, each] + [NEAR] * 4,
        out_specs=(each, each, each_ff, each_ff, each_ff),
        scratch=[pltpu.VMEM((width, span), LOW), pltpu.VMEM((2 * ff, span), LOW)],
        micros=8,
    )(after(x_a, *x_flight[0].ready, *cot_blocks[0]), x_b, cot_t, wgut, wgu, wd_t, wd)
    x_blocks = [x_flight[0].finish(own_out), None]
    cot_flight[1].arrive(own_out)

    def other_blocks(s, *others):
        half = pl.BlockSpec((1, width, span), lambda k, *_: (k // 2, 0, 0))
        per_block = pl.BlockSpec((ff, span), lambda k, *_: (0, k))
        act_shape, half_shape, ff_shape = shape_of((width, span)), shape_of((2, width, span)), shape_of((ff, 3 * span))
        return call(
            other_blocks_kernel,
            "other_blocks",
            (act_shape, half_shape, act_shape, half_shape, ff_shape, ff_shape, ff_shape),
            free=(0, 2),
            grid=(GROUP - 1,),
            in_specs=[ANY] * 6 + [NEAR] * 4,
            out_specs=(act, half, act, half) + (per_block,) * 3,
            scratch=[
                pltpu.VMEM((6, width, span), LOW),
                pltpu.VMEM((2 * ff, span), LOW),
                pltpu.SemaphoreType.DMA((6,)),
            ],
            micros=12,
        )(after(x_blocks[s][1], *others), *x_blocks[s][2:], *cot_blocks[s][1:], wgut, wgu, wd_t, wd)

    fo_a, so_a, fg_a, sg_a, hid_a, gg_a, gu_a = other_blocks(0, *cot_flight[1].ready)
    grad_a = Terms(own_grad[0], fg_a, sg_a)
    out_a = Terms(own_out[0], fo_a, so_a)
    x_flight[1].arrive(fg_a)
    x_blocks[1] = x_flight[1].finish()
    cot_blocks[1] = cot_flight[1].finish(fg_a)
    fo_b, so_b, fg_b, sg_b, hid_b, gg_b, gu_b = other_blocks(1, fg_a)
    grad_b = Terms(own_grad[1], fg_b, sg_b)
    out_b = Terms(own_out[1], fo_b, so_b)
    stage = (grad_a.cross(fg_b), out_a.cross(fg_b))
    grads = (grad_a, grad_b)

    part = width // PARTS

    def sums(name, blocks, kinds, *others):
        count = len(kinds)
        columns = count * ff
        pieces = call(
            functools.partial(weight_kernel, count),
            name,
            tuple(shape_of((n, part, columns)) for n in (4, 2, 1, 1)),
            prefetch=1,
            grid=(count,),
            in_specs=[ANY] * (2 * GROUP + 3 * count),
            out_specs=tuple(pl.BlockSpec((n, part, ff), lambda m, *_: (0, 0, m)) for n in (4, 2, 1, 1)),
            scratch=[
                pltpu.VMEM((2, width, length), LOW),
                pltpu.VMEM((count, 2, ff, length), LOW),
                pltpu.VMEM((width, ff), FULL),
                pltpu.SemaphoreType.DMA((2 * GROUP + 4 * count,)),
            ],
            micros=2 + 6 * count,
        )(place_of, after(blocks[0], *others), *blocks[1:], *sum(kinds, ()))
        return RepSum(pieces, ranks)

    x_all = x_blocks[0] + x_blocks[1]
    down_sum = sums("down_weights", cot_blocks[0] + cot_blocks[1], [(own_hid, hid_a, hid_b)], *stage)
    done = down_sum.pieces[0]
    stage = (grad_b.cross(done), out_b.beside, done)
    up_sum = sums("gate_up_weights", x_all, [(own_gg, gg_a, gg_b), (own_gu, gu_a, gu_b)], *stage)
    done = up_sum.pieces[0]
    stage = (grad_a.across, out_b.cross(done), down_sum.second(done), out_a.across, done)

    def branch_of(s, *others):
        _, beside_term, across_term = grads[s].all()
        first = whole((1, width, span))
        return call(
            functools.partial(branch_kernel, s),
            "branch",
            (
                shape_of((width, span), FULL),
                shape_of((width, span)),
                shape_of((width, span)),
                shape_of((16, span), FULL),
                shape_of((8, width), FULL),
            ),
            free=(3, 4),
            prefetch=1,
            in_specs=[NEAR, NEAR, one_seq(s), first, act, NEAR] + [NEAR] * 5,
            out_specs=(act, act, act, whole((16, span)), whole((8, width))),
            scratch=[pltpu.VMEM((width, width), LOW)],
            micros=4,
        )(place_of, middles[s], cot_t, own_grad, beside_term, after(across_term, *others), gain_cols, *o_blocks, attended[s])

    def attend_back_of(s, out_grad, delta):
        halves = pl.BlockSpec((2, 2 * HD, span), lambda h, *_: (0, h, 0))
        grad_q, *kv_parts = call(
            functools.partial(attend_back_kernel, s),
            "attend_back",
            (shape_of((width, span)), shape_of((kw2, span)), shape_of((kw2, span)), shape_of((2, kw2, span))),
            grid=(kv_heads,),
            in_specs=[q_spec(s)] + [head] * 4 + [probs_spec, per_head, whole((16, span)), table, table],
            out_specs=(per_head, head, head, halves),
            micros=11,
        )(queries, *kv_all[s], stats[s], out_grad, delta, cos_cols, sin_cols)
        return grad_q, Terms(*kv_parts)

    mid_a, branch_a, dout_a, delta_a, gain_a = branch_of(0, *stage)
    stage = (down_sum.third(branch_a), grad_b.across)
    gq_a, kv_grad_a = attend_back_of(0, after(dout_a, *stage), delta_a)
    stage = (out_b.across, down_sum.own(gq_a))
    mid_b, branch_b, dout_b, delta_b, gain_b = branch_of(1, *stage)
    stage = (kv_grad_a.cross(branch_b), up_sum.second(branch_b))
    gq_b, kv_grad_b = attend_back_of(1, after(dout_b, *stage), delta_b)
    stage = (down_sum.spread(gq_b), kv_grad_a.across)

    grown = shard + GAIN_ROWS
    piece = grown // PARTS
    spread_out = lambda columns: (shape_of((PARTS, piece, columns)),) * 2 + (shape_of((2, PARTS, piece, columns)),)
    spread_spec = lambda columns: (whole((PARTS, piece, columns)),) * 2 + (whole((2, PARTS, piece, columns)),)
    query_parts = call(
        query_weight_kernel,
        "query_weights",
        spread_out(2 * width),
        prefetch=1,
        in_specs=[NEAR, NEAR, act] + [NEAR] * 4,
        out_specs=spread_spec(2 * width),
        scratch=[pltpu.VMEM((GROUP, grown, 2 * width), FULL)],
        micros=8,
    )(place_of, norm_low, gq_a, after(gq_b, *stage), *attended, branch_a, branch_b)
    done = query_parts[0]
    stage = (kv_grad_b.cross(done), up_sum.third(done))
    query_terms = Terms(*query_parts, *stage)
    grad_part = call(
        query_grad_kernel,
        "query_grad",
        shape_of((seq_count, width, span), FULL),
        prefetch=1,
        in_specs=[NEAR, act] + [NEAR] * 4,
        out_specs=seqs,
        scratch=[pltpu.VMEM((width, width), LOW)],
        micros=4,
    )(place_of, gq_a, after(gq_b, *stage), *q_blocks)
    stage = (query_terms.cross(grad_part),)
    stage = (*stage, kv_grad_b.across)

    def owned(terms):
        own, beside_term, across = terms.all()
        cuts = (slice(0, 4), slice(4, 6), slice(6, 7), slice(7, 8))
        return [three((own[c], beside_term[:, c], across[c])) for c in cuts]

    first = whole((1, kw2, span))
    terms = []
    for term in (kv_grad_a, kv_grad_b):
        terms += term.all()
    *key_parts, grad_tokens = call(
        key_weight_kernel,
        "key_weights",
        spread_out(kw2) + (shape_of((seq_count, width, span), FULL),),
        free=range(1, 7),
            prefetch=1,
        in_specs=[NEAR]
        + [whole((kw2, span)), first, whole((kw2, span))] * 2
        + [table, table, seqs]
        + [NEAR] * 7
        + [whole((8, width))] * 2,
        out_specs=spread_spec(kw2) + (seqs,),
        scratch=[
            pltpu.VMEM((kw2, rows), LOW),
            pltpu.VMEM((width, kw2 + LANES), LOW),
            pltpu.VMEM((GROUP, grown, kw2), FULL),
        ],
        micros=10,
    )(
        place_of,
        norm_low,
        after(terms[0], *stage),
        *terms[1:],
        cos_cols,
        sin_cols,
        grad_part,
        *kv_blocks,
        tok_t,
        mid_a,
        mid_b,
        gain_a,
        gain_b,
    )
    down_pair = down_sum.done(grad_tokens)
    stage = (up_sum.own(grad_tokens), down_pair[0])
    key_terms = Terms(*key_parts)

    def finished(name, kernel, pair, outs, *others):
        columns = pair[0].shape[2]
        return call(
            kernel,
            name,
            (shape_of((width, ff), FULL),) * outs,
            free=range(2),
            prefetch=1,
            in_specs=[whole((4, part, columns))] * 2,
            out_specs=(whole((width, ff)),) * outs,
            micros=3.5 * outs,
        )(place_of, after(pair[0], *others), pair[1])

    block_out = jnp.stack(
        [middle + three(term.all()) for middle, term in zip(after(middles, *stage), (out_a, out_b))]
    )
    key_terms.cross(block_out)
    pieces = []
    for query_piece, key_piece in zip(owned(query_terms), owned(key_terms)):
        joint = jnp.concatenate([query_piece, key_piece], axis=-1)
        pieces.append(joint.astype(LOW))
    query_sum = ShortSum(pieces, ranks)

    up_sum.spread(*pieces)
    (grad_down,) = finished("down_done", forward_weights_kernel, down_pair, 1, *pieces)
    step = query_sum.second(grad_down)
    up_pair = up_sum.done(*step)
    step = query_sum.own(up_pair[0])
    query_pair = query_sum.done(step, up_pair[1])
    grad_gate, grad_up = finished("gate_up_done", forward_weights_kernel, up_pair, 2, query_pair[0])
    grad_down = grad_down.T
    grad_query, grad_out, grad_key, grad_value, grad_gains = call(
        attention_done_kernel,
        "attention_done",
        (shape_of((shard, width), FULL),) * 2 + (shape_of((kw, shard), FULL),) * 2 + (shape_of((8, shard), FULL),),
        free=range(2),
            prefetch=1,
        in_specs=[whole((4, piece, 2 * width + kw2))] * 2,
        out_specs=(whole((shard, width)),) * 2 + (whole((kw, shard)),) * 2 + (whole((8, shard)),),
        scratch=[pltpu.VMEM((grown, 2 * width + kw2), FULL)],
        micros=5,
    )(place_of, *query_pair)
    return (
        jnp.swapaxes(block_out, 1, 2),
        jnp.swapaxes(grad_tokens, 1, 2),
        grad_query,
        grad_key.T,
        grad_value.T,
        grad_out,
        grad_gate,
        grad_up,
        grad_down,
        grad_gains[0],
        grad_gains[1],
    )


def solution(mesh):
    placed = (
        P("rep", "grp", None),
        P("grp", None),
        P("grp", None),
        P("grp", None),
        P("grp", None),
        P(None, "grp"),
        P(None, "grp"),
        P("grp", None),
        P("grp"),
        P("grp"),
        P("rep", None),
        P("rep", None),
        P("rep", "grp", None),
    )
    return jax.shard_map(
        body,
        mesh=mesh,
        in_specs=placed,
        out_specs=(
            P("rep", "grp", None),
            P("rep", "grp", None),
            P("grp", None),
            P("grp", None),
            P("grp", None),
            P("grp", None),
            P(None, "grp"),
            P(None, "grp"),
            P("grp", None),
            P("grp"),
            P("grp"),
        ),
        check_vma=False,
    )
```

```python
import functools

import jax
import jax.numpy as jnp
from jax import lax
from jax.experimental import pallas as pl
from jax.experimental.pallas import tpu as pltpu
from jax.sharding import PartitionSpec as P

HD = 64
PIECE = 256
LANES = 128
GROUP = 4
PARTS = 8
GAIN_ROWS = 16
RATE = 2.0e9
SLOTS = (7, 3, 5, 1, 6, 2, 4, 0)


NORM_EPS = 1e-05
ROPE_BASE = 10000.0
MASKED_SCORE = -1e30
SCALE = HD ** (-0.5)

LOW = jnp.bfloat16
FULL = jnp.float32
NN = (((1,), (0,)), ((), ()))
NT = (((1,), (1,)), ((), ()))
TN = (((0,), (0,)), ((), ()))


def dot(left_mat, right_mat, form=NN):
    return lax.dot_general(left_mat, right_mat, form, preferred_element_type=FULL)


def swap(values, axis, count, mask):
    return lax.ppermute(values, axis, [(i, i ^ mask) for i in range(count)])


def after(values, *others):
    return lax.optimization_barrier((values,) + others)[0] if others else values


class Blocks:
    def __init__(self, own, *others):
        self.own = own
        sent = after(own, *others)
        self.across = swap(sent, "grp", GROUP, 2)
        self.sent = sent

    def arrive(self, *others):
        pair = after((self.sent, self.across), *others)
        self.ready = pair
        self.core = swap(pair[0], "grp", GROUP, 1), swap(pair[1], "grp", GROUP, 1)

    def finish(self, *others):
        if not hasattr(self, "core"):
            self.arrive(*others)
        beside, corner = after(self.core, *others)
        return self.own, beside, self.across, corner


class Terms:
    def __init__(self, own, far, send, *others):
        self.own, self.far = own, far
        self.beside = swap(after(send, *others), "grp", GROUP, 1)

    def cross(self, *others):
        far, beside = after((self.far, self.beside), *others)
        across = (far.astype(FULL) + beside[1].astype(FULL)).astype(LOW)
        self.sent = across
        self.across = swap(across, "grp", GROUP, 2)
        return across

    def all(self):
        return self.own, self.beside, self.across


def three(terms):
    return terms[0].astype(FULL) + terms[1][0].astype(FULL) + terms[2].astype(FULL)


class RepSum:
    def __init__(self, pieces, ranks):
        self.pieces, self.ranks = pieces, ranks
        self.one = swap(pieces[0], "rep", ranks, 1)

    def second(self, *others):
        self.one = after(self.one, *others)
        two = (self.pieces[1].astype(FULL) + self.one[0:2].astype(FULL)).astype(LOW)
        self.held_two = two
        self.two = swap(two, "rep", self.ranks, 2)
        return two

    def third(self, *others):
        self.two = after(self.two, *others)
        four = self.pieces[2].astype(FULL) + self.one[2:3].astype(FULL) + self.two[0:1].astype(FULL)
        four = four.astype(LOW)
        self.four = swap(four, "rep", self.ranks, 4)
        return four

    def own(self, *others):
        ranks = self.ranks
        self.four = after(self.four, *others)
        mine = self.pieces[3].astype(FULL) + self.one[3:4].astype(FULL) + self.two[1:2].astype(FULL)
        mine = (mine + self.four.astype(FULL)).astype(LOW)
        if ranks > PARTS:
            others = [[j * PARTS + i for j in range(ranks // PARTS)] for i in range(PARTS)]
            mine = lax.psum(mine, "rep", axis_index_groups=others)
        self.mine = mine
        self.back = swap(mine, "rep", ranks, 4)
        return mine

    def spread(self, *others):
        self.back = after(self.back, *others)
        held = jnp.concatenate([self.mine, self.back])
        self.held = held
        self.wide = swap(held, "rep", self.ranks, 2)
        return held

    def done(self, *others):
        self.wide = after(self.wide, *others)
        held = jnp.concatenate([self.held, self.wide])
        return held, swap(held, "rep", self.ranks, 1)


class ShortSum(RepSum):
    def second(self, *others):
        one = after(self.one, *others)
        self.one = one
        six = (self.pieces[1][0:1].astype(FULL) + one[0:1].astype(FULL)).astype(LOW)
        two = (self.pieces[1][1:2].astype(FULL) + one[1:2].astype(FULL)).astype(LOW)
        four = (self.pieces[2].astype(FULL) + one[2:3].astype(FULL)).astype(LOW)
        self.terms = [swap(sent, "rep", self.ranks, mask) for sent, mask in ((six, 6), (two, 2), (four, 4))]
        return six, two, four

    def own(self, *others):
        ranks = self.ranks
        terms = after(self.terms, *others)
        mine = self.pieces[3].astype(FULL) + self.one[3:4].astype(FULL)
        mine = (mine + terms[0].astype(FULL) + terms[1].astype(FULL) + terms[2].astype(FULL)).astype(LOW)
        if ranks > PARTS:
            others = [[j * PARTS + i for j in range(ranks // PARTS)] for i in range(PARTS)]
            mine = lax.psum(mine, "rep", axis_index_groups=others)
        self.mine = mine
        self.back = [swap(mine, "rep", ranks, mask) for mask in (4, 2, 6)]
        return mine

    def done(self, *others):
        held = jnp.concatenate([self.mine, *after(self.back, *others)])
        return held, swap(held, "rep", self.ranks, 1)


def call(kernel, name, out_shape, *, grid=(1,), prefetch=0, in_specs, out_specs, scratch=(), micros=1, vmem=36, free=()):
    def lies(shape):
        return pltpu.HBM(shape.shape, shape.dtype)

    several = isinstance(out_shape, tuple)
    run = pl.pallas_call(
        kernel,
        name=name,
        out_shape=tuple(map(lies, out_shape)) if several else lies(out_shape),
        grid_spec=pltpu.PrefetchScalarGridSpec(
            num_scalar_prefetch=prefetch,
            grid=grid,
            in_specs=in_specs,
            out_specs=out_specs,
            scratch_shapes=list(scratch),
        ),
        compiler_params=pltpu.CompilerParams(vmem_limit_bytes=vmem << 20),
        cost_estimate=pl.CostEstimate(flops=int(micros * RATE), bytes_accessed=1 << 10, transcendentals=0),
    )

    def placed(*args):
        rest = [
            arg if spec is NEAR or i in free else pltpu.with_memory_space_constraint(arg, pltpu.HBM)
            for i, (arg, spec) in enumerate(zip(args[prefetch:], in_specs, strict=True))
        ]
        return run(*args[:prefetch], *rest)

    return placed


def whole(shape):
    return pl.BlockSpec(shape, lambda *_: (0,) * len(shape))


ANY = pl.BlockSpec(memory_space=pl.ANY)
NEAR = pl.BlockSpec(memory_space=pltpu.VMEM)


def shape_of(shape, kind=LOW):
    return jax.ShapeDtypeStruct(shape, kind)


def turn(rows, cosine, sine_val, sign):
    one, two = rows[0 : HD // 2, :], rows[HD // 2 : HD, :]
    sine_val = sine_val * sign
    return one * cosine - two * sine_val, two * cosine + one * sine_val


def assemble(rank, blocks, scratch):
    rows = blocks[0].shape[0]
    for k in range(GROUP):
        start = pl.multiple_of((rank ^ k) * rows, 16)
        scratch[pl.ds(start, rows), :] = blocks[k][...]


def pack_kernel(wk_ref, wv_ref, gains_ref, out_ref):
    kw, shard = wk_ref.shape
    out_ref[:, 0:kw] = wk_ref[...].T
    out_ref[:, kw : 2 * kw] = wv_ref[...].T
    gains = jnp.concatenate([gains_ref[...], jnp.zeros((LANES - 2, shard), FULL)], axis=0)
    out_ref[:, 2 * kw :] = gains.T.astype(LOW)


def flip_two_kernel(wg_ref, wu_ref, wgut_ref, wgu_ref):
    ff = wg_ref.shape[1]
    wgut_ref[0:ff, :] = wg_ref[...].T
    wgut_ref[ff:, :] = wu_ref[...].T
    wgu_ref[:, 0:ff] = wg_ref[...]
    wgu_ref[:, ff:] = wu_ref[...]


def flip_one_kernel(wdt_ref, wd_ref):
    wd_ref[...] = wdt_ref[...].T


def keys_values_kernel(ranks, tok_ref, b0, b1, b2, b3, cos_ref, sin_ref, norm_ref, kv_a, kv_b, gain_ref, w_ref):
    span = tok_ref.shape[2]
    kw2 = kv_a.shape[0]
    kw = kw2 // 2
    assemble(ranks[0], (b0, b1, b2, b3), w_ref)
    gains = w_ref[:, kw2:]
    gain_ref[...] = gains
    gain_one = gains[:, 0:1].astype(FULL)
    for s, out in enumerate((kv_a, kv_b)):
        x = tok_ref[s].astype(FULL)
        inverse = lax.rsqrt(jnp.mean(x * x, axis=0, keepdims=True) + NORM_EPS)
        norm = (x * inverse * gain_one).astype(LOW)
        norm_ref[:, s * span : (s + 1) * span] = norm
        kv = dot(w_ref[:, 0:kw2], norm, TN)
        for h in range(kw // HD):
            one, two = turn(kv[h * HD : (h + 1) * HD, :], cos_ref[s], sin_ref[s], 1.0)
            top = h * 2 * HD
            out[top : top + HD // 2, :] = one.astype(LOW)
            out[top + HD // 2 : top + HD, :] = two.astype(LOW)
            out[top + HD : top + 2 * HD, :] = kv[kw + h * HD : kw + (h + 1) * HD, :].astype(LOW)


def queries_kernel(ranks, norm_ref, b0, b1, b2, b3, cos_ref, sin_ref, q_ref, w_ref):
    width = b0.shape[1]
    span = cos_ref.shape[2]
    assemble(ranks[0], (b0, b1, b2, b3), w_ref)
    for s in range(2):
        part = slice(s * span, (s + 1) * span)
        query = dot(w_ref[...], norm_ref[:, part], TN)
        for h in range(width // HD):
            one, two = turn(query[h * HD : (h + 1) * HD, :], cos_ref[s], sin_ref[s], 1.0)
            q_ref[h * HD : h * HD + HD // 2, part] = (one * SCALE).astype(LOW)
            q_ref[h * HD + HD // 2 : (h + 1) * HD, part] = (two * SCALE).astype(LOW)


def beside(ref):
    return jnp.concatenate([ref[i : i + HD, :] for i in range(0, ref.shape[0], HD)], axis=1)


def attend_kernel(seq, ranks, order, starts, q_ref, b0, b1, b2, b3, p_ref, o_ref, bias_ref):
    span = q_ref.shape[1]
    per = q_ref.shape[0] // HD
    rank = ranks[0]

    @pl.when(pl.program_id(0) == 0)
    def _():
        query_pos = order[seq, rank] * span + lax.broadcasted_iota(jnp.int32, (span, span), 1)
        query_in = []
        for m in range(2):
            start = starts[seq, m]
            query_in.append((query_pos >= start) & (query_pos < start + PIECE))
        for k in range(GROUP):
            key_pos = order[seq, rank ^ k] * span + lax.broadcasted_iota(jnp.int32, (span, span), 0)
            allowed = key_pos <= query_pos
            for m in range(2):
                start = starts[seq, m]
                key_in = (key_pos >= start) & (key_pos < start + PIECE)
                allowed = allowed | (query_in[m] & key_in)
            bias_ref[k * span : (k + 1) * span, :] = jnp.where(allowed, 0.0, MASKED_SCORE)

    kv_t = jnp.concatenate([b0[...], b1[...], b2[...], b3[...]], axis=1)
    keys = kv_t.T[:, 0:HD]
    values_t = kv_t[HD : 2 * HD, :]
    bias = jnp.concatenate([bias_ref[...]] * per, axis=1)
    scores = dot(keys, beside(q_ref)) + bias
    peak = jnp.max(scores, axis=0, keepdims=True)
    exponent = jnp.exp(scores - peak)
    total = jnp.sum(exponent, axis=0, keepdims=True)
    probs = (exponent * (1.0 / total)).astype(LOW)
    p_ref[0] = probs
    mixed = dot(values_t, probs).astype(LOW)
    for i in range(per):
        o_ref[i * HD : (i + 1) * HD, :] = mixed[:, i * span : (i + 1) * span]


def middle_kernel(ranks, att_ref, b0, b1, b2, b3, tok_ref, gain_ref, mid_ref, x_ref, w_ref):
    assemble(ranks[0], (b0, b1, b2, b3), w_ref)
    middle = tok_ref[0].astype(FULL) + dot(w_ref[...], att_ref[...], TN)
    mid_ref[...] = middle
    inverse = lax.rsqrt(jnp.mean(middle * middle, axis=0, keepdims=True) + NORM_EPS)
    x_ref[...] = (middle * inverse * gain_ref[:, 1:2].astype(FULL)).astype(LOW)


def forward_back_step(x, cot, wgut_ref, wgu_ref, wdt_ref, wd_ref, hid_ref, gg_ref, gu_ref, both):
    ff = wd_ref.shape[0]
    gate_up = dot(wgut_ref[...], x)
    grad_hidden = dot(wd_ref[...], cot)
    gate, up = gate_up[0:ff, :], gate_up[ff:, :]
    sig = 1.0 / (1.0 + jnp.exp(-gate))
    swish = gate * sig
    hidden = (swish * up).astype(LOW)
    grad_gate = (grad_hidden * up * sig * (1.0 + gate * (1.0 - sig))).astype(LOW)
    grad_up = (grad_hidden * swish).astype(LOW)
    hid_ref[...] = hidden
    gg_ref[...] = grad_gate
    gu_ref[...] = grad_up
    both[0:ff, :] = grad_gate
    both[ff:, :] = grad_up
    return dot(wgu_ref[...], both[...]).astype(LOW), dot(wdt_ref[...], hidden).astype(LOW)


def own_block_kernel(x_a, x_b, cot_ref, wgut_ref, wgu_ref, wdt_ref, wd_ref, out_ref, grad_ref, hid_ref, gg_ref, gu_ref, held, both):
    s = pl.program_id(0)
    for i, x in enumerate((x_a, x_b)):

        @pl.when(s == i)
        def _(x=x):
            held[...] = x[...]

    grad_x, out = forward_back_step(
        held[...], cot_ref[0], wgut_ref, wgu_ref, wdt_ref, wd_ref, hid_ref.at[0], gg_ref.at[0], gu_ref.at[0], both
    )
    grad_ref[0] = grad_x
    out_ref[0] = out


def other_blocks_kernel(*refs):
    blocks = refs[0:6]
    weights = refs[6:10]
    fo_ref, so_ref, fg_ref, sg_ref, hid_ref, gg_ref, gu_ref, held, both, sem = refs[10:]
    k = pl.program_id(0)
    copies = [pltpu.make_async_copy(block, held.at[i], sem.at[i]) for i, block in enumerate(blocks)]

    @pl.when(k == 0)
    def _():
        for i in range(3):
            copies[i].start()
            copies[3 + i].start()

    for i in range(3):

        @pl.when(k == i)
        def _(i=i):
            copies[i].wait()
            copies[3 + i].wait()

    grad_x, out = forward_back_step(held[k], held[3 + k], *weights, hid_ref, gg_ref, gu_ref, both)

    @pl.when(k == 1)
    def _():
        fg_ref[...] = grad_x
        fo_ref[...] = out

    @pl.when(k != 1)
    def _():
        sg_ref[0] = grad_x
        so_ref[0] = out


def weight_kernel(kinds, ranks, *refs):
    blocks = refs[0 : 2 * GROUP]
    rights = refs[2 * GROUP : 2 * GROUP + 3 * kinds]
    outs = refs[2 * GROUP + 3 * kinds : 2 * GROUP + 3 * kinds + 4]
    left, right, acc, sem = refs[2 * GROUP + 3 * kinds + 4 :]
    length = left.shape[1] // 2
    span = length // GROUP
    kind = pl.program_id(0)
    lefts, loads = [], []
    for b, block in enumerate(blocks):
        s, k = divmod(b, GROUP)
        lefts.append(pltpu.make_async_copy(block, left.at[:, pl.ds(b * span, span)], sem.at[b]))
    for n in range(kinds):
        own, *others = rights[3 * n : 3 * n + 3]
        for s in range(2):
            for i, (source, part) in enumerate(((own.at[s], pl.ds(s * length, span)), (others[s], pl.ds(s * length + span, length - span)))):
                at = sem.at[2 * GROUP + 4 * n + 2 * s + i]
                loads.append(pltpu.make_async_copy(source, right.at[n, :, part], at))

    @pl.when(kind == 0)
    def _():
        for copy in loads[0:2] + lefts[:GROUP] + loads[2:4] + lefts[GROUP:] + loads[4:]:
            copy.start()
        for copy in loads[0:2] + lefts[:GROUP]:
            copy.wait()

    for n in range(1, kinds):

        @pl.when(kind == n)
        def _(n=n):
            for copy in loads[4 * n : 4 * n + 4]:
                copy.wait()

    @pl.when(kind == 0)
    def _():
        acc[...] = dot(left[:, 0:length], right[0, :, 0:length], NT)
        for copy in loads[2:4] + lefts[GROUP:]:
            copy.wait()
        acc[...] += dot(left[:, length:], right[0, :, length:], NT)

    @pl.when(kind > 0)
    def _():
        acc[...] = dot(left[...], right[kind], NT)

    part = acc.shape[0] // PARTS
    places = [(outs[0], i) for i in range(4)] + [(outs[1], 0), (outs[1], 1), (outs[2], 0), (outs[3], 0)]
    for (out, i), slot in zip(places, SLOTS):
        start = pl.multiple_of((slot ^ ranks[1]) * part, 8)
        out[i] = acc[pl.ds(start, part), :].astype(LOW)


def branch_kernel(seq, ranks, mid_ref, cot_ref, e0, e1, e2, gain_ref, b0, b1, b2, b3, att_ref, gm_ref, gb_ref, do_ref, delta_ref, gain_out, w_ref):
    width, span = mid_ref.shape
    assemble(ranks[0], (b0, b1, b2, b3), w_ref)
    middle = mid_ref[...]
    grad = e0[0].astype(FULL) + e1[0].astype(FULL) + e2[...].astype(FULL)
    inverse = lax.rsqrt(jnp.mean(middle * middle, axis=0, keepdims=True) + NORM_EPS)
    scaled = grad * gain_ref[:, 1:2].astype(FULL)
    turned = jnp.mean(scaled * middle, axis=0, keepdims=True)
    grad_middle = cot_ref[seq].astype(FULL) + inverse * scaled - middle * (inverse * inverse * inverse * turned)
    gain_out[...] = dot(jnp.ones((8, span), LOW), (grad * middle * inverse).astype(LOW), NT)
    gm_ref[...] = grad_middle
    branch = grad_middle.astype(LOW)
    gb_ref[...] = branch
    grad_att = dot(w_ref[...], branch).astype(LOW)
    do_ref[...] = grad_att
    both = grad_att.astype(FULL) * att_ref[...].astype(FULL)
    heads = width // HD
    for h in range(heads):
        delta_ref[h : h + 1, :] = jnp.sum(both[h * HD : (h + 1) * HD, :], axis=0, keepdims=True)
    delta_ref[heads:, :] = jnp.zeros((delta_ref.shape[0] - heads, span), FULL)


def attend_back_kernel(seq, q_ref, b0, b1, b2, b3, p_ref, do_ref, delta_ref, cos_ref, sin_ref, gq_ref, own_ref, far_ref, send_ref):
    span = q_ref.shape[1]
    per = q_ref.shape[0] // HD
    h = pl.program_id(0)
    kv_t = jnp.concatenate([b0[...], b1[...], b2[...], b3[...]], axis=1)
    kv = kv_t.T
    query, out_grad = beside(q_ref), beside(do_ref)
    delta = jnp.concatenate([delta_ref[pl.ds(per * h + i, 1), :] for i in range(per)], axis=1)
    none = jnp.zeros(out_grad.shape, LOW)
    grad_probs = dot(kv, jnp.concatenate([none, out_grad], axis=0))
    grad_scores = (p_ref[0].astype(FULL) * (grad_probs - delta)).astype(LOW)
    grad_q = dot(kv_t[0:HD, :], grad_scores) * SCALE
    for i in range(per):
        one, two = turn(grad_q[:, i * span : (i + 1) * span], cos_ref[seq], sin_ref[seq], -1.0)
        gq_ref[i * HD : i * HD + HD // 2, :] = one.astype(LOW)
        gq_ref[i * HD + HD // 2 : (i + 1) * HD, :] = two.astype(LOW)
    keys = dot(query, grad_scores, NT).astype(LOW)
    values = dot(out_grad, p_ref[0], NT).astype(LOW)
    for k in range(GROUP):
        out = (own_ref, send_ref.at[0], far_ref, send_ref.at[1])[k]
        part = slice(k * span, (k + 1) * span)
        out[0:HD, :] = keys[:, part]
        out[HD:, :] = values[:, part]


def slot_at(i):
    n = PARTS - 1 - i
    return ((n & 1) << 2) | (n & 2) | ((n >> 2) & 1)


def spread(ranks, acc, own_ref, far_ref, send_ref):
    part = acc.shape[1] // PARTS
    outs = (own_ref, send_ref.at[0], far_ref, send_ref.at[1])

    def move(i, carry):
        start = pl.multiple_of((slot_at(i) ^ ranks[1]) * part, 8)
        for k, out in enumerate(outs):
            out[i] = acc[ranks[0] ^ k, pl.ds(start, part), :].astype(LOW)
        return carry

    lax.fori_loop(0, PARTS, move, 0)


def query_weight_kernel(ranks, norm_ref, gq_a, gq_b, att_a, att_b, gb_a, gb_b, own_ref, far_ref, send_ref, acc):
    width, span = gq_a.shape
    shard = width // GROUP
    for b in range(GROUP):
        rows = slice(b * shard, (b + 1) * shard)
        acc[b, 0:shard, 0:width] = dot(norm_ref[rows, 0:span], gq_a[...], NT) + dot(norm_ref[rows, span:], gq_b[...], NT)
        acc[b, 0:shard, width:] = dot(att_a[rows, :], gb_a[...], NT) + dot(att_b[rows, :], gb_b[...], NT)
        acc[b, shard:, :] = jnp.zeros((acc.shape[1] - shard, acc.shape[2]), FULL)
    spread(ranks, acc, own_ref, far_ref, send_ref)


def key_weight_kernel(ranks, *refs):
    norm_ref, *terms = refs[0:7]
    cos_ref, sin_ref, part_ref, k0, k1, k2, k3, tok_ref, gm_a, gm_b, gain_a, gain_b = refs[7:19]
    own_ref, far_ref, send_ref, out_ref, gkv_ref, wkv_ref, acc = refs[19:]
    width = norm_ref.shape[0]
    span = gm_a.shape[1]
    shard = width // GROUP
    kw2 = gkv_ref.shape[0]
    kw = kw2 // 2
    assemble(ranks[0], (k0, k1, k2, k3), wkv_ref)
    gain_one = wkv_ref[:, kw2 : kw2 + 1].astype(FULL)
    grad_gain = None
    for s in range(2):
        e0, e1, e2 = terms[3 * s : 3 * s + 3]
        part = slice(s * span, (s + 1) * span)
        grad = e0[...].astype(FULL) + e1[0].astype(FULL) + e2[...].astype(FULL)
        for h in range(kw // HD):
            top = h * 2 * HD
            one, two = turn(grad[top : top + HD, :], cos_ref[s], sin_ref[s], -1.0)
            gkv_ref[h * HD : h * HD + HD // 2, part] = one.astype(LOW)
            gkv_ref[h * HD + HD // 2 : (h + 1) * HD, part] = two.astype(LOW)
            gkv_ref[kw + h * HD : kw + (h + 1) * HD, part] = grad[top + HD : top + 2 * HD, :].astype(LOW)
        grad_norm = part_ref[s] + dot(wkv_ref[:, 0:kw2], gkv_ref[:, part])
        x = tok_ref[s].astype(FULL)
        inverse = lax.rsqrt(jnp.mean(x * x, axis=0, keepdims=True) + NORM_EPS)
        scaled = grad_norm * gain_one
        turned = jnp.mean(scaled * x, axis=0, keepdims=True)
        out_ref[s] = (gm_a, gm_b)[s][...] + inverse * scaled - x * (inverse * inverse * inverse * turned)
        row = dot(jnp.ones((8, span), LOW), (grad_norm * x * inverse).astype(LOW), NT)
        grad_gain = row if grad_gain is None else grad_gain + row
    gains = jnp.concatenate([grad_gain[0:1, :], gain_a[0:1, :] + gain_b[0:1, :], jnp.zeros((6, width), FULL)], axis=0)
    for b in range(GROUP):
        rows = slice(b * shard, (b + 1) * shard)
        acc[b, 0:shard, :] = dot(norm_ref[rows, :], gkv_ref[...], NT)
        acc[b, shard:, :] = jnp.zeros((acc.shape[1] - shard, kw2), FULL)
        acc[b, shard : shard + 8, 0:shard] = gains[:, rows]
    spread(ranks, acc, own_ref, far_ref, send_ref)


def query_grad_kernel(ranks, gq_a, gq_b, q0, q1, q2, q3, out_ref, wq_ref):
    assemble(ranks[0], (q0, q1, q2, q3), wq_ref)
    out_ref[0] = dot(wq_ref[...], gq_a[...])
    out_ref[1] = dot(wq_ref[...], gq_b[...])


def place(slot):
    return ((slot >> 2) & 1) + ((slot >> 1) & 1) * 2


def gathered(ranks, pairs):
    def move(a, carry):
        slot = ranks[1] ^ a
        index = place(slot)
        for parity in range(2):

            @pl.when(slot % 2 == parity)
            def _(parity=parity):
                for pair in pairs:
                    part = pair[parity].shape[1]
                    rows = pl.ds(pl.multiple_of(a * part, 8), part)
                    pair[2][rows, :] = pair[parity][index].astype(FULL)

        return carry

    lax.fori_loop(0, PARTS, move, 0)


def forward_weights_kernel(ranks, even, odd, *outs):
    columns = outs[0].shape[1]
    for i, out in enumerate(outs):
        part = slice(i * columns, (i + 1) * columns)
        gathered(ranks, [(even.at[:, :, part], odd.at[:, :, part], out)])


def attention_done_kernel(ranks, even, odd, q_ref, o_ref, k_ref, v_ref, gain_ref, scratch):
    shard, width = q_ref.shape
    kw = k_ref.shape[0]
    gathered(ranks, [(even, odd, scratch)])
    q_ref[...] = scratch[0:shard, 0:width]
    o_ref[...] = scratch[0:shard, width : 2 * width]
    k_ref[...] = scratch[0:shard, 2 * width : 2 * width + kw].T
    v_ref[...] = scratch[0:shard, 2 * width + kw :].T
    gain_ref[...] = scratch[shard : shard + 8, 2 * width : 2 * width + shard]


def tables(places):
    half = HD // 2
    frequency = ROPE_BASE ** (-2.0 * jnp.arange(half, dtype=FULL) / HD)
    angles = places.astype(FULL)[:, None, :] * frequency[None, :, None]
    return jnp.cos(angles), jnp.sin(angles)


def body(
    tokens,
    w_query,
    w_key,
    w_value,
    w_out,
    w_gate,
    w_up,
    w_down,
    gain_attn,
    gain_mlp,
    span_order,
    piece_starts,
    cotangent,
):
    ranks = lax.axis_size("rep")
    rank_grp = lax.axis_index("grp")
    seq_count, span, width = tokens.shape
    shard = w_query.shape[0]
    kw = w_key.shape[1]
    kw2 = 2 * kw
    kv_heads = kw // HD
    per = width // kw
    ff = w_gate.shape[1]
    rows = seq_count * span
    length = GROUP * span
    place_of = jnp.stack([rank_grp, lax.axis_index("rep") % PARTS]).astype(jnp.int32)
    tok_t = jnp.swapaxes(tokens, 1, 2)
    cot_t = jnp.swapaxes(cotangent, 1, 2)
    wd_t = w_down.T
    act = whole((width, span))
    seqs = whole((seq_count, width, span))
    one_seq = lambda s: pl.BlockSpec((1, width, span), lambda *_: (s, 0, 0))
    table = whole((seq_count, HD // 2, span))
    gain_spec = whole((width, LANES))
    head = pl.BlockSpec((2 * HD, span), lambda h, *_: (h, 0))
    probs_spec = pl.BlockSpec((1, length, per * span), lambda h, *_: (h, 0, 0))
    q_spec = lambda s: pl.BlockSpec((per * HD, span), lambda h, *_: (h, s))
    per_head = pl.BlockSpec((per * HD, span), lambda h, *_: (h, 0))

    kv_shard = call(
        pack_kernel,
        "pack",
        shape_of((shard, kw2 + LANES)),
        in_specs=[whole((kw, shard))] * 2 + [whole((2, shard))],
        out_specs=whole((shard, kw2 + LANES)),
        micros=2,
    )(w_key.T, w_value.T, jnp.stack([gain_attn, gain_mlp]).astype(FULL))
    kv_flight = Blocks(kv_shard)
    q_flight = Blocks(w_query, kv_shard)
    own_span = lax.dynamic_slice(span_order, (0, rank_grp), (seq_count, 1))
    places = own_span * span + jnp.arange(span, dtype=jnp.int32)[None, :]
    cos_cols, sin_cols = tables(places)
    wgut, wgu = call(
        flip_two_kernel,
        "flip_two",
        (shape_of((2 * ff, width)), shape_of((width, 2 * ff))),
        in_specs=[whole((width, ff))] * 2,
        out_specs=(whole((2 * ff, width)), whole((width, 2 * ff))),
        micros=4,
    )(after(w_gate, kv_flight.sent), w_up)
    wd = call(
        flip_one_kernel,
        "flip_one",
        shape_of((ff, width)),
        in_specs=[whole((width, ff))],
        out_specs=whole((ff, width)),
        micros=2,
    )(after(wd_t, wgut))
    kv_blocks = kv_flight.finish(wd)
    norm_low, kv_a, kv_b, gain_cols = call(
        keys_values_kernel,
        "keys_values",
        (shape_of((width, rows)), shape_of((kw2, span)), shape_of((kw2, span)), shape_of((width, LANES))),
        free=range(1, 5),
            prefetch=1,
        in_specs=[NEAR] + [whole(kv_shard.shape)] * 4 + [table, table],
        out_specs=(whole((width, rows)), whole((kw2, span)), whole((kw2, span)), gain_spec),
        scratch=[pltpu.VMEM((width, kw2 + LANES), LOW)],
        micros=4.3,
    )(place_of, tok_t, *kv_blocks, cos_cols, sin_cols)
    kv_flight = [Blocks(kv_a), None]
    q_blocks = q_flight.finish(norm_low)
    queries = call(
        queries_kernel,
        "queries",
        shape_of((width, rows)),
        free=range(1, 5),
            prefetch=1,
        in_specs=[whole((width, rows))] + [whole((shard, width))] * 4 + [table, table],
        out_specs=whole((width, rows)),
        scratch=[pltpu.VMEM((width, width), LOW)],
        micros=0.1,
    )(place_of, norm_low, *q_blocks, cos_cols, sin_cols)

    o_flight = Blocks(w_out, kv_a)
    kv_flight[1] = Blocks(kv_b, *q_blocks)
    cot_flight = [Blocks(cot_t[0], queries), None]
    cot_blocks = [None, None]
    kv_all = [kv_flight[0].finish(queries), None]

    def attend_of(s, query):
        return call(
            functools.partial(attend_kernel, s),
            "attend",
            (shape_of((kv_heads, length, per * span)), shape_of((width, span))),
            free=range(1, 5),
            prefetch=3,
            grid=(kv_heads,),
            in_specs=[q_spec(s)] + [head] * 4,
            out_specs=(probs_spec, per_head),
            scratch=[pltpu.VMEM((length, span), FULL)],
            micros=0.1,
        )(place_of, span_order, piece_starts, query, *kv_all[s])

    def middle_of(s, att):
        return call(
            middle_kernel,
            "middle",
            (shape_of((width, span), FULL), shape_of((width, span))),
            free=range(1, 5),
            prefetch=1,
            in_specs=[act] + [whole((shard, width))] * 4 + [one_seq(s), gain_spec],
            out_specs=(act, act),
            scratch=[pltpu.VMEM((width, width), LOW)],
            micros=3,
        )(place_of, att, *o_blocks, tok_t, gain_cols)

    probs_a, att_a = attend_of(0, queries)
    o_blocks = o_flight.finish(att_a)
    kv_all[1] = kv_flight[1].finish(att_a)
    middle_a, x_a = middle_of(0, att_a)
    x_flight = [Blocks(x_a), None]
    cot_flight[1] = Blocks(cot_t[1], x_flight[0].sent, x_a)
    probs_b, att_b = attend_of(1, after(queries, x_a))
    cot_flight[0].arrive(att_b)
    middle_b, x_b = middle_of(1, after(att_b, *cot_flight[0].ready))
    x_flight[1] = Blocks(x_b)
    x_flight[0].arrive(middle_b)
    cot_blocks[0] = cot_flight[0].finish(middle_b)
    stats, attended, middles = (probs_a, probs_b), (att_a, att_b), (middle_a, middle_b)

    each = pl.BlockSpec((1, width, span), lambda s, *_: (s, 0, 0))
    each_ff = pl.BlockSpec((1, ff, span), lambda s, *_: (s, 0, 0))
    two = shape_of((seq_count, width, span))
    two_ff = shape_of((seq_count, ff, span))
    own_out, own_grad, own_hid, own_gg, own_gu = call(
        own_block_kernel,
        "own_blocks",
        (two, two, two_ff, two_ff, two_ff),
        grid=(seq_count,),
        in_specs=[act, act, each] + [NEAR] * 4,
        out_specs=(each, each, each_ff, each_ff, each_ff),
        scratch=[pltpu.VMEM((width, span), LOW), pltpu.VMEM((2 * ff, span), LOW)],
        micros=8,
    )(after(x_a, *x_flight[0].ready, *cot_blocks[0]), x_b, cot_t, wgut, wgu, wd_t, wd)
    x_blocks = [x_flight[0].finish(own_out), None]
    cot_flight[1].arrive(own_out)

    def other_blocks(s, *others):
        half = pl.BlockSpec((1, width, span), lambda k, *_: (k // 2, 0, 0))
        per_block = pl.BlockSpec((ff, span), lambda k, *_: (0, k))
        act_shape, half_shape, ff_shape = shape_of((width, span)), shape_of((2, width, span)), shape_of((ff, 3 * span))
        return call(
            other_blocks_kernel,
            "other_blocks",
            (act_shape, half_shape, act_shape, half_shape, ff_shape, ff_shape, ff_shape),
            free=(0, 2),
            grid=(GROUP - 1,),
            in_specs=[ANY] * 6 + [NEAR] * 4,
            out_specs=(act, half, act, half) + (per_block,) * 3,
            scratch=[
                pltpu.VMEM((6, width, span), LOW),
                pltpu.VMEM((2 * ff, span), LOW),
                pltpu.SemaphoreType.DMA((6,)),
            ],
            micros=12,
        )(after(x_blocks[s][1], *others), *x_blocks[s][2:], *cot_blocks[s][1:], wgut, wgu, wd_t, wd)

    fo_a, so_a, fg_a, sg_a, hid_a, gg_a, gu_a = other_blocks(0, *cot_flight[1].ready)
    grad_a = Terms(own_grad[0], fg_a, sg_a)
    out_a = Terms(own_out[0], fo_a, so_a)
    x_flight[1].arrive(fg_a)
    x_blocks[1] = x_flight[1].finish()
    cot_blocks[1] = cot_flight[1].finish(fg_a)
    fo_b, so_b, fg_b, sg_b, hid_b, gg_b, gu_b = other_blocks(1, fg_a)
    grad_b = Terms(own_grad[1], fg_b, sg_b)
    out_b = Terms(own_out[1], fo_b, so_b)
    stage = (grad_a.cross(fg_b), out_a.cross(fg_b))
    grads = (grad_a, grad_b)

    part = width // PARTS

    def sums(name, blocks, kinds, *others):
        count = len(kinds)
        columns = count * ff
        pieces = call(
            functools.partial(weight_kernel, count),
            name,
            tuple(shape_of((n, part, columns)) for n in (4, 2, 1, 1)),
            prefetch=1,
            grid=(count,),
            in_specs=[ANY] * (2 * GROUP + 3 * count),
            out_specs=tuple(pl.BlockSpec((n, part, ff), lambda m, *_: (0, 0, m)) for n in (4, 2, 1, 1)),
            scratch=[
                pltpu.VMEM((width, 2 * length), LOW),
                pltpu.VMEM((count, ff, 2 * length), LOW),
                pltpu.VMEM((width, ff), FULL),
                pltpu.SemaphoreType.DMA((2 * GROUP + 4 * count,)),
            ],
            micros=2 + 6 * count,
        )(place_of, after(blocks[0], *others), *blocks[1:], *sum(kinds, ()))
        return RepSum(pieces, ranks)

    x_all = x_blocks[0] + x_blocks[1]
    down_sum = sums("down_weights", cot_blocks[0] + cot_blocks[1], [(own_hid, hid_a, hid_b)], *stage)
    done = down_sum.pieces[0]
    stage = (grad_b.cross(done), out_b.beside, done)
    up_sum = sums("gate_up_weights", x_all, [(own_gg, gg_a, gg_b), (own_gu, gu_a, gu_b)], *stage)
    done = up_sum.pieces[0]
    stage = (grad_a.across, out_b.cross(done), down_sum.second(done), out_a.across, done)

    def branch_of(s, *others):
        _, beside_term, across_term = grads[s].all()
        first = whole((1, width, span))
        return call(
            functools.partial(branch_kernel, s),
            "branch",
            (
                shape_of((width, span), FULL),
                shape_of((width, span)),
                shape_of((width, span)),
                shape_of((16, span), FULL),
                shape_of((8, width), FULL),
            ),
            free=(3, 4),
            prefetch=1,
            in_specs=[NEAR, NEAR, one_seq(s), first, act, NEAR] + [NEAR] * 5,
            out_specs=(act, act, act, whole((16, span)), whole((8, width))),
            scratch=[pltpu.VMEM((width, width), LOW)],
            micros=4,
        )(place_of, middles[s], cot_t, own_grad, beside_term, after(across_term, *others), gain_cols, *o_blocks, attended[s])

    def attend_back_of(s, out_grad, delta):
        halves = pl.BlockSpec((2, 2 * HD, span), lambda h, *_: (0, h, 0))
        grad_q, *kv_parts = call(
            functools.partial(attend_back_kernel, s),
            "attend_back",
            (shape_of((width, span)), shape_of((kw2, span)), shape_of((kw2, span)), shape_of((2, kw2, span))),
            grid=(kv_heads,),
            in_specs=[q_spec(s)] + [head] * 4 + [probs_spec, per_head, whole((16, span)), table, table],
            out_specs=(per_head, head, head, halves),
            micros=11,
        )(queries, *kv_all[s], stats[s], out_grad, delta, cos_cols, sin_cols)
        return grad_q, Terms(*kv_parts)

    mid_a, branch_a, dout_a, delta_a, gain_a = branch_of(0, *stage)
    stage = (down_sum.third(branch_a), grad_b.across)
    gq_a, kv_grad_a = attend_back_of(0, after(dout_a, *stage), delta_a)
    stage = (out_b.across, down_sum.own(gq_a))
    mid_b, branch_b, dout_b, delta_b, gain_b = branch_of(1, *stage)
    stage = (kv_grad_a.cross(branch_b), up_sum.second(branch_b))
    gq_b, kv_grad_b = attend_back_of(1, after(dout_b, *stage), delta_b)
    stage = (down_sum.spread(gq_b), kv_grad_a.across)

    grown = shard + GAIN_ROWS
    piece = grown // PARTS
    spread_out = lambda columns: (shape_of((PARTS, piece, columns)),) * 2 + (shape_of((2, PARTS, piece, columns)),)
    spread_spec = lambda columns: (whole((PARTS, piece, columns)),) * 2 + (whole((2, PARTS, piece, columns)),)
    query_parts = call(
        query_weight_kernel,
        "query_weights",
        spread_out(2 * width),
        prefetch=1,
        in_specs=[NEAR, NEAR, act] + [NEAR] * 4,
        out_specs=spread_spec(2 * width),
        scratch=[pltpu.VMEM((GROUP, grown, 2 * width), FULL)],
        micros=8,
    )(place_of, norm_low, gq_a, after(gq_b, *stage), *attended, branch_a, branch_b)
    done = query_parts[0]
    stage = (kv_grad_b.cross(done), up_sum.third(done))
    query_terms = Terms(*query_parts, *stage)
    grad_part = call(
        query_grad_kernel,
        "query_grad",
        shape_of((seq_count, width, span), FULL),
        prefetch=1,
        in_specs=[NEAR, act] + [NEAR] * 4,
        out_specs=seqs,
        scratch=[pltpu.VMEM((width, width), LOW)],
        micros=4,
    )(place_of, gq_a, after(gq_b, *stage), *q_blocks)
    stage = (query_terms.cross(grad_part),)
    stage = (*stage, kv_grad_b.across)

    def owned(terms):
        own, beside_term, across = terms.all()
        cuts = (slice(0, 4), slice(4, 6), slice(6, 7), slice(7, 8))
        return [three((own[c], beside_term[:, c], across[c])) for c in cuts]

    first = whole((1, kw2, span))
    terms = []
    for term in (kv_grad_a, kv_grad_b):
        terms += term.all()
    *key_parts, grad_tokens = call(
        key_weight_kernel,
        "key_weights",
        spread_out(kw2) + (shape_of((seq_count, width, span), FULL),),
        free=range(1, 7),
            prefetch=1,
        in_specs=[NEAR]
        + [whole((kw2, span)), first, whole((kw2, span))] * 2
        + [table, table, seqs]
        + [NEAR] * 7
        + [whole((8, width))] * 2,
        out_specs=spread_spec(kw2) + (seqs,),
        scratch=[
            pltpu.VMEM((kw2, rows), LOW),
            pltpu.VMEM((width, kw2 + LANES), LOW),
            pltpu.VMEM((GROUP, grown, kw2), FULL),
        ],
        micros=10,
    )(
        place_of,
        norm_low,
        after(terms[0], *stage),
        *terms[1:],
        cos_cols,
        sin_cols,
        grad_part,
        *kv_blocks,
        tok_t,
        mid_a,
        mid_b,
        gain_a,
        gain_b,
    )
    down_pair = down_sum.done(grad_tokens)
    stage = (up_sum.own(grad_tokens), down_pair[0])
    key_terms = Terms(*key_parts)

    def finished(name, kernel, pair, outs, *others):
        columns = pair[0].shape[2]
        return call(
            kernel,
            name,
            (shape_of((width, ff), FULL),) * outs,
            free=range(2),
            prefetch=1,
            in_specs=[whole((4, part, columns))] * 2,
            out_specs=(whole((width, ff)),) * outs,
            micros=3.5 * outs,
        )(place_of, after(pair[0], *others), pair[1])

    block_out = jnp.stack(
        [middle + three(term.all()) for middle, term in zip(after(middles, *stage), (out_a, out_b))]
    )
    key_terms.cross(block_out)
    pieces = []
    for query_piece, key_piece in zip(owned(query_terms), owned(key_terms)):
        joint = jnp.concatenate([query_piece, key_piece], axis=-1)
        pieces.append(joint.astype(LOW))
    query_sum = ShortSum(pieces, ranks)

    up_sum.spread(*pieces)
    (grad_down,) = finished("down_done", forward_weights_kernel, down_pair, 1, *pieces)
    step = query_sum.second(grad_down)
    up_pair = up_sum.done(*step)
    step = query_sum.own(up_pair[0])
    query_pair = query_sum.done(step, up_pair[1])
    grad_gate, grad_up = finished("gate_up_done", forward_weights_kernel, up_pair, 2, query_pair[0])
    grad_down = grad_down.T
    grad_query, grad_out, grad_key, grad_value, grad_gains = call(
        attention_done_kernel,
        "attention_done",
        (shape_of((shard, width), FULL),) * 2 + (shape_of((kw, shard), FULL),) * 2 + (shape_of((8, shard), FULL),),
        free=range(2),
            prefetch=1,
        in_specs=[whole((4, piece, 2 * width + kw2))] * 2,
        out_specs=(whole((shard, width)),) * 2 + (whole((kw, shard)),) * 2 + (whole((8, shard)),),
        scratch=[pltpu.VMEM((grown, 2 * width + kw2), FULL)],
        micros=5,
    )(place_of, *query_pair)
    return (
        jnp.swapaxes(block_out, 1, 2),
        jnp.swapaxes(grad_tokens, 1, 2),
        grad_query,
        grad_key.T,
        grad_value.T,
        grad_out,
        grad_gate,
        grad_up,
        grad_down,
        grad_gains[0],
        grad_gains[1],
    )


def solution(mesh):
    placed = (
        P("rep", "grp", None),
        P("grp", None),
        P("grp", None),
        P("grp", None),
        P("grp", None),
        P(None, "grp"),
        P(None, "grp"),
        P("grp", None),
        P("grp"),
        P("grp"),
        P("rep", None),
        P("rep", None),
        P("rep", "grp", None),
    )
    return jax.shard_map(
        body,
        mesh=mesh,
        in_specs=placed,
        out_specs=(
            P("rep", "grp", None),
            P("rep", "grp", None),
            P("grp", None),
            P("grp", None),
            P("grp", None),
            P("grp", None),
            P(None, "grp"),
            P(None, "grp"),
            P("grp", None),
            P("grp"),
            P("grp"),
        ),
        check_vma=False,
    )
```
